32 devices in a mesh: dp: 16 (over z, y, x), mp: 2 (over core).
Axes of the slice: x: 2, y: 2, z: 4, core: 2. Of those that a mesh axis runs over, the one named last changes fastest.
Arguments:
- inputs: float32 [64, 256, 768], P('dp'), may hold values from -6 to 6
- segment_ids: int32 [64, 256], P('dp'), may hold values from 0 to 7, never falling along the last dimension, each value on 1 to 64 neighbouring positions
- ln1_gain: float32 [768], replicated, may hold values from 0.1 to 1.9
- ln1_bias: float32 [768], replicated, may hold values from -1.75 to 1.75
- w_query: bfloat16 [768, 768], P(None, 'mp'), may hold values from -0.21875 to 0.21875
- b_query: float32 [768], P('mp'), may hold values from -3 to 3
- w_key: bfloat16 [768, 768], P(None, 'mp'), may hold values from -0.21875 to 0.21875
- w_value: bfloat16 [768, 768], P(None, 'mp'), may hold values from -0.21875 to 0.21875
- b_value: float32 [768], P('mp'), may hold values from -3 to 3
- w_output: bfloat16 [768, 768], P('mp'), may hold values from -1.25 to 1.25
- b_output: float32 [768], replicated, may hold values from -3 to 3
- ln2_gain: float32 [768], replicated, may hold values from 0.1 to 1.9
- ln2_bias: float32 [768], replicated, may hold values from -1.75 to 1.75
- w_up: bfloat16 [768, 3072], P(None, 'mp'), may hold values from -0.21875 to 0.21875
- b_up: float32 [3072], P('mp'), may hold values from -3 to 3
- w_down: bfloat16 [3072, 768], P('mp'), may hold values from -0.109375 to 0.109375
- b_down: float32 [768], replicated, may hold values from -3 to 3
- cotangent: float32 [64, 256, 768], P('dp'), may hold values from -6 to 6
Outputs:
- result: float32 [64, 256, 768], P('dp')
- grad_inputs: float32 [64, 256, 768], P('dp')
- grad_ln1_gain: float32 [768], replicated
- grad_ln1_bias: float32 [768], replicated
- grad_w_query: float32 [768, 768], P('dp', 'mp')
- grad_b_query: float32 [768], P('mp')
- grad_w_key: float32 [768, 768], P('dp', 'mp')
- grad_w_value: float32 [768, 768], P('dp', 'mp')
- grad_b_value: float32 [768], P('mp')
- grad_w_output: float32 [768, 768], P('mp', 'dp')
- grad_b_output: float32 [768], replicated
- grad_ln2_gain: float32 [768], replicated
- grad_ln2_bias: float32 [768], replicated
- grad_w_up: float32 [768, 3072], P('dp', 'mp')
- grad_b_up: float32 [3072], P('mp')
- grad_w_down: float32 [3072, 768], P('mp', 'dp')
- grad_b_down: float32 [768], replicated
The draws below stay inside these ranges and needn't reach their ends.
Inputs may be any that keep to these rules, and one draw needn't show every extreme that they name: `segment_ids`: along each row the ids never fall; every id of 0 to 7 covers 1 to 64 consecutive positions, some one exactly 64.
All inputs are finite; a program needn't handle non-finite values.
Results may differ from the reference program's by a relative error of at most 0.011.
Values sent between devices are 32-bit elements; how exact they have to be, the bound alone decides.
No kernel may reach another device: no remote copies, remote signals or barrier semaphores. Data moves between devices by JAX's collectives and lax.ppermute only.
A program may use at most 128 MiB of HBM per device.

```python
import math
from functools import partial
import jax
import jax.numpy as jnp
import numpy as np
from jax import lax

D = 768
HEADS = 12
HD = 64
FF = 3072
SEQ = 256
MOST = 64
ROWS = 64
SEGS = 8


def spiked(values, rng, source, target, blocks, factor):
    def block_of(axis_at):
        return (jnp.arange(values.shape[axis_at]) // (values.shape[axis_at] // blocks)).reshape((-1,) + (1,) * (values.ndim - 1 - axis_at))

    one_side = jax.random.permutation(rng, blocks)[block_of(target)]
    second = (block_of(target) + blocks // 2) % blocks
    return jnp.where((block_of(source) == one_side) | (block_of(source) == second), factor * values, values)


def block_scale(stream_key, shape, split, least, top_value):
    def one(dim, parts):
        draws = jax.random.uniform(jax.random.fold_in(jax.random.fold_in(stream_key, 6), dim), (parts,), jnp.float32, least / len(split), top_value / len(split))
        return jnp.repeat(jnp.exp(draws), shape[dim] // parts).reshape((-1,) + (1,) * (len(shape) - dim - 1))

    level = one(*split[0])
    for cut in split[1:]:
        level = level * one(*cut)
    return level


def profile(count, total, bound, lean):
    weights = [(1 << 20) // math.isqrt(standing ** lean) + 1 for standing in range(2, count + 1)]
    spare, counts = total - bound - (count - 1), [1] * (count - 1)
    while spare > 0:
        candidates = [i for i in range(count - 1) if counts[i] < bound]
        pool, remaining = sum([weights[i] for i in candidates]), spare
        for i in candidates:
            extra = min(bound - counts[i], max(1, remaining * weights[i] // pool), spare)
            counts[i] = counts[i] + extra
            spare = spare - extra
    return np.array([bound] + counts)


def ragged(own_key, amount, total, bound, slope):
    if amount == 2:
        one = jax.random.randint(own_key, (), max(1, total - bound), min(bound, total - 1) + 1)
        return jnp.stack([one, total - one])
    tallies = jnp.asarray(profile(amount, total, bound, slope), jnp.int32)
    pairs = (amount - 1) // 2
    giver, sink = tallies[1:1 + 2 * pairs:2], tallies[2:2 + 2 * pairs:2]
    slack = jnp.minimum(giver - 1, bound - sink)
    shifted = jax.random.randint(jax.random.fold_in(own_key, 1), (pairs,), 0, 1 << 20) % (slack + 1)
    tallies = tallies.at[1:1 + 2 * pairs:2].set(giver - shifted).at[2:2 + 2 * pairs:2].set(sink + shifted)
    return tallies[jax.random.permutation(jax.random.fold_in(own_key, 2), amount)]


def scatter_about(key, shape, scale, most, split=(), kind=jnp.bfloat16):
    entries = scale * jax.random.normal(key, shape, jnp.float32)
    if split:
        entries = entries * block_scale(key, shape, split, -0.22, 0.18)
    return jnp.clip(entries, -most, most).astype(kind)


def noise_with(stream_key, dims, spread, reach, cuts, heavy, held_as=jnp.bfloat16):
    drawn = spread * jax.random.normal(stream_key, dims, jnp.float32)
    if cuts:
        drawn = drawn * block_scale(stream_key, dims, cuts, -0.22, 0.18)
    return jnp.clip(spiked(drawn, jax.random.fold_in(stream_key, 3), *heavy), -reach, reach).astype(held_as)


def setup_inputs(seed: int = 0) -> dict:
    key_of = jax.random.split(jax.random.key(seed), 19)
    inputs = noise_with(key_of[0], (ROWS, SEQ, D), 1.0, 6.0, ((0, 16),), (0, 2, 16, 2.0), jnp.float32)
    segment_ids = jax.vmap(lambda own: jnp.searchsorted(jnp.cumsum(ragged(own, SEGS, SEQ, MOST, 0)), jnp.arange(SEQ), side="right"))(jax.random.split(key_of[1], ROWS)).reshape((ROWS, SEQ)).astype(jnp.int32)
    ln1_gain = jnp.clip(1.0 + 0.18 * jax.random.normal(key_of[2], (D,), jnp.float32), 0.1, 1.9)
    ln1_bias = scatter_about(key_of[3], (D,), 0.3, 1.75, (), jnp.float32)
    w_query = scatter_about(key_of[4], (D, D), D ** -0.5, 0.21875, ((1, 2),))
    b_query = scatter_about(key_of[5], (D,), 0.5, 3.0, ((0, 2),), jnp.float32)
    w_key = scatter_about(key_of[6], (D, D), D ** -0.5, 0.21875, ((1, 2),))
    w_value = scatter_about(key_of[7], (D, D), D ** -0.5, 0.21875, ((1, 2),))
    b_value = scatter_about(key_of[8], (D,), 0.5, 3.0, ((0, 2),), jnp.float32)
    w_output = scatter_about(key_of[9], (D, D), (D // 32) ** -0.5, 1.25, ((0, 2),))
    b_output = scatter_about(key_of[10], (D,), 0.5, 3.0, (), jnp.float32)
    ln2_gain = jnp.clip(1.0 + 0.18 * jax.random.normal(key_of[11], (D,), jnp.float32), 0.1, 1.9)
    ln2_bias = scatter_about(key_of[12], (D,), 0.3, 1.75, (), jnp.float32)
    w_up = scatter_about(key_of[13], (D, FF), D ** -0.5, 0.21875, ((1, 2),))
    b_up = scatter_about(key_of[14], (FF,), 0.5, 3.0, ((0, 2),), jnp.float32)
    w_down = scatter_about(key_of[15], (FF, D), FF ** -0.5, 0.109375, ((0, 2),))
    b_down = scatter_about(key_of[16], (D,), 0.5, 3.0, (), jnp.float32)
    cotangent = noise_with(key_of[17], (ROWS, SEQ, D), 1.0, 6.0, ((0, 16),), (0, 2, 16, 2.0), jnp.float32)
    return {"inputs": inputs, "segment_ids": segment_ids, "ln1_gain": ln1_gain, "ln1_bias": ln1_bias, "w_query": w_query, "b_query": b_query, "w_key": w_key, "w_value": w_value, "b_value": b_value, "w_output": w_output, "b_output": b_output, "ln2_gain": ln2_gain, "ln2_bias": ln2_bias, "w_up": w_up, "b_up": b_up, "w_down": w_down, "b_down": b_down, "cotangent": cotangent}


@jax.custom_vjp
def low(v):
    return lax.optimization_barrier(v.astype(jnp.bfloat16)).astype(jnp.float32)

@jax.custom_vjp
def low_back(v):
    return v

def low_keep(v):
    return (low(v), None)

def low_pass(kept, grad):
    return (grad,)

def back_keep(v):
    return (v, None)

def back_low(kept, grad):
    return (low(grad),)
low.defvjp(low_keep, low_pass)
low_back.defvjp(back_keep, back_low)
EPSILON = 1e-06
MASKED = -1000000000.0

def layer_norm(values, gain_vec, shift_vec):
    row_mean = lax.optimization_barrier(jnp.mean(values, axis=-1, keepdims=True))
    centered = values - row_mean
    variance = lax.optimization_barrier(jnp.mean(centered * centered, axis=-1, keepdims=True))
    return centered * lax.rsqrt(variance + EPSILON) * gain_vec + shift_vec

def product(left, right):
    return jnp.dot(left, right, precision=lax.Precision.HIGHEST, preferred_element_type=jnp.float32)

def attend_group(pieces):
    queries, keys, values, segments = pieces
    raw = jnp.einsum('gqhe,gkhe->ghqk', queries, keys, precision=lax.Precision.HIGHEST)
    raw = low_back(raw)
    same = segments[:, None, :, None] == segments[:, None, None, :]
    scores = jnp.where(same, raw * (1.0 / math.sqrt(HD)), MASKED)
    highest = lax.optimization_barrier(jnp.max(scores, axis=-1, keepdims=True))
    expo = jnp.exp(scores - highest)
    probs = expo / lax.optimization_barrier(jnp.sum(expo, axis=-1, keepdims=True))
    return jnp.einsum('ghqk,gkhe->gqhe', low(probs), values, precision=lax.Precision.HIGHEST)

def forward(segment_ids, inputs, ln1_gain, ln1_bias, w_query, b_query, w_key, w_value, b_value, w_output, b_output, ln2_gain, ln2_bias, w_up, b_up, w_down, b_down):
    group_rows = math.gcd(ROWS, 16)
    blocks = ROWS // group_rows
    tokens_flat = inputs.reshape(ROWS * SEQ, D)
    normed = low(layer_norm(tokens_flat, ln1_gain, ln1_bias))
    queries = low(low_back(product(normed, w_query) + b_query))
    keys = low(low_back(product(normed, w_key)))
    values = low(low_back(product(normed, w_value) + b_value))
    shape_five = (blocks, group_rows, SEQ, HEADS, HD)
    context = lax.map(jax.checkpoint(attend_group), (queries.reshape(shape_five), keys.reshape(shape_five), values.reshape(shape_five), segment_ids.reshape(blocks, group_rows, SEQ)))
    context = low(low_back(context.reshape(ROWS * SEQ, D)))
    middle = tokens_flat + low_back(product(context, w_output)) + b_output
    normed_two = low(layer_norm(middle, ln2_gain, ln2_bias))
    upper = low_back(product(normed_two, w_up) + b_up)
    activated = low(jax.nn.gelu(upper, approximate=True))
    outcome = middle + low_back(product(activated, w_down)) + b_down
    return outcome.reshape(ROWS, SEQ, D)

def reference(inputs, segment_ids, ln1_gain, ln1_bias, w_query, b_query, w_key, w_value, b_value, w_output, b_output, ln2_gain, ln2_bias, w_up, b_up, w_down, b_down, cotangent):
    floats = tuple((array.astype(jnp.float32) for array in (inputs, ln1_gain, ln1_bias, w_query, b_query, w_key, w_value, b_value, w_output, b_output, ln2_gain, ln2_bias, w_up, b_up, w_down, b_down)))
    outcome, pullback = jax.vjp(partial(forward, segment_ids), *floats)
    grads = pullback(cotangent.astype(jnp.float32))
    return (outcome, grads[0], grads[1], grads[2], grads[3], grads[4], grads[5], grads[6], grads[7], grads[8], grads[9], grads[10], grads[11], grads[12], grads[13], grads[14], grads[15])
```

```python
from functools import partial
import math

import jax
import jax.numpy as jnp
from jax import lax
from jax.experimental import pallas as pl
from jax.experimental.pallas import tpu as pltpu
from jax.sharding import PartitionSpec as P

HD = 64


EPSILON = 1e-06
MASKED = -1000000000.0


def norm_parts(values, gain_vec, shift_vec):
    row_mean = jnp.mean(values, axis=-1, keepdims=True)
    centered = values - row_mean
    inv_std = lax.rsqrt(jnp.mean(centered * centered, axis=-1, keepdims=True) + EPSILON)
    unit_rows = centered * inv_std
    return (unit_rows * gain_vec + shift_vec, unit_rows, inv_std)


def norm_back(grad_out, unit_rows, inv_std, gain_vec):
    grad_gain = jnp.sum(grad_out * unit_rows, axis=0)
    grad_shift = jnp.sum(grad_out, axis=0)
    grad_unit = grad_out * gain_vec
    grad_in = inv_std * (
        grad_unit
        - jnp.mean(grad_unit, axis=-1, keepdims=True)
        - unit_rows * jnp.mean(grad_unit * unit_rows, axis=-1, keepdims=True)
    )
    return (grad_in, grad_gain, grad_shift)


def matmul(left, right):
    return jnp.dot(left, right, preferred_element_type=jnp.float32)


def left_product(left, right):
    return jnp.einsum("ta,tb->ab", left, right, preferred_element_type=jnp.float32)


def right_product(left, right):
    return jnp.einsum("tb,ab->ta", left, right, preferred_element_type=jnp.float32)


def sum_over_mp(part):
    size = lax.axis_size("mp")
    if size != 2:
        return lax.psum(part, "mp")
    return part + lax.ppermute(part, "mp", [(0, 1), (1, 0)])


def orders_for(kind, bits):
    low, rest = [1 << b for b in range(min(bits, 2))], [1 << b for b in range(2, bits)]
    if kind == "near":
        return [low + rest, low[::-1] + rest]
    return [rest[:1] + low + rest[1:], rest[:1] + low[::-1] + rest[1:]]


def order_of_member(orders, member):
    return orders[member % 2]


def block_table(orders, bits):
    me = lax.axis_index("dp")
    count = 1 << bits
    masks = []
    for order in orders:
        masks.append(
            [
                sum(order[k] for k in range(bits) if r >> (bits - 1 - k) & 1)
                for r in range(count)
            ]
        )
    masks = jnp.asarray(masks, jnp.int32)
    return masks[lax.axis_index("mp") % 2] ^ me.astype(jnp.int32)


def exchange(array, orders, stage):
    dp, mp = lax.axis_size("dp"), lax.axis_size("mp")
    pairs = []
    for d in range(dp):
        for m in range(mp):
            pairs.append((d * mp + m, (d ^ order_of_member(orders, m)[stage]) * mp + m))
    return lax.ppermute(array, ("dp", "mp"), pairs)


def finish_scatter(send, keep, orders, bits):
    received = []
    for stage in range(bits):
        received.append(exchange(send, orders, stage))
        half = keep.shape[0] >> (stage + 1)
        if stage + 1 < bits:
            send = keep[half : 2 * half]
            for got in received:
                send = send + got[half : 2 * half]
    total = keep[0]
    for got in received:
        total = total + got[0]
    return total


def all_sum(vector, bits):
    orders = orders_for("near", bits)
    for stage in range(bits):
        vector = vector + exchange(vector, orders, stage)
    return vector


def grad_kernel(table, left_ref, right_ref, *refs):
    outs, acc = refs[:-1], refs[-1]
    acc[...] = lax.dot_general(
        left_ref[...],
        right_ref[...],
        (((0,), (0,)), ((), ())),
        preferred_element_type=jnp.float32,
    )
    send, keep = outs
    half, size = keep.shape[0], keep.shape[1]
    for r in range(half):
        at = pl.multiple_of(table[r] * size, 8)
        keep[r] = acc[pl.ds(at, size), :]
        at = pl.multiple_of(table[half + r] * size, 8)
        send[r] = acc[pl.ds(at, size), :]


def blocked_grad(table, left, right, start, columns, tile):
    tokens, width = left.shape
    count = table.shape[0]
    size = width // count
    shape = jax.ShapeDtypeStruct((count // 2, size, columns), jnp.float32)
    block = pl.BlockSpec((count // 2, size, tile), lambda i, t: (0, 0, i))
    first = start // tile
    return pl.pallas_call(
        grad_kernel,
        grid_spec=pltpu.PrefetchScalarGridSpec(
            num_scalar_prefetch=1,
            grid=(columns // tile,),
            in_specs=[
                pl.BlockSpec((tokens, width), lambda i, t: (0, 0)),
                pl.BlockSpec((tokens, tile), lambda i, t: (0, i + first)),
            ],
            out_specs=[block, block],
            scratch_shapes=[pltpu.VMEM((width, tile), jnp.float32)],
        ),
        out_shape=[shape, shape],
        cost_estimate=pl.CostEstimate(
            flops=2 * tokens * width * columns,
            bytes_accessed=2 * tokens * (width + columns) + 4 * width * columns,
            transcendentals=0,
        ),
        compiler_params=pltpu.CompilerParams(vmem_limit_bytes=40 << 20),
    )(table, left, right)


def scattered_grad(left, right, kind, start, columns, tile):
    dp = lax.axis_size("dp")
    bits = dp.bit_length() - 1
    size = left.shape[1] // dp
    if (1 << bits) != dp or size % 8 or bits < 3:
        part = left_product(left, right[:, start : start + columns])
        return lax.psum_scatter(part, "dp", scatter_dimension=0, tiled=True)
    orders = orders_for(kind, bits)
    table = block_table(orders, bits)
    send, keep = blocked_grad(table, left, right, start, columns, tile)
    return finish_scatter(send, keep, orders, bits)


def sum_small(parts):
    dp = lax.axis_size("dp")
    bits = dp.bit_length() - 1
    if (1 << bits) != dp:
        return lax.psum(parts, "dp")
    sizes = [part.shape[0] for part in parts]
    flat = jnp.concatenate(parts).reshape(-1, 128)
    flat = all_sum(flat, bits).reshape(-1)
    out, at = [], 0
    for size in sizes:
        out.append(flat[at : at + size])
        at += size
    return out


def on_device(
    inputs,
    segment_ids,
    ln1_gain,
    ln1_bias,
    w_query,
    b_query,
    w_key,
    w_value,
    b_value,
    w_output,
    b_output,
    ln2_gain,
    ln2_bias,
    w_up,
    b_up,
    w_down,
    b_down,
    cotangent,
):
    rows, length, width = inputs.shape
    local_cols = w_query.shape[1]
    local_heads = local_cols // HD
    tokens = rows * length
    scale = 1.0 / math.sqrt(HD)
    tokens_flat = inputs.reshape(tokens, width)
    normed, unit_one, inv_one = norm_parts(tokens_flat, ln1_gain, ln1_bias)
    normed_b = normed.astype(jnp.bfloat16)
    queries = (matmul(normed_b, w_query) + b_query).astype(jnp.bfloat16)
    keys_b = matmul(normed_b, w_key).astype(jnp.bfloat16)
    values_b = (matmul(normed_b, w_value) + b_value).astype(jnp.bfloat16)
    head_shape = (rows, length, local_heads, HD)
    query_four = queries.reshape(head_shape)
    key_four = keys_b.reshape(head_shape)
    value_four = values_b.reshape(head_shape)
    same = segment_ids[:, None, :, None] == segment_ids[:, None, None, :]

    def scores_of(first, second):
        raw = jnp.einsum("rqhe,rkhe->rhqk", first, second, preferred_element_type=jnp.float32)
        return jnp.where(same, raw * scale, MASKED)

    scores = scores_of(query_four, key_four)
    highest = jnp.max(scores, axis=-1, keepdims=True)
    expo = jnp.exp(scores - highest)
    totals = jnp.sum(expo, axis=-1, keepdims=True)
    probs = expo / totals
    log_total = highest + jnp.log(totals)
    context = jnp.einsum(
        "rhqk,rkhe->rqhe",
        probs.astype(jnp.bfloat16),
        value_four,
        preferred_element_type=jnp.float32,
    )
    context_b = context.reshape(tokens, local_cols).astype(jnp.bfloat16)
    attn_out = sum_over_mp(matmul(context_b, w_output))
    middle = tokens_flat + attn_out + b_output
    normed_two, unit_two, inv_two = norm_parts(middle, ln2_gain, ln2_bias)
    normed_two_b = normed_two.astype(jnp.bfloat16)
    upper = matmul(normed_two_b, w_up) + b_up
    activated, gelu_pull = jax.vjp(partial(jax.nn.gelu, approximate=True), upper)
    activated_b = activated.astype(jnp.bfloat16)
    down_out = sum_over_mp(matmul(activated_b, w_down))
    outcome = middle + down_out + b_down
    grad_top = cotangent.reshape(tokens, width)
    grad_top_b = grad_top.astype(jnp.bfloat16)
    hidden = w_up.shape[1]
    far = hidden // 3
    down_near = scattered_grad(grad_top_b, activated_b, "near", 0, hidden - far, far)
    down_far = scattered_grad(grad_top_b, activated_b, "far", hidden - far, far, far)
    grad_b_down = jnp.sum(grad_top, axis=0)
    grad_act = right_product(grad_top_b, w_down)
    grad_upper = gelu_pull(grad_act)[0].astype(jnp.bfloat16)
    up_near = scattered_grad(normed_two_b, grad_upper, "near", 0, hidden - far, far)
    up_far = scattered_grad(normed_two_b, grad_upper, "far", hidden - far, far, far)
    grad_b_up = jnp.sum(grad_upper.astype(jnp.float32), axis=0)
    grad_norm_two = sum_over_mp(right_product(grad_upper, w_up))
    grad_mid_part, grad_ln2_gain, grad_ln2_bias = norm_back(
        grad_norm_two, unit_two, inv_two, ln2_gain
    )
    grad_middle = grad_top + grad_mid_part
    grad_middle_b = grad_middle.astype(jnp.bfloat16)
    grad_b_output = jnp.sum(grad_middle, axis=0)
    out_part = scattered_grad(grad_middle_b, context_b, "far", 0, local_cols, local_cols)
    grad_context = right_product(grad_middle_b, w_output).astype(jnp.bfloat16).reshape(head_shape)
    again = jnp.exp(scores_of(query_four, key_four) - log_total)
    grad_probs = jnp.einsum(
        "rqhe,rkhe->rhqk", grad_context, value_four, preferred_element_type=jnp.float32
    )
    grad_values = jnp.einsum(
        "rhqk,rqhe->rkhe",
        again.astype(jnp.bfloat16),
        grad_context,
        preferred_element_type=jnp.float32,
    ).astype(jnp.bfloat16)
    row_delta = jnp.sum(again * grad_probs, axis=-1, keepdims=True)
    grad_scores = (again * (grad_probs - row_delta) * scale).astype(jnp.bfloat16)
    grad_queries = jnp.einsum(
        "rhqk,rkhe->rqhe", grad_scores, key_four, preferred_element_type=jnp.float32
    ).astype(jnp.bfloat16)
    grad_keys = jnp.einsum(
        "rhqk,rqhe->rkhe", grad_scores, query_four, preferred_element_type=jnp.float32
    ).astype(jnp.bfloat16)
    grad_queries = grad_queries.reshape(tokens, local_cols)
    grad_keys = grad_keys.reshape(tokens, local_cols)
    grad_values = grad_values.reshape(tokens, local_cols)
    out_value = scattered_grad(normed_b, grad_values, "far", 0, local_cols, local_cols)
    two = jnp.concatenate([grad_queries, grad_keys], axis=1)
    pair = scattered_grad(normed_b, two, "near", 0, 2 * local_cols, local_cols)
    out_query, out_key = pair[:, :local_cols], pair[:, local_cols:]
    grad_b_query = jnp.sum(grad_queries.astype(jnp.float32), axis=0)
    grad_b_value = jnp.sum(grad_values.astype(jnp.float32), axis=0)
    partial_norm = (
        right_product(grad_queries, w_query)
        + right_product(grad_keys, w_key)
        + right_product(grad_values, w_value)
    )
    grad_norm_one = sum_over_mp(partial_norm)
    grad_in_part, grad_ln1_gain, grad_ln1_bias = norm_back(
        grad_norm_one, unit_one, inv_one, ln1_gain
    )
    grad_inputs = grad_middle + grad_in_part
    out_up = jnp.concatenate([up_near, up_far], axis=1)
    out_down = jnp.concatenate([down_near, down_far], axis=1).T
    out_output = out_part.T
    smalls = sum_small(
        (
            grad_ln1_gain,
            grad_ln1_bias,
            grad_b_query,
            grad_b_value,
            grad_b_output,
            grad_ln2_gain,
            grad_ln2_bias,
            grad_b_up,
            grad_b_down,
        )
    )
    return (
        outcome.reshape(rows, length, width),
        grad_inputs.reshape(rows, length, width),
        smalls[0],
        smalls[1],
        out_query,
        smalls[2],
        out_key,
        out_value,
        smalls[3],
        out_output,
        smalls[4],
        smalls[5],
        smalls[6],
        out_up,
        smalls[7],
        out_down,
        smalls[8],
    )


def solution(mesh):
    return jax.shard_map(
        on_device,
        mesh=mesh,
        in_specs=(
            P("dp", None, None),
            P("dp", None),
            P(),
            P(),
            P(None, "mp"),
            P("mp"),
            P(None, "mp"),
            P(None, "mp"),
            P("mp"),
            P("mp", None),
            P(),
            P(),
            P(),
            P(None, "mp"),
            P("mp"),
            P("mp", None),
            P(),
            P("dp", None, None),
        ),
        out_specs=(
            P("dp", None, None),
            P("dp", None, None),
            P(),
            P(),
            P("dp", "mp"),
            P("mp"),
            P("dp", "mp"),
            P("dp", "mp"),
            P("mp"),
            P("mp", "dp"),
            P(),
            P(),
            P(),
            P("dp", "mp"),
            P("mp"),
            P("mp", "dp"),
            P(),
        ),
        check_vma=False,
    )
```

```python
import math

import jax
import jax.numpy as jnp
from jax import lax
from jax.experimental import pallas as pl
from jax.experimental.pallas import tpu as pltpu
from jax.sharding import PartitionSpec as P

HD = 64
PAIR = 2 * HD
EPSILON = 1e-06
MASKED = -1000000000.0
SCALE = 1.0 / math.sqrt(HD)
CURVE = math.sqrt(2.0 / math.pi)
CUBIC = 0.044715
F32 = jnp.float32
BF16 = jnp.bfloat16


def product(left, right, over):
    return lax.dot_general(
        left, right, ((over[:1], over[1:]), ((), ())), preferred_element_type=F32
    )


def left_product(left, right):
    return product(left, right, (0, 0))


def unit_rows(values):
    centered = values - jnp.mean(values, axis=-1, keepdims=True)
    inv_std = lax.rsqrt(jnp.mean(centered * centered, axis=-1, keepdims=True) + EPSILON)
    return centered * inv_std, inv_std


def norm_back(grad_out, unit, inv_std, gain):
    grad_unit = grad_out * gain
    return inv_std * (
        grad_unit
        - jnp.mean(grad_unit, axis=-1, keepdims=True)
        - unit * jnp.mean(grad_unit * unit, axis=-1, keepdims=True)
    )


def column_sum(values):
    return jnp.sum(values, axis=0, keepdims=True)


def add_up(ref, value):
    @pl.when(pl.program_id(0) == 0)
    def _():
        ref[...] = jnp.zeros_like(ref)

    ref[...] += value


def lane_halves(width):
    lane = lax.broadcasted_iota(jnp.int32, (1, width), 1)
    low = (lane % PAIR < HD).astype(F32)
    return low, 1.0 - low


def attend_kernel(
    x_ref, seg_col, seg_row, gain, shift, wq, bq, wk, wv, bv, wo,
    normed_ref, qkv_ref, probs_ref, context_ref, out_ref,
):
    cols = wq.shape[1]
    unit, _ = unit_rows(x_ref[...])
    normed = (unit * gain[...] + shift[...]).astype(BF16)
    normed_ref[...] = normed
    low, high = lane_halves(cols)
    queries = (product(normed, wq[...], (1, 0)) + bq[...]) * SCALE
    keys = product(normed, wk[...], (1, 0)).astype(BF16)
    values = (product(normed, wv[...], (1, 0)) + bv[...]).astype(BF16)
    qkv_ref[:, :cols] = queries.astype(BF16)
    qkv_ref[:, cols : 2 * cols] = keys
    qkv_ref[:, 2 * cols :] = values
    split = ((queries * low).astype(BF16), (queries * high).astype(BF16))
    same = seg_col[0] == seg_row[0]
    first = lax.broadcasted_iota(jnp.int32, (1, PAIR), 1) < HD
    for pair in range(cols // PAIR):
        part = slice(pair * PAIR, (pair + 1) * PAIR)
        made = []
        for half in range(2):
            scores = product(keys[:, part], split[half][:, part], (1, 1))
            scores = jnp.where(same, scores, MASKED)
            expo = jnp.exp(scores - jnp.max(scores, axis=0, keepdims=True))
            probs = (expo * (1.0 / column_sum(expo))).astype(BF16)
            probs_ref[0, 2 * pair + half] = probs
            made.append(product(probs, values[:, part], (0, 0)))
        context_ref[:, part] = jnp.where(first, made[0], made[1]).astype(BF16)
    out_ref[...] = product(context_ref[...], wo[...], (1, 0))


def whole(array):
    zeros = (0,) * array.ndim
    return pl.BlockSpec(array.shape, lambda i: zeros, pipeline_mode=pl.Buffered(1))


def rows_of(length, width):
    return pl.BlockSpec((length, width), lambda i: (i, 0))


def cost(flops, moved, special=0):
    return pl.CostEstimate(flops=flops, bytes_accessed=moved, transcendentals=special)


def params():
    return pltpu.CompilerParams(vmem_limit_bytes=48 << 20)


def attend(x, segments, gain, shift, wq, bq, wk, wv, bv, wo):
    rows, length = segments.shape
    tokens, width = x.shape
    cols = wq.shape[1]
    heads = cols // HD
    made = lambda w, kind: jax.ShapeDtypeStruct((tokens, w), kind)
    return pl.pallas_call(
        attend_kernel,
        grid=(rows,),
        in_specs=[
            rows_of(length, width),
            pl.BlockSpec((1, length, 1), lambda i: (i, 0, 0)),
            pl.BlockSpec((1, 1, length), lambda i: (i, 0, 0)),
        ]
        + [whole(w) for w in (gain, shift, wq, bq, wk, wv, bv, wo)],
        out_specs=[
            rows_of(length, width),
            rows_of(length, 3 * cols),
            pl.BlockSpec((1, heads, length, length), lambda i: (i, 0, 0, 0)),
            rows_of(length, cols),
            rows_of(length, width),
        ],
        out_shape=[
            made(width, BF16),
            made(3 * cols, BF16),
            jax.ShapeDtypeStruct((rows, heads, length, length), BF16),
            made(cols, BF16),
            made(width, F32),
        ],
        cost_estimate=cost(
            8 * tokens * width * cols + 4 * tokens * length * cols,
            tokens * (10 * width + 8 * cols + 2 * heads * length) + 8 * width * cols,
            tokens * heads * length,
        ),
        compiler_params=params(),
    )(x, segments[:, :, None], segments[:, None, :], gain, shift, wq, bq, wk, wv, bv, wo)


def upper_kernel(
    x_ref, mine, other, bias, gain, shift, w_up, b_up,
    middle_ref, normed_ref, act_ref, slope_ref, *, step,
):
    middle = x_ref[...] + (mine[...] + other[...]) + bias[...]
    middle_ref[...] = middle
    unit, _ = unit_rows(middle)
    normed = (unit * gain[...] + shift[...]).astype(BF16)
    normed_ref[...] = normed
    for at in range(0, w_up.shape[1], step):
        part = slice(at, at + step)
        u = product(normed, w_up[:, part], (1, 0)) + b_up[:, part]
        square = u * u
        bend = jnp.tanh(u * (CURVE + (CURVE * CUBIC) * square))
        half = 0.5 + 0.5 * bend
        act = u * half
        act_ref[:, part] = act.astype(BF16)
        slope = half + act * (1.0 - bend) * (CURVE + (3.0 * CURVE * CUBIC) * square)
        slope_ref[:, part] = slope.astype(BF16)


def upper(x, mine, other, bias, gain, shift, w_up, b_up, length):
    tokens, width = x.shape
    hidden = w_up.shape[1]
    made = lambda w, kind: jax.ShapeDtypeStruct((tokens, w), kind)
    return pl.pallas_call(
        lambda *refs: upper_kernel(*refs, step=hidden // 6),
        grid=(tokens // length,),
        in_specs=[rows_of(length, width)] * 3
        + [whole(w) for w in (bias, gain, shift, w_up, b_up)],
        out_specs=[
            rows_of(length, width),
            rows_of(length, width),
            rows_of(length, hidden),
            rows_of(length, hidden),
        ],
        out_shape=[made(width, F32), made(width, BF16), made(hidden, BF16), made(hidden, BF16)],
        cost_estimate=cost(
            2 * tokens * width * hidden,
            tokens * (18 * width + 4 * hidden) + 2 * width * hidden,
            tokens * hidden,
        ),
        compiler_params=params(),
    )(x, mine, other, bias, gain, shift, w_up, b_up)


def hidden_kernel(
    top_ref, act_ref, slope_ref, w_down, w_up,
    grad_ref, down_ref, back_ref, bias_ref, *, step,
):
    sums = []
    for at in range(0, w_up.shape[1], step):
        part = slice(at, at + step)
        grad = product(top_ref[...], w_down[part, :], (1, 1)) * slope_ref[:, part].astype(F32)
        grad = grad.astype(BF16)
        grad_ref[:, part] = grad
        sums.append(column_sum(grad.astype(F32)))
    add_up(bias_ref, jnp.concatenate(sums, axis=1))
    back_ref[...] = product(grad_ref[...], w_up[...], (1, 1))
    down_ref[...] = product(act_ref[...], w_down[...], (1, 0))


def hidden_back(top, act, slope, w_down, w_up, length):
    tokens, width = top.shape
    hidden = w_up.shape[1]
    made = lambda w, kind: jax.ShapeDtypeStruct((tokens, w), kind)
    return pl.pallas_call(
        lambda *refs: hidden_kernel(*refs, step=hidden // 6),
        grid=(tokens // length,),
        in_specs=[rows_of(length, width), rows_of(length, hidden), rows_of(length, hidden)]
        + [whole(w) for w in (w_down, w_up)],
        out_specs=[
            rows_of(length, hidden),
            rows_of(length, width),
            rows_of(length, width),
            pl.BlockSpec((1, hidden), lambda i: (0, 0)),
        ],
        out_shape=[
            made(hidden, BF16),
            made(width, F32),
            made(width, F32),
            jax.ShapeDtypeStruct((1, hidden), F32),
        ],
        cost_estimate=cost(
            6 * tokens * width * hidden,
            tokens * (10 * width + 6 * hidden) + 4 * width * hidden,
        ),
        compiler_params=params(),
    )(top, act, slope, w_down, w_up)


def attend_back_kernel(
    top_ref, mine, other, middle_ref, gain, wo, qkv_ref, probs_ref, wq, wk, wv,
    grad_middle_ref, rounded_ref, grad_qkv_ref, back_ref,
    sum_gain, sum_shift, sum_out, sum_qkv,
):
    cols = wq.shape[1]
    unit, inv_std = unit_rows(middle_ref[...])
    grad_normed = mine[...] + other[...]
    add_up(sum_gain, column_sum(grad_normed * unit))
    add_up(sum_shift, column_sum(grad_normed))
    grad_middle = top_ref[...] + norm_back(grad_normed, unit, inv_std, gain[...])
    grad_middle_ref[...] = grad_middle
    add_up(sum_out, column_sum(grad_middle))
    rounded = grad_middle.astype(BF16)
    rounded_ref[...] = rounded
    grad_context = product(rounded, wo[...], (1, 1)).astype(BF16).astype(F32)
    low, high = lane_halves(cols)
    split = ((grad_context * low).astype(BF16), (grad_context * high).astype(BF16))
    first = lax.broadcasted_iota(jnp.int32, (1, PAIR), 1) < HD
    for pair in range(cols // PAIR):
        at = pair * PAIR
        query = qkv_ref[:, at : at + PAIR]
        key = qkv_ref[:, cols + at : cols + at + PAIR]
        value = qkv_ref[:, 2 * cols + at : 2 * cols + at + PAIR]
        to_query, to_key, to_value = [], [], []
        for half in range(2):
            grad_out = split[half][:, at : at + PAIR]
            probs = probs_ref[0, 2 * pair + half]
            wide = probs.astype(F32)
            grad_probs = product(value, grad_out, (1, 1))
            delta = column_sum(wide * grad_probs)
            grad_scores = (wide * (grad_probs - delta)).astype(BF16)
            to_value.append(product(probs, grad_out, (1, 0)))
            to_key.append(product(grad_scores, query, (1, 0)))
            to_query.append(product(grad_scores, key, (0, 0)))
        grad_query = jnp.where(first, to_query[0], to_query[1]) * SCALE
        grad_key = jnp.where(first, to_key[0], to_key[1])
        grad_value = to_value[0] + to_value[1]
        grad_qkv_ref[:, at : at + PAIR] = grad_query.astype(BF16)
        grad_qkv_ref[:, cols + at : cols + at + PAIR] = grad_key.astype(BF16)
        grad_qkv_ref[:, 2 * cols + at : 2 * cols + at + PAIR] = grad_value.astype(BF16)
    grads = grad_qkv_ref[...]
    add_up(sum_qkv, column_sum(grads.astype(F32)))
    back_ref[...] = (
        product(grads[:, :cols], wq[...], (1, 1))
        + product(grads[:, cols : 2 * cols], wk[...], (1, 1))
        + product(grads[:, 2 * cols :], wv[...], (1, 1))
    )


def attend_back(top, mine, other, middle, gain, wo, qkv, probs, wq, wk, wv):
    tokens, width = top.shape
    rows, heads, length, _ = probs.shape
    cols = wq.shape[1]
    made = lambda w, kind: jax.ShapeDtypeStruct((tokens, w), kind)
    line = lambda w: jax.ShapeDtypeStruct((1, w), F32)
    fixed = lambda w: pl.BlockSpec((1, w), lambda i: (0, 0))
    return pl.pallas_call(
        attend_back_kernel,
        grid=(rows,),
        in_specs=[rows_of(length, width)] * 4
        + [whole(gain), whole(wo), rows_of(length, 3 * cols)]
        + [pl.BlockSpec((1, heads, length, length), lambda i: (i, 0, 0, 0))]
        + [whole(w) for w in (wq, wk, wv)],
        out_specs=[
            rows_of(length, width),
            rows_of(length, width),
            rows_of(length, 3 * cols),
            rows_of(length, width),
            fixed(width),
            fixed(width),
            fixed(width),
            fixed(3 * cols),
        ],
        out_shape=[
            made(width, F32),
            made(width, BF16),
            made(3 * cols, BF16),
            made(width, F32),
            line(width),
            line(width),
            line(width),
            line(3 * cols),
        ],
        cost_estimate=cost(
            8 * tokens * width * cols + 8 * tokens * length * cols,
            tokens * (26 * width + 12 * cols + 2 * heads * length) + 8 * width * cols,
        ),
        compiler_params=params(),
    )(top, mine, other, middle, gain, wo, qkv, probs, wq, wk, wv)


def first_back_kernel(x_ref, mine, other, above, gain, out_ref, sum_gain, sum_shift):
    unit, inv_std = unit_rows(x_ref[...])
    grad_normed = mine[...] + other[...]
    add_up(sum_gain, column_sum(grad_normed * unit))
    add_up(sum_shift, column_sum(grad_normed))
    out_ref[...] = above[...] + norm_back(grad_normed, unit, inv_std, gain[...])


def first_back(x, mine, other, above, gain, length):
    tokens, width = x.shape
    line = jax.ShapeDtypeStruct((1, width), F32)
    fixed = pl.BlockSpec((1, width), lambda i: (0, 0))
    return pl.pallas_call(
        first_back_kernel,
        grid=(tokens // length,),
        in_specs=[rows_of(length, width)] * 4 + [whole(gain)],
        out_specs=[rows_of(length, width), fixed, fixed],
        out_shape=[jax.ShapeDtypeStruct((tokens, width), F32), line, line],
        cost_estimate=cost(20 * tokens * width, 20 * tokens * width),
        compiler_params=params(),
    )(x, mine, other, above, gain)


def from_partner(part):
    return lax.ppermute(part, "mp", [(0, 1), (1, 0)])


def orders_for(kind, bits):
    low, rest = [1 << b for b in range(min(bits, 2))], [1 << b for b in range(2, bits)]
    if kind == "near":
        return [low + rest, low[::-1] + rest]
    return [rest[:1] + low + rest[1:], rest[:1] + low[::-1] + rest[1:]]


def order_of_member(orders, member):
    return orders[member % 2]


def block_table(orders, bits):
    me = lax.axis_index("dp")
    count = 1 << bits
    masks = []
    for order in orders:
        masks.append(
            [
                sum(order[k] for k in range(bits) if r >> (bits - 1 - k) & 1)
                for r in range(count)
            ]
        )
    masks = jnp.asarray(masks, jnp.int32)
    return masks[lax.axis_index("mp") % 2] ^ me.astype(jnp.int32)


def exchange(array, orders, stage):
    dp, mp = lax.axis_size("dp"), lax.axis_size("mp")
    pairs = []
    for d in range(dp):
        for m in range(mp):
            pairs.append((d * mp + m, (d ^ order_of_member(orders, m)[stage]) * mp + m))
    return lax.ppermute(array, ("dp", "mp"), pairs)


def finish_scatter(send, keep, orders, bits):
    received = []
    for stage in range(bits):
        received.append(exchange(send, orders, stage))
        half = keep.shape[0] >> (stage + 1)
        if stage + 1 < bits:
            send = keep[half : 2 * half]
            for got in received:
                send = send + got[half : 2 * half]
    total = keep[0]
    for got in received:
        total = total + got[0]
    return total


def all_sum(vector, bits):
    orders = orders_for("near", bits)
    for stage in range(bits):
        vector = vector + exchange(vector, orders, stage)
    return vector


def grad_kernel(table, left_ref, right_ref, *refs):
    outs, acc = refs[:-1], refs[-1]
    acc[...] = lax.dot_general(
        left_ref[...],
        right_ref[...],
        (((0,), (0,)), ((), ())),
        preferred_element_type=jnp.float32,
    )
    send, keep = outs
    half, size = keep.shape[0], keep.shape[1]
    for r in range(half):
        at = pl.multiple_of(table[r] * size, 8)
        keep[r] = acc[pl.ds(at, size), :]
        at = pl.multiple_of(table[half + r] * size, 8)
        send[r] = acc[pl.ds(at, size), :]


def blocked_grad(table, left, right, start, columns, tile):
    tokens, width = left.shape
    count = table.shape[0]
    size = width // count
    shape = jax.ShapeDtypeStruct((count // 2, size, columns), jnp.float32)
    block = pl.BlockSpec((count // 2, size, tile), lambda i, t: (0, 0, i))
    first = start // tile
    return pl.pallas_call(
        grad_kernel,
        grid_spec=pltpu.PrefetchScalarGridSpec(
            num_scalar_prefetch=1,
            grid=(columns // tile,),
            in_specs=[
                pl.BlockSpec((tokens, width), lambda i, t: (0, 0)),
                pl.BlockSpec((tokens, tile), lambda i, t: (0, i + first)),
            ],
            out_specs=[block, block],
            scratch_shapes=[pltpu.VMEM((width, tile), jnp.float32)],
        ),
        out_shape=[shape, shape],
        cost_estimate=pl.CostEstimate(
            flops=2 * tokens * width * columns,
            bytes_accessed=2 * tokens * (width + columns) + 4 * width * columns,
            transcendentals=0,
        ),
        compiler_params=pltpu.CompilerParams(vmem_limit_bytes=40 << 20),
    )(table, left, right)


def scattered_grad(left, right, kind, start, columns, tile):
    dp = lax.axis_size("dp")
    bits = dp.bit_length() - 1
    size = left.shape[1] // dp
    if (1 << bits) != dp or size % 8 or bits < 3:
        part = left_product(left, right[:, start : start + columns])
        return lax.psum_scatter(part, "dp", scatter_dimension=0, tiled=True)
    orders = orders_for(kind, bits)
    table = block_table(orders, bits)
    send, keep = blocked_grad(table, left, right, start, columns, tile)
    return finish_scatter(send, keep, orders, bits)


def sum_small(parts):
    dp = lax.axis_size("dp")
    bits = dp.bit_length() - 1
    if (1 << bits) != dp:
        return lax.psum(parts, "dp")
    sizes = [part.shape[0] for part in parts]
    flat = jnp.concatenate(parts).reshape(-1, 128)
    flat = all_sum(flat, bits).reshape(-1)
    out, at = [], 0
    for size in sizes:
        out.append(flat[at : at + size])
        at += size
    return out


def on_device(
    inputs,
    segment_ids,
    ln1_gain,
    ln1_bias,
    w_query,
    b_query,
    w_key,
    w_value,
    b_value,
    w_output,
    b_output,
    ln2_gain,
    ln2_bias,
    w_up,
    b_up,
    w_down,
    b_down,
    cotangent,
):
    rows, length, width = inputs.shape
    cols = w_query.shape[1]
    tokens = rows * length
    hidden = w_up.shape[1]
    far = hidden // 3
    row = lambda vector: vector.reshape(1, -1)
    x = inputs.reshape(tokens, width)
    top = cotangent.reshape(tokens, width)
    normed, qkv, probs, context, out_mine = attend(
        x, segment_ids, row(ln1_gain), row(ln1_bias), w_query, row(b_query),
        w_key, w_value, row(b_value), w_output,
    )
    out_other = from_partner(out_mine)
    top_b = top.astype(BF16)
    middle, normed_two, act, slope = upper(
        x, out_mine, out_other, row(b_output), row(ln2_gain), row(ln2_bias), w_up, row(b_up), length
    )
    down_far = scattered_grad(top_b, act, "far", hidden - far, far, far)
    down_near = scattered_grad(top_b, act, "near", 0, hidden - far, far)
    grad_upper, down_mine, back_mine, sum_up = hidden_back(top_b, act, slope, w_down, w_up, length)
    back_other = from_partner(back_mine)
    down_other = from_partner(down_mine)
    up_far = scattered_grad(normed_two, grad_upper, "far", hidden - far, far, far)
    up_near = scattered_grad(normed_two, grad_upper, "near", 0, hidden - far, far)
    outcome = middle + (down_mine + down_other) + b_down
    (
        grad_middle, grad_middle_b, grad_qkv, first_mine,
        sum_gain_two, sum_shift_two, sum_out, sum_qkv,
    ) = attend_back(
        top, back_mine, back_other, middle, row(ln2_gain), w_output, qkv, probs,
        w_query, w_key, w_value,
    )
    first_other = from_partner(first_mine)
    out_value = scattered_grad(normed, grad_qkv, "far", 2 * cols, cols, cols)
    pair = scattered_grad(normed, grad_qkv, "near", 0, 2 * cols, cols)
    out_part = scattered_grad(grad_middle_b, context, "far", 0, cols, cols)
    grad_x, sum_gain_one, sum_shift_one = first_back(
        x, first_mine, first_other, grad_middle, row(ln1_gain), length
    )
    smalls = sum_small(
        (
            sum_gain_one[0],
            sum_shift_one[0],
            sum_qkv[0, :cols],
            sum_qkv[0, 2 * cols :],
            sum_out[0],
            sum_gain_two[0],
            sum_shift_two[0],
            sum_up[0],
            jnp.sum(top, axis=0),
        )
    )
    shape = inputs.shape
    return (
        outcome.reshape(shape),
        grad_x.reshape(shape),
        smalls[0],
        smalls[1],
        pair[:, :cols],
        smalls[2],
        pair[:, cols:],
        out_value,
        smalls[3],
        out_part.T,
        smalls[4],
        smalls[5],
        smalls[6],
        jnp.concatenate([up_near, up_far], axis=1),
        smalls[7],
        jnp.concatenate([down_near, down_far], axis=1).T,
        smalls[8],
    )


def solution(mesh):
    return jax.shard_map(
        on_device,
        mesh=mesh,
        in_specs=(
            P("dp", None, None),
            P("dp", None),
            P(),
            P(),
            P(None, "mp"),
            P("mp"),
            P(None, "mp"),
            P(None, "mp"),
            P("mp"),
            P("mp", None),
            P(),
            P(),
            P(),
            P(None, "mp"),
            P("mp"),
            P("mp", None),
            P(),
            P("dp", None, None),
        ),
        out_specs=(
            P("dp", None, None),
            P("dp", None, None),
            P(),
            P(),
            P("dp", "mp"),
            P("mp"),
            P("dp", "mp"),
            P("dp", "mp"),
            P("mp"),
            P("mp", "dp"),
            P(),
            P(),
            P(),
            P("dp", "mp"),
            P("mp"),
            P("mp", "dp"),
            P(),
        ),
        check_vma=False,
    )
```

```python
import math

import jax
import jax.numpy as jnp
from jax import lax
from jax.experimental import pallas as pl
from jax.experimental.pallas import tpu as pltpu
from jax.sharding import PartitionSpec as P

HD = 64
PAIR = 2 * HD
EPSILON = 1e-06
MASKED = -1000000000.0
SCALE = 1.0 / math.sqrt(HD)
CURVE = math.sqrt(2.0 / math.pi)
CUBIC = 0.044715
WEIGHT = 60
F32 = jnp.float32
BF16 = jnp.bfloat16


def product(left, right, over):
    return lax.dot_general(
        left, right, ((over[:1], over[1:]), ((), ())), preferred_element_type=F32
    )


def left_product(left, right):
    return product(left, right, (0, 0))


def unit_rows(values):
    centered = values - jnp.mean(values, axis=-1, keepdims=True)
    inv_std = lax.rsqrt(jnp.mean(centered * centered, axis=-1, keepdims=True) + EPSILON)
    return centered * inv_std, inv_std


def norm_back(grad_out, unit, inv_std, gain):
    grad_unit = grad_out * gain
    return inv_std * (
        grad_unit
        - jnp.mean(grad_unit, axis=-1, keepdims=True)
        - unit * jnp.mean(grad_unit * unit, axis=-1, keepdims=True)
    )


def column_sum(values):
    return jnp.sum(values, axis=0, keepdims=True)


def line(ref):
    return jnp.concatenate([ref[r : r + 1, :] for r in range(ref.shape[0])], axis=1)


def add_up(ref, value):
    @pl.when(pl.program_id(0) == 0)
    def _():
        ref[...] = jnp.zeros_like(ref)

    ref[...] += value


def lane_halves(width):
    lane = lax.broadcasted_iota(jnp.int32, (1, width), 1)
    low = (lane % PAIR < HD).astype(F32)
    return low, 1.0 - low


def attend_kernel(
    seg_ref, gain, shift, wq, bq, wk, wv, bv, wo, x_ref, *refs, first_row
):
    normed_ref, qkv_ref, probs_ref, context_ref, out_ref = refs[-5:]
    cols = wq.shape[1]
    unit, _ = unit_rows(x_ref[...])
    normed = (unit * line(gain) + line(shift)).astype(BF16)
    normed_ref[...] = normed
    low, high = lane_halves(cols)
    queries = (product(normed, wq[...], (1, 0)) + line(bq)) * SCALE
    keys = product(normed, wk[...], (1, 0)).astype(BF16)
    values = (product(normed, wv[...], (1, 0)) + line(bv)).astype(BF16)
    qkv_ref[:, :cols] = queries.astype(BF16)
    qkv_ref[:, cols : 2 * cols] = keys
    qkv_ref[:, 2 * cols :] = values
    split = ((queries * low).astype(BF16), (queries * high).astype(BF16))
    seg_row = seg_ref[pl.ds(pl.program_id(0) + first_row, 1), :].astype(F32)
    length = seg_row.shape[1]
    seg_col = jnp.broadcast_to(seg_row, (128, length)).T
    same = jnp.concatenate([seg_col] * (length // 128), axis=1) == seg_row
    first = lax.broadcasted_iota(jnp.int32, (1, PAIR), 1) < HD
    for pair in range(cols // PAIR):
        part = slice(pair * PAIR, (pair + 1) * PAIR)
        made = []
        for half in range(2):
            scores = product(keys[:, part], split[half][:, part], (1, 1))
            scores = jnp.where(same, scores, MASKED)
            expo = jnp.exp(scores - jnp.max(scores, axis=0, keepdims=True))
            probs = (expo * (1.0 / column_sum(expo))).astype(BF16)
            probs_ref[0, 2 * pair + half] = probs
            made.append(product(probs, values[:, part], (0, 0)))
        context_ref[:, part] = jnp.where(first, made[0], made[1]).astype(BF16)
    out_ref[...] = product(context_ref[...], wo[...], (1, 0))


def whole(array):
    zeros = (0,) * array.ndim
    return pl.BlockSpec(array.shape, lambda i: zeros, pipeline_mode=pl.Buffered(1))


def rows_of(length, width):
    return pl.BlockSpec((length, width), lambda i: (i, 0))


def cost(flops, moved, special=0):
    return pl.CostEstimate(
        flops=WEIGHT * flops, bytes_accessed=WEIGHT * moved, transcendentals=special
    )


def params(limit=26 << 20):
    return pltpu.CompilerParams(vmem_limit_bytes=limit)


def attend(x, segments, gain, shift, wq, bq, wk, wv, bv, wo, first_row, count, made):
    rows, length = segments.shape
    tokens, width = x.shape
    cols = wq.shape[1]
    heads = cols // HD
    at = lambda w: pl.BlockSpec((length, w), lambda i: (i + first_row, 0))
    shape = lambda w, kind: jax.ShapeDtypeStruct((tokens, w), kind)
    fixed = (segments, gain, shift, wq, bq, wk, wv, bv, wo)
    done = tokens * count // rows
    return pl.pallas_call(
        lambda *refs: attend_kernel(*refs, first_row=first_row),
        grid=(count,),
        in_specs=[whole(w) for w in fixed]
        + [at(width)]
        + [pl.BlockSpec(memory_space=pl.ANY)] * len(made),
        out_specs=[
            at(width),
            at(3 * cols),
            pl.BlockSpec((1, heads, length, length), lambda i: (i + first_row, 0, 0, 0)),
            at(cols),
            rows_of(length, width),
        ],
        out_shape=[
            shape(width, BF16),
            shape(3 * cols, BF16),
            jax.ShapeDtypeStruct((rows, heads, length, length), BF16),
            shape(cols, BF16),
            jax.ShapeDtypeStruct((count * length, width), F32),
        ],
        input_output_aliases={len(fixed) + 1 + i: i for i in range(len(made))},
        cost_estimate=cost(
            8 * done * width * cols + 4 * done * length * cols,
            done * (10 * width + 8 * cols + 2 * heads * length) + 8 * width * cols,
            done * heads * length,
        ),
        compiler_params=params(63 << 20),
    )(*fixed, x, *made)


def upper_kernel(
    x_ref, mine, other, bias, gain, shift, w_up, b_up, *refs, step
):
    middle_ref, normed_ref, act_ref, slope_ref = refs[-4:]
    bias_up = line(b_up)
    middle = x_ref[...] + (mine[...] + other[...]) + line(bias)
    middle_ref[...] = middle
    unit, _ = unit_rows(middle)
    normed = (unit * line(gain) + line(shift)).astype(BF16)
    normed_ref[...] = normed
    for at in range(0, w_up.shape[1], step):
        part = slice(at, at + step)
        u = product(normed, w_up[:, part], (1, 0)) + bias_up[:, part]
        square = u * u
        bend = jnp.tanh(u * (CURVE + (CURVE * CUBIC) * square))
        half = 0.5 + 0.5 * bend
        act = u * half
        act_ref[:, part] = act.astype(BF16)
        slope = half + act * (1.0 - bend) * (CURVE + (3.0 * CURVE * CUBIC) * square)
        slope_ref[:, part] = slope.astype(BF16)


def upper(x, mine, other, bias, gain, shift, w_up, b_up, length, first_row, made):
    tokens, width = x.shape
    hidden = w_up.shape[1]
    count = mine.shape[0] // length
    at = lambda w: pl.BlockSpec((length, w), lambda i: (i + first_row, 0))
    shape = lambda w, kind: jax.ShapeDtypeStruct((tokens, w), kind)
    fixed = (bias, gain, shift, w_up, b_up)
    return pl.pallas_call(
        lambda *refs: upper_kernel(*refs, step=hidden // 6),
        grid=(count,),
        in_specs=[at(width), rows_of(length, width), rows_of(length, width)]
        + [whole(w) for w in fixed]
        + [pl.BlockSpec(memory_space=pl.ANY)] * len(made),
        out_specs=[at(width), at(width), at(hidden), at(hidden)],
        out_shape=[shape(width, F32), shape(width, BF16), shape(hidden, BF16), shape(hidden, BF16)],
        input_output_aliases={3 + len(fixed) + i: i for i in range(len(made))},
        cost_estimate=cost(
            2 * count * length * width * hidden,
            count * length * (18 * width + 4 * hidden) + 2 * width * hidden,
            count * length * hidden,
        ),
        compiler_params=params(),
    )(x, mine, other, *fixed, *made)


def hidden_kernel(
    top_ref, act_ref, slope_ref, w_down, w_up,
    grad_ref, down_ref, back_ref, bias_ref, *, step,
):
    sums = []
    for at in range(0, w_up.shape[1], step):
        part = slice(at, at + step)
        grad = product(top_ref[...], w_down[part, :], (1, 1)) * slope_ref[:, part].astype(F32)
        grad = grad.astype(BF16)
        grad_ref[:, part] = grad
        sums.append(column_sum(grad.astype(F32)))
    add_up(bias_ref, jnp.concatenate(sums, axis=1))
    back_ref[...] = product(grad_ref[...], w_up[...], (1, 1))
    down_ref[...] = product(act_ref[...], w_down[...], (1, 0))


def hidden_back(top, act, slope, w_down, w_up, length):
    tokens, width = top.shape
    hidden = w_up.shape[1]
    made = lambda w, kind: jax.ShapeDtypeStruct((tokens, w), kind)
    return pl.pallas_call(
        lambda *refs: hidden_kernel(*refs, step=hidden // 6),
        grid=(tokens // length,),
        in_specs=[rows_of(length, width), rows_of(length, hidden), rows_of(length, hidden)]
        + [whole(w) for w in (w_down, w_up)],
        out_specs=[
            rows_of(length, hidden),
            rows_of(length, width),
            rows_of(length, width),
            pl.BlockSpec((1, hidden), lambda i: (0, 0)),
        ],
        out_shape=[
            made(hidden, BF16),
            made(width, F32),
            made(width, F32),
            jax.ShapeDtypeStruct((1, hidden), F32),
        ],
        cost_estimate=cost(
            6 * tokens * width * hidden,
            tokens * (10 * width + 6 * hidden) + 4 * width * hidden,
        ),
        compiler_params=params(),
    )(top, act, slope, w_down, w_up)


def attend_back_kernel(
    top_ref, mine, other, middle_ref, gain, wo, qkv_ref, probs_ref, wq, wk, wv,
    grad_middle_ref, rounded_ref, grad_qkv_ref, back_ref,
    sum_gain, sum_shift, sum_out, sum_qkv,
):
    cols = wq.shape[1]
    unit, inv_std = unit_rows(middle_ref[...])
    grad_normed = mine[...] + other[...]
    add_up(sum_gain, column_sum(grad_normed * unit))
    add_up(sum_shift, column_sum(grad_normed))
    grad_middle = top_ref[...] + norm_back(grad_normed, unit, inv_std, line(gain))
    grad_middle_ref[...] = grad_middle
    add_up(sum_out, column_sum(grad_middle))
    rounded = grad_middle.astype(BF16)
    rounded_ref[...] = rounded
    grad_context = product(rounded, wo[...], (1, 1)).astype(BF16).astype(F32)
    low, high = lane_halves(cols)
    split = ((grad_context * low).astype(BF16), (grad_context * high).astype(BF16))
    first = lax.broadcasted_iota(jnp.int32, (1, PAIR), 1) < HD
    for pair in range(cols // PAIR):
        at = pair * PAIR
        query = qkv_ref[:, at : at + PAIR]
        key = qkv_ref[:, cols + at : cols + at + PAIR]
        value = qkv_ref[:, 2 * cols + at : 2 * cols + at + PAIR]
        to_query, to_key, to_value = [], [], []
        for half in range(2):
            grad_out = split[half][:, at : at + PAIR]
            probs = probs_ref[0, 2 * pair + half]
            wide = probs.astype(F32)
            grad_probs = product(value, grad_out, (1, 1))
            delta = column_sum(wide * grad_probs)
            grad_scores = (wide * (grad_probs - delta)).astype(BF16)
            to_value.append(product(probs, grad_out, (1, 0)))
            to_key.append(product(grad_scores, query, (1, 0)))
            to_query.append(product(grad_scores, key, (0, 0)))
        grad_query = jnp.where(first, to_query[0], to_query[1]) * SCALE
        grad_key = jnp.where(first, to_key[0], to_key[1])
        grad_value = to_value[0] + to_value[1]
        grad_qkv_ref[:, at : at + PAIR] = grad_query.astype(BF16)
        grad_qkv_ref[:, cols + at : cols + at + PAIR] = grad_key.astype(BF16)
        grad_qkv_ref[:, 2 * cols + at : 2 * cols + at + PAIR] = grad_value.astype(BF16)
    grads = grad_qkv_ref[...]
    add_up(sum_qkv, column_sum(grads.astype(F32)))
    back_ref[...] = (
        product(grads[:, :cols], wq[...], (1, 1))
        + product(grads[:, cols : 2 * cols], wk[...], (1, 1))
        + product(grads[:, 2 * cols :], wv[...], (1, 1))
    )


def attend_back(top, mine, other, middle, gain, wo, qkv, probs, wq, wk, wv):
    tokens, width = top.shape
    rows, heads, length, _ = probs.shape
    cols = wq.shape[1]
    made = lambda w, kind: jax.ShapeDtypeStruct((tokens, w), kind)
    line = lambda w: jax.ShapeDtypeStruct((1, w), F32)
    fixed = lambda w: pl.BlockSpec((1, w), lambda i: (0, 0))
    return pl.pallas_call(
        attend_back_kernel,
        grid=(rows,),
        in_specs=[rows_of(length, width)] * 4
        + [whole(gain), whole(wo), rows_of(length, 3 * cols)]
        + [pl.BlockSpec((1, heads, length, length), lambda i: (i, 0, 0, 0))]
        + [whole(w) for w in (wq, wk, wv)],
        out_specs=[
            rows_of(length, width),
            rows_of(length, width),
            rows_of(length, 3 * cols),
            rows_of(length, width),
            fixed(width),
            fixed(width),
            fixed(width),
            fixed(3 * cols),
        ],
        out_shape=[
            made(width, F32),
            made(width, BF16),
            made(3 * cols, BF16),
            made(width, F32),
            line(width),
            line(width),
            line(width),
            line(3 * cols),
        ],
        cost_estimate=cost(
            8 * tokens * width * cols + 8 * tokens * length * cols,
            tokens * (26 * width + 12 * cols + 2 * heads * length) + 8 * width * cols,
        ),
        compiler_params=params(),
    )(top, mine, other, middle, gain, wo, qkv, probs, wq, wk, wv)


def first_back_kernel(
    x_ref, mine, other, above, gain, qkv_sum, out_sum, gain_two, shift_two, up_sum, top_sum,
    out_ref, smalls_ref, sum_gain, sum_shift,
):
    unit, inv_std = unit_rows(x_ref[...])
    grad_normed = mine[...] + other[...]
    add_up(sum_gain, column_sum(grad_normed * unit))
    add_up(sum_shift, column_sum(grad_normed))
    out_ref[...] = above[...] + norm_back(grad_normed, unit, inv_std, line(gain))

    @pl.when(pl.program_id(0) == pl.num_programs(0) - 1)
    def _():
        smalls_ref[...] = jnp.zeros_like(smalls_ref)
        cols = qkv_sum.shape[1] // 3
        to = 0
        for ref, start, size in (
            (sum_gain, 0, sum_gain.shape[1]),
            (sum_shift, 0, sum_shift.shape[1]),
            (qkv_sum, 0, cols),
            (qkv_sum, 2 * cols, cols),
            (out_sum, 0, out_sum.shape[1]),
            (gain_two, 0, gain_two.shape[1]),
            (shift_two, 0, shift_two.shape[1]),
            (up_sum, 0, up_sum.shape[1]),
            (top_sum, 0, top_sum.shape[1]),
        ):
            for r in range(size // 128):
                at = start + 128 * r
                smalls_ref[to + r : to + r + 1, :] = ref[:, at : at + 128]
            to += padded_rows(size)


def padded_rows(size):
    return -(-size // 1024) * 8


def first_back(x, mine, other, above, gain, sums, length):
    tokens, width = x.shape
    cols = sums[0].shape[1] // 3
    sizes = [width, width, cols, cols] + [array.shape[1] for array in sums[1:]]
    shape = (sum(padded_rows(size) for size in sizes), 128)
    grad_x, smalls = pl.pallas_call(
        first_back_kernel,
        grid=(tokens // length,),
        in_specs=[rows_of(length, width)] * 4 + [whole(w) for w in (gain, *sums)],
        out_specs=[rows_of(length, width), pl.BlockSpec(shape, lambda i: (0, 0))],
        out_shape=[
            jax.ShapeDtypeStruct((tokens, width), F32),
            jax.ShapeDtypeStruct(shape, F32),
        ],
        scratch_shapes=[pltpu.VMEM((1, width), F32)] * 2,
        cost_estimate=cost(20 * tokens * width, 20 * tokens * width),
        compiler_params=params(),
    )(x, mine, other, above, gain, *sums)
    return grad_x, smalls, sizes


def from_partner(part):
    return lax.ppermute(part, "mp", [(0, 1), (1, 0)])


def orders_for(kind, bits):
    low, rest = [1 << b for b in range(min(bits, 2))], [1 << b for b in range(2, bits)]
    if kind == "near":
        return [low + rest, low[::-1] + rest]
    return [rest[:1] + low + rest[1:], rest[:1] + low[::-1] + rest[1:]]


def order_of_member(orders, member):
    return orders[member % 2]


def block_table(orders, bits):
    me = lax.axis_index("dp")
    count = 1 << bits
    masks = []
    for order in orders:
        masks.append(
            [
                sum(order[k] for k in range(bits) if r >> (bits - 1 - k) & 1)
                for r in range(count)
            ]
        )
    masks = jnp.asarray(masks, jnp.int32)
    return masks[lax.axis_index("mp") % 2] ^ me.astype(jnp.int32)


def exchange(array, orders, stage):
    dp, mp = lax.axis_size("dp"), lax.axis_size("mp")
    pairs = []
    for d in range(dp):
        for m in range(mp):
            pairs.append((d * mp + m, (d ^ order_of_member(orders, m)[stage]) * mp + m))
    return lax.ppermute(array, ("dp", "mp"), pairs)


def add_kernel(*refs):
    total = refs[0][...]
    for ref in refs[1:-1]:
        total = total + ref[...]
    refs[-1][...] = total


def add_blocks(arrays, first, count):
    shape = (count, *arrays[0].shape[1:])
    step = min(count, 2)
    spec = pl.BlockSpec((step, *shape[1:]), lambda i: (i + first // step, 0, 0))
    size = math.prod(shape)
    return pl.pallas_call(
        add_kernel,
        grid=(count // step,),
        in_specs=[spec] * len(arrays),
        out_specs=pl.BlockSpec((step, *shape[1:]), lambda i: (i, 0, 0)),
        out_shape=jax.ShapeDtypeStruct(shape, F32),
        cost_estimate=cost(size * len(arrays), 4 * size * (1 + len(arrays))),
        compiler_params=params(),
    )(*arrays)


class Scatter:
    def __init__(self, send, keep, orders):
        self.keep, self.orders = keep, orders
        self.got = [exchange(send, orders, 0)]

    def take(self, after):
        self.got[-1] = lax.optimization_barrier((self.got[-1], after))[0]
        return [self.keep, *self.got]

    def step(self, after):
        half = self.keep.shape[0] >> len(self.got)
        send = add_blocks(self.take(after), half, half)
        self.got.append(exchange(send, self.orders, len(self.got)))
        return send

    def result(self, after):
        return add_blocks(self.take(after), 0, 1)[0]


def all_sum(vector, bits):
    order = [1 << b for b in range(bits)]
    for stage in range(bits):
        vector = vector + exchange(vector, [order, order], stage)
    return vector


def grad_kernel(table, left_ref, right_ref, *refs):
    outs, acc = refs[:-1], refs[-1]
    acc[...] = lax.dot_general(
        left_ref[...],
        right_ref[...],
        (((0,), (0,)), ((), ())),
        preferred_element_type=jnp.float32,
    )
    send, keep = outs
    half, size = keep.shape[0], keep.shape[1]
    for r in range(half):
        at = pl.multiple_of(table[r] * size, 8)
        keep[r] = acc[pl.ds(at, size), :]
        at = pl.multiple_of(table[half + r] * size, 8)
        send[r] = acc[pl.ds(at, size), :]


def blocked_grad(table, left, right, start, columns, tile):
    tokens, width = left.shape
    count = table.shape[0]
    size = width // count
    shape = jax.ShapeDtypeStruct((count // 2, size, columns), jnp.float32)
    block = pl.BlockSpec((count // 2, size, tile), lambda i, t: (0, 0, i))
    first = start // tile
    return pl.pallas_call(
        grad_kernel,
        grid_spec=pltpu.PrefetchScalarGridSpec(
            num_scalar_prefetch=1,
            grid=(columns // tile,),
            in_specs=[
                pl.BlockSpec((tokens, width), lambda i, t: (0, 0)),
                pl.BlockSpec((tokens, tile), lambda i, t: (0, i + first)),
            ],
            out_specs=[block, block],
            scratch_shapes=[pltpu.VMEM((width, tile), jnp.float32)],
        ),
        out_shape=[shape, shape],
        cost_estimate=cost(
            2 * tokens * width * columns, 2 * tokens * (width + columns) + 4 * width * columns
        ),
        compiler_params=params(),
    )(table, left, right)


def pieces_kernel(table, *refs, pieces, sources):
    lefts, rights = refs[:sources], refs[sources : 2 * sources]
    send, keep, acc = refs[2 * sources :]
    half, size = keep.shape[0], keep.shape[1]
    to = 0
    for source, start, columns in pieces:
        acc[:, :columns] = product(
            lefts[source][...], rights[source][:, start : start + columns], (0, 0)
        )
        for r in range(half):
            at = pl.multiple_of(table[r] * size, 8)
            keep[r, :, to : to + columns] = acc[pl.ds(at, size), :columns]
            at = pl.multiple_of(table[half + r] * size, 8)
            send[r, :, to : to + columns] = acc[pl.ds(at, size), :columns]
        to += columns


def blocked_pieces(table, lefts, rights, pieces):
    tokens, width = lefts[0].shape
    count = table.shape[0]
    columns = sum(piece[2] for piece in pieces)
    shape = jax.ShapeDtypeStruct((count // 2, width // count, columns), F32)
    spec = lambda array: pl.BlockSpec(array.shape, lambda i, t: (0, 0), pipeline_mode=pl.Buffered(1))
    block = pl.BlockSpec(shape.shape, lambda i, t: (0, 0, 0))
    return pl.pallas_call(
        lambda *refs: pieces_kernel(*refs, pieces=pieces, sources=len(lefts)),
        grid_spec=pltpu.PrefetchScalarGridSpec(
            num_scalar_prefetch=1,
            grid=(1,),
            in_specs=[spec(array) for array in (*lefts, *rights)],
            out_specs=[block, block],
            scratch_shapes=[pltpu.VMEM((width, max(p[2] for p in pieces)), F32)],
        ),
        out_shape=[shape, shape],
        cost_estimate=cost(
            2 * tokens * width * columns, 2 * tokens * (width + columns) + 4 * width * columns
        ),
        compiler_params=params(),
    )(table, *lefts, *rights)


def butterfly_bits(width):
    dp = lax.axis_size("dp")
    bits = dp.bit_length() - 1
    return bits if (1 << bits) == dp and bits >= 3 and width // dp % 8 == 0 else 0


def sum_small(rows, sizes):
    dp = lax.axis_size("dp")
    bits = dp.bit_length() - 1
    rows = all_sum(rows, bits) if (1 << bits) == dp else lax.psum(rows, "dp")
    out, at = [], 0
    for size in sizes:
        out.append(rows[at : at + size // 128].reshape(size))
        at += padded_rows(size)
    return out


def on_device(
    inputs,
    segment_ids,
    ln1_gain,
    ln1_bias,
    w_query,
    b_query,
    w_key,
    w_value,
    b_value,
    w_output,
    b_output,
    ln2_gain,
    ln2_bias,
    w_up,
    b_up,
    w_down,
    b_down,
    cotangent,
):
    rows, length, width = inputs.shape
    cols = w_query.shape[1]
    tokens = rows * length
    hidden = w_up.shape[1]
    far = hidden // 3
    near = hidden - far
    row = lambda vector: vector.reshape(-1, 128)
    pin = lambda values, after: lax.optimization_barrier((values, after))[0]
    x = inputs.reshape(tokens, width)
    top = cotangent.reshape(tokens, width)
    bits = butterfly_bits(width)

    half = rows // 2
    ln1 = (row(ln1_gain), row(ln1_bias))
    firsts = (*ln1, w_query, row(b_query), w_key, w_value, row(b_value), w_output)
    *made, out_low = attend(x, segment_ids, *firsts, 0, half, ())
    low_other = from_partner(out_low)
    *made, out_high = attend(x, segment_ids, *firsts, half, rows - half, made)
    high_other = from_partner(out_high)
    normed, qkv, probs, context = made
    seconds = (row(b_output), row(ln2_gain), row(ln2_bias), w_up, row(b_up), length)
    made = upper(x, pin(out_low, out_high), low_other, *seconds, 0, ())
    top_pinned = pin(top, made[1])
    top_b, sum_top = top_pinned.astype(BF16), jnp.sum(top_pinned, axis=0, keepdims=True)
    made = upper(x, pin(out_high, top_b), high_other, *seconds, half, made)
    middle, normed_two, act, slope = made

    if bits:
        near_orders, far_orders = orders_for("near", bits), orders_for("far", bits)
        near_table, far_table = block_table(near_orders, bits), block_table(far_orders, bits)
        down_far = blocked_grad(far_table, top_b, act, near, far, far)
        after = down_far[0]
        down_far = Scatter(*down_far, far_orders)
        down_near = blocked_grad(near_table, pin(top_b, after), act, 0, near, far)
        after = down_near[0]
        down_near = Scatter(*down_near, near_orders)
    else:
        after = middle
    grad_upper, down_mine, back_mine, sum_up = hidden_back(
        pin(top_b, after), act, slope, w_down, w_up, length
    )
    back_other = from_partner(back_mine)
    down_other = from_partner(down_mine)
    after = sum_up
    if bits:
        after = down_far.step(after)
        after = down_near.step(after)
        up_far = blocked_grad(far_table, normed_two, pin(grad_upper, after), near, far, far)
        after = up_far[0]
        up_far = Scatter(*up_far, far_orders)
        up_near = blocked_grad(near_table, normed_two, pin(grad_upper, after), 0, near, far)
        after = up_near[0]
        up_near = Scatter(*up_near, near_orders)
    (
        grad_middle, grad_middle_b, grad_qkv, first_mine,
        sum_gain_two, sum_shift_two, sum_out, sum_qkv,
    ) = attend_back(
        top, pin(back_mine, after), back_other, middle, row(ln2_gain), w_output, qkv, probs,
        w_query, w_key, w_value,
    )
    first_other = from_partner(first_mine)
    after = sum_qkv
    if bits:
        lefts, rights = (normed, grad_middle_b), (grad_qkv, context)
        split = cols // 3 * 2
        pieces = ((0, cols, cols), (0, 2 * cols, cols), (1, 0, split))
        last_near = blocked_pieces(near_table, lefts, rights, pieces)
        after = last_near[0]
        last_near = Scatter(*last_near, near_orders)
        pieces = ((0, 0, cols), (1, split, cols - split))
        last_far = blocked_pieces(far_table, lefts, pin(rights, after), pieces)
        after = last_far[0]
        last_far = Scatter(*last_far, far_orders)
        after = up_far.step(after)
        after = up_near.step(after)
        after = down_far.step(after)
        after = down_near.step(after)
    grad_x, smalls, sizes = first_back(
        x, pin(first_mine, after), first_other, grad_middle, row(ln1_gain),
        (sum_qkv, sum_out, sum_gain_two, sum_shift_two, sum_up, sum_top), length,
    )
    after = smalls
    smalls = sum_small(smalls, sizes)
    if bits:
        after = last_near.step(after)
        after = last_far.step(after)
        after = up_far.step(after)
        after = up_near.step(after)
        after = down_far.step(after)
        after = down_near.step(after)
    outcome = pin(middle, after) + (down_mine + down_other) + b_down
    after = outcome
    if bits:
        after = last_near.step(after)
        after = last_far.step(after)
        after = up_far.step(after)
        after = up_near.step(after)
        out_down = jnp.concatenate([down_near.result(after), down_far.result(after)], axis=1).T
        after = out_down
        after = last_near.step(after)
        after = last_far.step(after)
        out_up = jnp.concatenate([up_near.result(after), up_far.result(after)], axis=1)
        after = out_up
        last_near, last_far = last_near.result(after), last_far.result(after)
        out_query, out_key, out_value = (
            last_far[:, :cols],
            last_near[:, :cols],
            last_near[:, cols : 2 * cols],
        )
        out_output = jnp.concatenate([last_near[:, 2 * cols :], last_far[:, cols:]], axis=1).T
    else:
        scatter = lambda left, right: lax.psum_scatter(
            left_product(left, right), "dp", scatter_dimension=0, tiled=True
        )
        out_down, out_up = scatter(top_b, act).T, scatter(normed_two, grad_upper)
        out_query, out_key, out_value = (
            scatter(normed, grad_qkv[:, at : at + cols]) for at in (0, cols, 2 * cols)
        )
        out_output = scatter(grad_middle_b, context).T
    shape = inputs.shape
    return (
        outcome.reshape(shape),
        grad_x.reshape(shape),
        smalls[0],
        smalls[1],
        out_query,
        smalls[2],
        out_key,
        out_value,
        smalls[3],
        out_output,
        smalls[4],
        smalls[5],
        smalls[6],
        out_up,
        smalls[7],
        out_down,
        smalls[8],
    )


def solution(mesh):
    return jax.shard_map(
        on_device,
        mesh=mesh,
        in_specs=(
            P("dp", None, None),
            P("dp", None),
            P(),
            P(),
            P(None, "mp"),
            P("mp"),
            P(None, "mp"),
            P(None, "mp"),
            P("mp"),
            P("mp", None),
            P(),
            P(),
            P(),
            P(None, "mp"),
            P("mp"),
            P("mp", None),
            P(),
            P("dp", None, None),
        ),
        out_specs=(
            P("dp", None, None),
            P("dp", None, None),
            P(),
            P(),
            P("dp", "mp"),
            P("mp"),
            P("dp", "mp"),
            P("dp", "mp"),
            P("mp"),
            P("mp", "dp"),
            P(),
            P(),
            P(),
            P("dp", "mp"),
            P("mp"),
            P("mp", "dp"),
            P(),
        ),
        check_vma=False,
    )
```

```python
import math

import jax
import jax.numpy as jnp
from jax import lax
from jax.experimental import pallas as pl
from jax.experimental.pallas import tpu as pltpu
from jax.sharding import PartitionSpec as P

HD = 64
PAIR = 2 * HD
EPSILON = 1e-06
MASKED = -1000000000.0
SCALE = 1.0 / math.sqrt(HD)
CURVE = math.sqrt(2.0 / math.pi)
CUBIC = 0.044715
COSTS = {"attend": 0.01, "forward": 0.01, "back": 0.01, "first": 0.01, "add": 0.01}
BIG = 63 << 20
STEP = 512
SLAB = 64
F32 = jnp.float32
BF16 = jnp.bfloat16


def product(left, right, over):
    return lax.dot_general(
        left, right, ((over[:1], over[1:]), ((), ())), preferred_element_type=F32
    )


def left_product(left, right):
    return product(left, right, (0, 0))


def unit_rows(values):
    centered = values - jnp.mean(values, axis=-1, keepdims=True)
    inv_std = lax.rsqrt(jnp.mean(centered * centered, axis=-1, keepdims=True) + EPSILON)
    return centered * inv_std, inv_std


def norm_back(grad_out, unit, inv_std, gain):
    grad_unit = grad_out * gain
    return inv_std * (
        grad_unit
        - jnp.mean(grad_unit, axis=-1, keepdims=True)
        - unit * jnp.mean(grad_unit * unit, axis=-1, keepdims=True)
    )


def column_sum(values):
    return jnp.sum(values, axis=0, keepdims=True)


def line(ref):
    return jnp.concatenate([ref[r : r + 1, :] for r in range(ref.shape[0])], axis=1)


def add_up(ref, value):
    @pl.when(pl.program_id(0) == 0)
    def _():
        ref[...] = jnp.zeros_like(ref)

    ref[...] += value


def in_rows(far, near, sems, first, chunks):
    size = far.shape[0] // chunks
    rows = [pl.ds(c * size, size) for c in range(chunks)]
    return [
        pltpu.make_async_copy(far.at[part], near.at[part], sems.at[first + c])
        for c, part in enumerate(rows)
    ]


def started(copies):
    return lambda: [copy.start() for copy in copies] and None


def arrived(copies):
    return lambda: [copy.wait() for copy in copies] and None


def when_first(action):
    pl.when(pl.program_id(0) == 0)(action)


def either(low, high, rows_low, slab):
    return jnp.where(pl.program_id(0) < rows_low, low[slab, :], high[slab, :])


def last_step():
    return pl.program_id(0) == pl.num_programs(0) - 1


def leaving(tables, outs, pieces, widths, total, sems, make):
    copies, start = [], 0
    for turned, right, at, columns, index, to in pieces:
        if make:
            total[:, start : start + columns] = product(
                turned[...], right[:, at : at + columns], (1, 0)
            )
        fresh = []
        if tables:
            table, send, keep = tables[index], outs[2 * index], outs[2 * index + 1]
            half, size, _ = send.shape
            for r in range(2 * half):
                row = pl.multiple_of(table[r] * size, 8)
                far = send.at[r - half] if r >= half else keep.at[r]
                fresh.append(
                    pltpu.make_async_copy(
                        total.at[pl.ds(row, size), pl.ds(start, columns)],
                        far.at[:, pl.ds(to, columns)],
                        sems.at[len(copies) + r],
                    )
                )
        else:
            fresh.append(
                pltpu.make_async_copy(
                    total.at[:, pl.ds(start, columns)],
                    outs[0].at[:, pl.ds(sum(widths[:index]) + to, columns)],
                    sems.at[len(copies)],
                )
            )
        if make:
            started(fresh)()
        copies += fresh
        start += columns
    return copies


def leave(*args):
    arrived(leaving(*args, True))()


def pieces_of(sources, first, widths):
    pieces = []
    for turned, right, at, columns in sources:
        end = at + columns
        while at < end:
            index, to, left = place_of(first, widths)
            size = min(512, end - at, left)
            pieces.append((turned, right, at, size, index, to))
            at, first = at + size, first + size
    return pieces


def place_of(column, widths):
    for index, width in enumerate(widths):
        if column < width:
            return index, column, width - column
        column -= width


def step_rows(length):
    return pl.ds(pl.multiple_of(pl.program_id(0) * length, length), length)


def gradient_outs(tables, widths, width):
    if not tables:
        return [jax.ShapeDtypeStruct((width, sum(widths)), F32)], 8
    blocks = tables[0].shape[0]
    shapes = [
        jax.ShapeDtypeStruct((blocks // 2, width // blocks, columns), F32)
        for columns in widths
        for _ in range(2)
    ]
    return shapes, blocks * 6


def table_spec():
    return pl.BlockSpec(memory_space=pltpu.SMEM)


def in_turn(stages, count):
    for turn in range(count + len(stages) - 1):
        for late, stage in enumerate(stages):
            if 0 <= turn - late < count:
                stage(turn - late)


def lane_halves(width):
    lane = lax.broadcasted_iota(jnp.int32, (1, width), 1)
    low = (lane % PAIR < HD).astype(F32)
    return low, 1.0 - low


def attend_kernel(
    seg_ref, gain, shift, bq, bv, bo, wq_far, wk_far, wv_far, wo_far, x_ref, *refs, first_row
):
    normed_ref, qkv_ref, probs_ref, context_ref, out_ref = refs[-10:-5]
    wq, wk, wv, wo, sems = refs[-5:]
    fetches = []
    for i, (far, near) in enumerate(((wq_far, wq), (wk_far, wk), (wv_far, wv), (wo_far, wo))):
        fetches += in_rows(far, near, sems, 2 * i, 2)
    when_first(started(fetches))

    cols = wq.shape[1]
    gain_row, shift_row = line(gain), line(shift)
    for at in range(0, x_ref.shape[0], SLAB):
        slab = slice(at, at + SLAB)
        unit, _ = unit_rows(x_ref[slab, :])
        normed_ref[slab, :] = (unit * gain_row + shift_row).astype(BF16)
    normed = normed_ref[...]
    low, high = lane_halves(cols)
    when_first(arrived(fetches))
    queries = (product(normed, wq[...], (1, 0)) + line(bq)) * SCALE
    keys = product(normed, wk[...], (1, 0)).astype(BF16)
    values = (product(normed, wv[...], (1, 0)) + line(bv)).astype(BF16)
    qkv_ref[:, :cols] = queries.astype(BF16)
    qkv_ref[:, cols : 2 * cols] = keys
    qkv_ref[:, 2 * cols :] = values
    split = ((queries * low).astype(BF16), (queries * high).astype(BF16))
    seg_row = seg_ref[pl.ds(pl.program_id(0) + first_row, 1), :].astype(F32)
    length = seg_row.shape[1]
    seg_col = jnp.broadcast_to(seg_row, (128, length)).T
    same = jnp.concatenate([seg_col] * (length // 128), axis=1) == seg_row
    first = lax.broadcasted_iota(jnp.int32, (1, PAIR), 1) < HD
    scores, probs, made = {}, {}, {}

    def score(head):
        part = slice(head // 2 * PAIR, head // 2 * PAIR + PAIR)
        scores[head] = product(keys[:, part], split[head % 2][:, part], (1, 1))

    def soften(head):
        masked = jnp.where(same, scores.pop(head), MASKED)
        expo = jnp.exp(masked - jnp.max(masked, axis=0, keepdims=True))
        probs[head] = (expo * (1.0 / column_sum(expo))).astype(BF16)
        probs_ref[0, head] = probs[head]

    def gather(head):
        part = slice(head // 2 * PAIR, head // 2 * PAIR + PAIR)
        made[head] = product(probs.pop(head), values[:, part], (0, 0))
        if head % 2:
            context_ref[:, part] = jnp.where(first, made.pop(head - 1), made.pop(head)).astype(BF16)

    in_turn((score, soften, gather), cols // HD)
    out_ref[...] = product(context_ref[...], wo[...], (1, 0)) + 0.5 * (x_ref[...] + line(bo))


def whole(array):
    zeros = (0,) * array.ndim
    return pl.BlockSpec(array.shape, lambda i: zeros, pipeline_mode=pl.Buffered(1))


def rows_of(length, width):
    return pl.BlockSpec((length, width), lambda i: (i, 0))


def cost(name, flops, moved):
    weight = COSTS[name]
    return pl.CostEstimate(
        flops=int(weight * flops), bytes_accessed=int(weight * moved), transcendentals=0
    )


def params(limit=26 << 20):
    return pltpu.CompilerParams(vmem_limit_bytes=limit)


def attend(x, segments, gain, shift, wq, bq, wk, wv, bv, wo, bo, first_row, count, made):
    rows, length = segments.shape
    tokens, width = x.shape
    cols = wq.shape[1]
    heads = cols // HD
    at = lambda w: pl.BlockSpec((length, w), lambda i: (i + first_row, 0))
    shape = lambda w, kind: jax.ShapeDtypeStruct((tokens, w), kind)
    fixed = (segments, gain, shift, bq, bv, bo)
    weights = (wq, wk, wv, wo)
    done = tokens * count // rows
    return pl.pallas_call(
        lambda *refs: attend_kernel(*refs, first_row=first_row),
        grid=(count,),
        in_specs=[whole(w) for w in fixed]
        + [pl.BlockSpec(memory_space=pl.ANY)] * len(weights)
        + [at(width)]
        + [pl.BlockSpec(memory_space=pl.ANY)] * len(made),
        out_specs=[
            at(width),
            at(3 * cols),
            pl.BlockSpec((1, heads, length, length), lambda i: (i + first_row, 0, 0, 0)),
            at(cols),
            rows_of(length, width),
        ],
        out_shape=[
            shape(width, BF16),
            shape(3 * cols, BF16),
            jax.ShapeDtypeStruct((rows, heads, length, length), BF16),
            shape(cols, BF16),
            jax.ShapeDtypeStruct((count * length, width), F32),
        ],
        input_output_aliases={len(fixed) + len(weights) + 1 + i: i for i in range(len(made))},
        scratch_shapes=[pltpu.VMEM(w.shape, w.dtype) for w in weights]
        + [pltpu.SemaphoreType.DMA((2 * len(weights),))],
        name="attend",
        cost_estimate=cost("attend",
            8 * done * width * cols + 4 * done * length * cols,
            done * (10 * width + 8 * cols + 2 * heads * length) + 8 * width * cols,
        ),
        compiler_params=params(BIG),
    )(*fixed, *weights, x, *made)


def forward_kernel(*refs, count, rows, rows_low, widths):
    tables, refs = refs[:count], refs[count:]
    mine_low, mine_high, other_low, other_high, top_ref, gain, shift, b_up, w_up, w_down = refs[:10]
    middle_ref, down_ref, back_ref, by_top, by_up = refs[10:15]
    outs, refs = refs[15:-14], refs[-14:]
    up_near, down_near, tops, turned_top, turned, acts, slopes, down_total, up_total = refs[:9]
    normed, up_sems, down_sems, down_outs, up_outs = refs[9:]
    step, length = pl.program_id(0), top_ref.shape[0]
    here = pl.ds(pl.multiple_of(step % rows * length, length), length)
    ups, downs = in_rows(w_up, up_near, up_sems, 0, 4), in_rows(w_down, down_near, down_sems, 0, 4)
    hidden = up_near.shape[1]
    of_down = pieces_of([(turned_top, acts, 0, hidden)], 0, widths)
    of_up = pieces_of([(turned, slopes, 0, hidden)], hidden, widths)
    down_args = (tables, outs, of_down, widths, down_total, down_outs)
    up_args = (tables, outs, of_up, widths, up_total, up_outs)
    when_first(started(ups + downs))

    @pl.when(step < rows)
    def _():
        bias_up, gain_row, shift_row, top_sum = line(b_up), line(gain), line(shift), 0.0
        for at in range(0, length, SLAB):
            slab = slice(at, at + SLAB)
            middle = either(mine_low, mine_high, rows_low, slab) + either(
                other_low, other_high, rows_low, slab
            )
            middle_ref[slab, :] = middle
            unit, _ = unit_rows(middle)
            normed[slab, :] = (unit * gain_row + shift_row).astype(BF16)
            top_sum += column_sum(top_ref[slab, :])
        add_up(by_top, top_sum)
        tops[here, :] = top_ref[...].astype(BF16)
        turned_top[:, here] = tops[here, :].T
        turned[:, here] = normed[...].T
        when_first(arrived(ups))
        for at in range(0, hidden, STEP):
            units = slice(at, at + STEP)
            u = product(normed[...], up_near[:, units], (1, 0)) + bias_up[:, units]
            square = u * u
            bend = jnp.tanh(u * (CURVE + (CURVE * CUBIC) * square))
            above = 0.5 + 0.5 * bend
            act = u * above
            acts[here, units] = act.astype(BF16)
            slope = above + act * (1.0 - bend) * (CURVE + (3.0 * CURVE * CUBIC) * square)
            slopes[here, units] = slope.astype(BF16)

    @pl.when(step == rows - 1)
    def _():
        leaving(*down_args, True)

    @pl.when(step == rows)
    def _():
        arrived(downs)()
        by_up[...] = jnp.zeros_like(by_up)

    @pl.when(step >= rows)
    def _():
        for at in range(0, hidden, STEP):
            units = slice(at, at + STEP)
            grad = product(tops[here, :], down_near[units, :], (1, 1))
            grad = (grad * slopes[here, units].astype(F32)).astype(BF16)
            slopes[here, units] = grad
            by_up[:, units] += column_sum(grad.astype(F32))
        back_ref[...] = product(slopes[here, :], up_near[...], (1, 1))
        down_ref[...] = product(acts[here, :], down_near[...], (1, 0))

    @pl.when(step == 2 * rows - 1)
    def _():
        leave(*up_args)
        arrived(leaving(*down_args, False))()


def forward(mines, others, top, gain, shift, w_up, b_up, w_down, length, tables, widths):
    tokens, width = top.shape
    hidden = w_up.shape[1]
    rows, low = tokens // length, mines[0].shape[0] // length
    first = lambda i: jnp.minimum(i, rows - 1)
    low_spec = pl.BlockSpec((length, width), lambda i: (jnp.minimum(i, low - 1), 0))
    high_spec = pl.BlockSpec((length, width), lambda i: (jnp.clip(i - low, 0, rows - low - 1), 0))
    up_spec = pl.BlockSpec((length, width), lambda i: (first(i), 0))
    back_spec = pl.BlockSpec((length, width), lambda i: (jnp.maximum(i - rows, 0), 0))
    sum_spec = lambda w: pl.BlockSpec((1, w), lambda i: (0, 0))
    shape = lambda *dims: jax.ShapeDtypeStruct(dims, F32)
    anywhere = pl.BlockSpec(memory_space=pl.ANY)
    outs, copies = gradient_outs(tables, widths, width)
    fixed = (gain, shift, b_up)
    made = pl.pallas_call(
        lambda *refs: forward_kernel(
            *refs, count=len(tables), rows=rows, rows_low=low, widths=widths
        ),
        grid=(2 * rows,),
        in_specs=[table_spec()] * len(tables)
        + [low_spec, high_spec] * 2
        + [up_spec]
        + [whole(w) for w in fixed]
        + [anywhere] * 2,
        out_specs=[up_spec, back_spec, back_spec, sum_spec(width), sum_spec(hidden)]
        + [anywhere] * len(outs),
        out_shape=[shape(tokens, width)] * 3 + [shape(1, width), shape(1, hidden)] + outs,
        scratch_shapes=[
            pltpu.VMEM(w_up.shape, BF16),
            pltpu.VMEM(w_down.shape, BF16),
            pltpu.VMEM((tokens, width), BF16),
            pltpu.VMEM((width, tokens), BF16),
            pltpu.VMEM((width, tokens), BF16),
            pltpu.VMEM((tokens, hidden), BF16),
            pltpu.VMEM((tokens, hidden), BF16),
            pltpu.VMEM((width, hidden), F32),
            pltpu.VMEM((width, hidden), F32),
            pltpu.VMEM((length, width), BF16),
            pltpu.SemaphoreType.DMA((4,)),
            pltpu.SemaphoreType.DMA((4,)),
            pltpu.SemaphoreType.DMA((copies,)),
            pltpu.SemaphoreType.DMA((copies,)),
        ],
        name="forward",
        cost_estimate=cost(
            "forward",
            12 * tokens * width * hidden,
            tokens * 24 * width + 12 * width * hidden,
        ),
        compiler_params=params(BIG),
    )(*tables, *mines, *others, top, *fixed, w_up, w_down)
    return made[:5], made[5:]


def attend_back_kernel(*refs, count, widths):
    tables, refs = refs[:count], refs[count:]
    mine, other, refs = refs[0], refs[1], refs[2:]
    top_ref, middle_ref, gain, qkv_ref, probs_ref, normed_ref, context_ref = refs[:7]
    wo_far, wq_far, wk_far, wv_far = refs[7:11]
    grad_middle_ref, back_ref, sum_gain, sum_shift, sum_out, sum_qkv = refs[11:17]
    outs, refs = refs[17:-12], refs[-12:]
    rounded, grad_qkv_ref, contexts, turned, turned_two, total, wo, wq, wk, wv = refs[:10]
    sems, out_sems = refs[10:]
    cols, length = wq.shape[1], top_ref.shape[0]
    here = step_rows(length)
    fetches = []
    for i, (far, near) in enumerate(((wo_far, wo), (wq_far, wq), (wk_far, wk), (wv_far, wv))):
        fetches += in_rows(far, near, sems, 2 * i, 2)
    when_first(started(fetches))
    gain_row, by_gain, by_shift, by_out = line(gain), 0.0, 0.0, 0.0
    for at in range(0, length, SLAB):
        slab = slice(at, at + SLAB)
        unit, inv_std = unit_rows(middle_ref[slab, :])
        grad_normed = mine[slab, :] + other[slab, :]
        by_gain += column_sum(grad_normed * unit)
        by_shift += column_sum(grad_normed)
        grad_middle = top_ref[slab, :] + norm_back(grad_normed, unit, inv_std, gain_row)
        grad_middle_ref[slab, :] = grad_middle
        by_out += column_sum(grad_middle)
        rounded[slab, :] = grad_middle.astype(BF16)
    add_up(sum_gain, by_gain)
    add_up(sum_shift, by_shift)
    add_up(sum_out, by_out)
    turned[:, here] = normed_ref[...].T
    turned_two[:, here] = rounded[...].T
    contexts[here, :] = context_ref[...]
    when_first(arrived(fetches))
    grad_context = product(rounded[...], wo[...], (1, 1)).astype(BF16).astype(F32)
    low, high = lane_halves(cols)
    split = ((grad_context * low).astype(BF16), (grad_context * high).astype(BF16))
    first = lax.broadcasted_iota(jnp.int32, (1, PAIR), 1) < HD
    grad_probs, grad_scores, made = {}, {}, {}

    def at(head, which):
        start = which * cols + head // 2 * PAIR
        return slice(start, start + PAIR)

    def spread(head):
        grad_probs[head] = product(
            qkv_ref[:, at(head, 2)], split[head % 2][:, at(head, 0)], (1, 1)
        )

    def soften(head):
        wide = probs_ref[0, head].astype(F32)
        moved = wide * grad_probs.pop(head)
        grad_scores[head] = (moved - wide * column_sum(moved)).astype(BF16)

    def gather(head):
        grads = grad_scores.pop(head)
        made[head] = (
            product(grads, qkv_ref[:, at(head, 1)], (0, 0)),
            product(grads, qkv_ref[:, at(head, 0)], (1, 0)),
            product(probs_ref[0, head], split[head % 2][:, at(head, 0)], (1, 0)),
        )
        if head % 2:
            even, odd = made.pop(head - 1), made.pop(head)
            grad_query = jnp.where(first, even[0], odd[0]) * SCALE
            grad_qkv_ref[here, at(head, 0)] = grad_query.astype(BF16)
            grad_qkv_ref[here, at(head, 1)] = jnp.where(first, even[1], odd[1]).astype(BF16)
            grad_qkv_ref[here, at(head, 2)] = (even[2] + odd[2]).astype(BF16)

    in_turn((spread, soften, gather), cols // HD)
    grads = grad_qkv_ref[here, :]
    add_up(sum_qkv, column_sum(grads.astype(F32)))
    back_ref[...] = (
        product(grads[:, :cols], wq[...], (1, 1))
        + product(grads[:, cols : 2 * cols], wk[...], (1, 1))
        + product(grads[:, 2 * cols :], wv[...], (1, 1))
    )
    pieces = pieces_of(
        [(turned, grad_qkv_ref, 0, 3 * cols), (turned_two, contexts, 0, cols)], 0, widths
    )
    pl.when(last_step())(lambda: leave(tables, outs, pieces, widths, total, out_sems))


def attend_back(
    top, mine, other, middle, gain, wo, qkv, probs, normed, context, wq, wk, wv, tables, widths
):
    tokens, width = top.shape
    rows, heads, length, _ = probs.shape
    cols = wq.shape[1]
    line = lambda w: jax.ShapeDtypeStruct((1, w), F32)
    fixed = lambda w: pl.BlockSpec((1, w), lambda i: (0, 0))
    weights = (wo, wq, wk, wv)
    outs, copies = gradient_outs(tables, widths, width)
    anywhere = pl.BlockSpec(memory_space=pl.ANY)
    made = pl.pallas_call(
        lambda *refs: attend_back_kernel(*refs, count=len(tables), widths=widths),
        grid=(rows,),
        in_specs=[table_spec()] * len(tables)
        + [rows_of(length, width)] * 4
        + [whole(gain), rows_of(length, 3 * cols)]
        + [pl.BlockSpec((1, heads, length, length), lambda i: (i, 0, 0, 0))]
        + [rows_of(length, width), rows_of(length, cols)]
        + [anywhere] * len(weights),
        out_specs=[rows_of(length, width)] * 2
        + [fixed(width), fixed(width), fixed(width), fixed(3 * cols)]
        + [anywhere] * len(outs),
        out_shape=[jax.ShapeDtypeStruct((tokens, width), F32)] * 2
        + [line(width), line(width), line(width), line(3 * cols)]
        + outs,
        scratch_shapes=[
            pltpu.VMEM((length, width), BF16),
            pltpu.VMEM((tokens, 3 * cols), BF16),
            pltpu.VMEM((tokens, cols), BF16),
            pltpu.VMEM((width, tokens), BF16),
            pltpu.VMEM((width, tokens), BF16),
            pltpu.VMEM((width, 4 * cols), F32),
        ]
        + [pltpu.VMEM(w.shape, w.dtype) for w in weights]
        + [
            pltpu.SemaphoreType.DMA((2 * len(weights),)),
            pltpu.SemaphoreType.DMA((copies,)),
        ],
        name="back",
        cost_estimate=cost(
            "back",
            16 * tokens * width * cols + 8 * tokens * length * cols,
            tokens * (26 * width + 8 * cols + 2 * heads * length) + 24 * width * cols,
        ),
        compiler_params=params(BIG),
    )(*tables, mine, other, top, middle, gain, qkv, probs, normed, context, *weights)
    return made[:6], made[6:]


def first_back_kernel(*refs):
    mine, other, refs = refs[0], refs[1], refs[2:]
    x_ref, above, gain, qkv_sum, out_sum, gain_two, shift_two, up_sum, top_sum = refs[:9]
    out_ref, smalls_ref, sum_gain, sum_shift = refs[9:]
    gain_row, by_gain, by_shift = line(gain), 0.0, 0.0
    for at in range(0, x_ref.shape[0], SLAB):
        slab = slice(at, at + SLAB)
        unit, inv_std = unit_rows(x_ref[slab, :])
        grad_normed = mine[slab, :] + other[slab, :]
        by_gain += column_sum(grad_normed * unit)
        by_shift += column_sum(grad_normed)
        out_ref[slab, :] = above[slab, :] + norm_back(grad_normed, unit, inv_std, gain_row)
    add_up(sum_gain, by_gain)
    add_up(sum_shift, by_shift)

    @pl.when(pl.program_id(0) == pl.num_programs(0) - 1)
    def _():
        smalls_ref[...] = jnp.zeros_like(smalls_ref)
        cols = qkv_sum.shape[1] // 3
        to = 0
        for ref, start, size in (
            (sum_gain, 0, sum_gain.shape[1]),
            (sum_shift, 0, sum_shift.shape[1]),
            (qkv_sum, 0, cols),
            (qkv_sum, 2 * cols, cols),
            (out_sum, 0, out_sum.shape[1]),
            (gain_two, 0, gain_two.shape[1]),
            (shift_two, 0, shift_two.shape[1]),
            (up_sum, 0, up_sum.shape[1]),
            (top_sum, 0, top_sum.shape[1]),
        ):
            wide = smalls_ref.shape[2]
            for at in range(0, size, wide):
                count = min(wide, size - at)
                smalls_ref[0, to : to + 1, :count] = ref[:, start + at : start + at + count]
                to += 1
            to += to % 2


def first_back(x, mine, other, above, gain, sums, length, shape):
    tokens, width = x.shape
    cols = sums[0].shape[1] // 3
    sizes = [width, width, cols, cols] + [array.shape[1] for array in sums[1:]]
    grad_x, smalls = pl.pallas_call(
        first_back_kernel,
        grid=(tokens // length,),
        in_specs=[rows_of(length, width)] * 4
        + [whole(w) for w in (gain, *sums)],
        out_specs=[rows_of(length, width), pl.BlockSpec(shape, lambda i: (0, 0, 0))],
        out_shape=[
            jax.ShapeDtypeStruct((tokens, width), F32),
            jax.ShapeDtypeStruct(shape, F32),
        ],
        scratch_shapes=[pltpu.VMEM((1, width), F32)] * 2,
        name="first",
        cost_estimate=cost("first", 20 * tokens * width, 20 * tokens * width),
        compiler_params=params(),
    )(mine, other, x, above, gain, *sums)
    return grad_x, smalls, sizes


def from_partner(part):
    return lax.ppermute(part, "mp", [(0, 1), (1, 0)])


ORDERS = {"a": ("xynf", "yfxn"), "b": ("fnxy", "nyfx"), "q": ("xfyn", "xyfn"), "r": ("nyxf", "yxnf")}
SIXTHS = {"a": 4, "b": 2, "q": 3, "r": 3}


def orders_for(kind, bits):
    orders = []
    for names in kind:
        order = ["xynf".index(name) for name in names]
        order = [b for b in order if b < bits] + list(range(4, bits))
        orders.append([1 << b for b in order])
    return orders


def order_of_member(orders, member):
    return orders[member % 2]


def block_table(orders, bits):
    me = lax.axis_index("dp")
    count = 1 << bits
    masks = []
    for order in orders:
        masks.append(
            [
                sum(order[k] for k in range(bits) if r >> (bits - 1 - k) & 1)
                for r in range(count)
            ]
        )
    masks = jnp.asarray(masks, jnp.int32)
    return masks[lax.axis_index("mp") % 2] ^ me.astype(jnp.int32)


def exchange(array, orders, stage):
    dp, mp = lax.axis_size("dp"), lax.axis_size("mp")
    pairs = []
    for d in range(dp):
        for m in range(mp):
            pairs.append((d * mp + m, (d ^ order_of_member(orders, m)[stage]) * mp + m))
    return lax.ppermute(array, ("dp", "mp"), pairs)


def last_block(array):
    last = array.shape[0] - 1
    return pl.BlockSpec((1, *array.shape[1:]), lambda i: (last, 0, 0))


def add_kernel(*refs, counts, riders):
    outs, at = refs[sum(counts) + riders :], riders
    for k, count in enumerate(counts):
        total = refs[at][...]
        for ref in refs[at + 1 : at + count]:
            total = total + ref[...]
        if riders and not k:
            blocks = outs[k].shape[0] - 1
            outs[k][:blocks] = total
            outs[k][blocks:] = refs[0][...] + refs[1][...]
        else:
            outs[k][...] = total
        at += count


class Scatter:
    def __init__(self, send, keep, orders):
        self.keep, self.orders = keep, orders
        self.got, self.riders = [exchange(send, orders, 0)], ()

    def board(self, block):
        self.riders = (block, exchange(block, self.orders, 0))

    def take(self, after):
        self.got[-1] = lax.optimization_barrier((self.got[-1], after))[0]
        return [self.keep, *self.got]


def advance(scatters, after, passing=()):
    arrays = [scatter.take(after) for scatter in scatters]
    riders = list(scatters[0].riders)
    stage = len(scatters[0].got)
    half = scatters[0].keep.shape[0] >> stage
    step = half if riders or half == 1 else half // 2
    shapes, in_specs, out_specs = [], [last_block(array) for array in riders], []
    for k, group in enumerate(arrays):
        kept = group[0].shape[1:]
        more = 1 if riders and not k else 0
        spec = pl.BlockSpec((step, *kept), lambda i: (i + half // step, 0, 0))
        in_specs += [spec] * len(group)
        out_specs.append(pl.BlockSpec((step + more, *kept), lambda i: (i, 0, 0)))
        shapes.append(jax.ShapeDtypeStruct((half + more, *kept), F32))
    flat = riders + [array for group in arrays for array in group]
    anywhere = [pl.BlockSpec(memory_space=pl.ANY)] * len(passing)
    counts = [len(group) for group in arrays]
    made = pl.pallas_call(
        lambda *refs: add_kernel(
            *refs[: len(flat)],
            *refs[len(flat) + len(passing) : len(flat) + len(passing) + len(counts)],
            counts=counts,
            riders=len(riders),
        ),
        grid=(half // step,),
        in_specs=in_specs + anywhere,
        out_specs=out_specs + anywhere,
        out_shape=shapes + [jax.ShapeDtypeStruct(array.shape, array.dtype) for array in passing],
        input_output_aliases={len(flat) + i: len(shapes) + i for i in range(len(passing))},
        name="add",
        cost_estimate=cost("add", 0, 4 * sum(math.prod(shape.shape) for shape in shapes)),
        compiler_params=params(),
    )(*flat, *passing)
    for scatter, send in zip(scatters, made):
        scatter.got.append(exchange(send, scatter.orders, stage))
        if scatter.riders:
            scatter.riders = (send, scatter.got[-1])
    return made[0], made[len(scatters) :]


def finish_kernel(*refs, counts, outs, riders):
    values, at = [], riders
    for count in counts:
        total = refs[at][0]
        for ref in refs[at + 1 : at + count]:
            total = total + ref[0]
        values.append(total)
        at += count
    for out_ref, pieces in zip(refs[at:], outs):
        to = 0
        for part, start, columns in pieces:
            out_ref[:, to : to + columns] = values[part][:, start : start + columns]
            to += columns
    if riders:
        refs[-1][...] = refs[0][0] + refs[1][0]


def finish(scatters, after, widths):
    arrays = [scatter.take(after) for scatter in scatters]
    riders = [array for scatter in scatters for array in scatter.riders]
    flat = [array for group in arrays for array in group]
    size, parts = flat[0].shape[1], [group[0].shape[2] for group in arrays]
    outs, first = [], 0
    for width in widths:
        pieces, end = [], first + width
        while first < end:
            index, start, left = place_of(first, parts)
            pieces.append((index, start, min(end - first, left)))
            first += min(end - first, left)
        outs.append(pieces)
    shapes = [(size, width) for width in widths] + [(size, parts[0])] * (len(riders) // 2)
    block = lambda array: pl.BlockSpec((1, *array.shape[1:]), lambda i: (0, 0, 0))
    return pl.pallas_call(
        lambda *refs: finish_kernel(
            *refs, counts=[len(group) for group in arrays], outs=outs, riders=len(riders)
        ),
        grid=(1,),
        in_specs=[last_block(array) for array in riders] + [block(array) for array in flat],
        out_specs=[pl.BlockSpec(shape, lambda i: (0, 0)) for shape in shapes],
        out_shape=[jax.ShapeDtypeStruct(shape, F32) for shape in shapes],
        name="finish",
        cost_estimate=cost("add", 0, 4 * len(flat) * size * max(parts)),
        compiler_params=params(),
    )(*riders, *flat)


def butterfly_bits(width):
    dp = lax.axis_size("dp")
    bits = dp.bit_length() - 1
    return bits if (1 << bits) == dp and bits >= 3 and width // dp % 8 == 0 else 0


def parted(block, sizes):
    out, at, wide = [], 0, block.shape[1]
    for size in sizes:
        rows = -(-size // wide)
        out.append(block[at : at + rows].reshape(-1)[:size])
        at += rows + rows % 2
    return out


def on_device(
    inputs,
    segment_ids,
    ln1_gain,
    ln1_bias,
    w_query,
    b_query,
    w_key,
    w_value,
    b_value,
    w_output,
    b_output,
    ln2_gain,
    ln2_bias,
    w_up,
    b_up,
    w_down,
    b_down,
    cotangent,
):
    rows, length, width = inputs.shape
    cols = w_query.shape[1]
    tokens = rows * length
    hidden = w_up.shape[1]
    row = lambda vector: vector.reshape(-1, 128)
    pin = lambda values, after: lax.optimization_barrier((values, after))[0]
    x = inputs.reshape(tokens, width)
    top = cotangent.reshape(tokens, width)
    bits = butterfly_bits(width)

    orders = {key: orders_for(ORDERS[key], bits) for key in ORDERS}
    widths = [2 * hidden * SIXTHS[key] // 6 for key in "ab"] + [4 * cols * SIXTHS[key] // 6 for key in "qr"]
    tables = {key: block_table(orders[key], bits) for key in ORDERS} if bits else {}

    most = rows - 1
    firsts = (
        row(ln1_gain), row(ln1_bias), w_query, row(b_query), w_key, w_value, row(b_value),
        w_output, row(b_output),
    )
    *made, out_low = attend(x, segment_ids, *firsts, 0, most, ())
    low_other = from_partner(out_low)
    *made, out_high = attend(x, segment_ids, *firsts, most, rows - most, made)
    high_other = from_partner(out_high)
    normed, qkv, probs, context = made
    (middle, down_mine, back_mine, sum_top, sum_up), grad_hidden = forward(
        (out_low, out_high), (low_other, high_other), top, row(ln2_gain), row(ln2_bias),
        w_up, row(b_up), w_down, length, [tables[key] for key in "ab" if bits], widths[:2],
    )
    back_other, down_other = from_partner(back_mine), from_partner(down_mine)
    if bits:
        hiddens = [
            Scatter(*grad_hidden[:2], orders["a"]), Scatter(*grad_hidden[2:], orders["b"])
        ]
    (
        grad_middle, first_mine, sum_gain_two, sum_shift_two, sum_out, sum_qkv,
    ), grad_heads = attend_back(
        top, back_mine, back_other, middle, row(ln2_gain), w_output, qkv, probs, normed, context,
        w_query, w_key, w_value, [tables[key] for key in "qr" if bits], widths[2:],
    )
    outcome = pin(middle, sum_qkv) + (down_mine + down_other) + b_down

    if bits:
        after, passed = advance(hiddens, outcome, (first_mine, grad_heads[0], grad_heads[2]))
        first_mine = passed[0]
        heads = [
            Scatter(passed[1], grad_heads[1], orders["q"]),
            Scatter(passed[2], grad_heads[3], orders["r"]),
        ]
    first_other = from_partner(first_mine)
    grad_x, smalls, sizes = first_back(
        x, first_mine, first_other, grad_middle, row(ln1_gain),
        (sum_qkv, sum_out, sum_gain_two, sum_shift_two, sum_up, sum_top), length,
        (1, width // (1 << bits) if bits else 48, widths[2]),
    )
    if bits:
        heads[0].board(smalls)
        after, _ = advance(heads, smalls)
        for _ in range(2, bits):
            after, _ = advance(hiddens, after)
            after, _ = advance(heads, after)
        out_down, out_up = finish(hiddens, after, (hidden,) * 2)
        out_query, out_key, out_value, out_output, smalls = finish(heads, out_up, (cols,) * 4)
    else:
        scatter = lambda whole: lax.psum_scatter(whole, "dp", scatter_dimension=0, tiled=True)
        out_down, out_up = scatter(grad_hidden[0][:, :hidden]), scatter(grad_hidden[0][:, hidden:])
        out_query, out_key, out_value, out_output = (
            scatter(grad_heads[0][:, at : at + cols]) for at in range(0, 4 * cols, cols)
        )
        smalls = lax.psum(smalls[0], "dp")
    out_down, out_output = out_down.T, out_output.T
    smalls = parted(smalls, sizes)
    shape = inputs.shape
    return (
        outcome.reshape(shape),
        grad_x.reshape(shape),
        smalls[0],
        smalls[1],
        out_query,
        smalls[2],
        out_key,
        out_value,
        smalls[3],
        out_output,
        smalls[4],
        smalls[5],
        smalls[6],
        out_up,
        smalls[7],
        out_down,
        smalls[8],
    )


def solution(mesh):
    return jax.shard_map(
        on_device,
        mesh=mesh,
        in_specs=(
            P("dp", None, None),
            P("dp", None),
            P(),
            P(),
            P(None, "mp"),
            P("mp"),
            P(None, "mp"),
            P(None, "mp"),
            P("mp"),
            P("mp", None),
            P(),
            P(),
            P(),
            P(None, "mp"),
            P("mp"),
            P("mp", None),
            P(),
            P("dp", None, None),
        ),
        out_specs=(
            P("dp", None, None),
            P("dp", None, None),
            P(),
            P(),
            P("dp", "mp"),
            P("mp"),
            P("dp", "mp"),
            P("dp", "mp"),
            P("mp"),
            P("mp", "dp"),
            P(),
            P(),
            P(),
            P("dp", "mp"),
            P("mp"),
            P("mp", "dp"),
            P(),
        ),
        check_vma=False,
    )
```

```python
import math

import jax
import jax.numpy as jnp
from jax import lax
from jax.experimental import pallas as pl
from jax.experimental.pallas import tpu as pltpu
from jax.sharding import PartitionSpec as P

HD = 64
PAIR = 2 * HD
EPSILON = 1e-06
MASKED = -1000000000.0
SCALE = 1.0 / math.sqrt(HD)
CURVE = math.sqrt(2.0 / math.pi)
CUBIC = 0.044715
COSTS = {"attend": 0.01, "forward": 0.01, "back": 0.01, "first": 0.01, "add": 0.01}
BIG = 67043328
STEP = 512
SLAB = 64
F32 = jnp.float32
BF16 = jnp.bfloat16


def product(left, right, over):
    return lax.dot_general(
        left, right, ((over[:1], over[1:]), ((), ())), preferred_element_type=F32
    )


def left_product(left, right):
    return product(left, right, (0, 0))


def unit_rows(values):
    centered = values - jnp.mean(values, axis=-1, keepdims=True)
    inv_std = lax.rsqrt(jnp.mean(centered * centered, axis=-1, keepdims=True) + EPSILON)
    return centered * inv_std, inv_std


def norm_back(grad_out, unit, inv_std, gain):
    grad_unit = grad_out * gain
    return inv_std * (
        grad_unit
        - jnp.mean(grad_unit, axis=-1, keepdims=True)
        - unit * jnp.mean(grad_unit * unit, axis=-1, keepdims=True)
    )


def column_sum(values):
    return jnp.sum(values, axis=0, keepdims=True)


def line(ref):
    return jnp.concatenate([ref[r : r + 1, :] for r in range(ref.shape[0])], axis=1)


def add_up(ref, value):
    @pl.when(pl.program_id(0) == 0)
    def _():
        ref[...] = jnp.zeros_like(ref)

    ref[...] += value


def in_rows(far, near, sems, first, chunks):
    size = far.shape[0] // chunks
    rows = [pl.ds(c * size, size) for c in range(chunks)]
    return [
        pltpu.make_async_copy(far.at[part], near.at[part], sems.at[first + c])
        for c, part in enumerate(rows)
    ]


def started(copies):
    return lambda: [copy.start() for copy in copies] and None


def arrived(copies):
    return lambda: [copy.wait() for copy in copies] and None


def when_first(action):
    pl.when(pl.program_id(0) == 0)(action)


def either(low, high, rows_low, slab):
    return jnp.where(pl.program_id(0) < rows_low, low[slab, :], high[slab, :])


def last_step():
    return pl.program_id(0) == pl.num_programs(0) - 1


def leaving(tables, outs, pieces, widths, total, sems, make):
    copies, start = [], 0
    me, even = lax.axis_index("dp"), lax.axis_index("mp") % 2 == 0
    for turned, right, at, columns, index, to in pieces:
        if make:
            total[:, start : start + columns] = product(
                turned[...], right[:, at : at + columns], (1, 0)
            )
        fresh = []
        if tables:
            table, send, keep = tables[index], outs[2 * index], outs[2 * index + 1]
            half, size, _ = send.shape
            for r in range(2 * half):
                owner = jnp.where(even, table[0][r], table[1][r]) ^ me
                row = pl.multiple_of(owner * size, 8)
                far = send.at[r - half] if r >= half else keep.at[r]
                fresh.append(
                    pltpu.make_async_copy(
                        total.at[pl.ds(row, size), pl.ds(start, columns)],
                        far.at[:, pl.ds(to, columns)],
                        sems.at[len(copies) + r],
                    )
                )
        else:
            fresh.append(
                pltpu.make_async_copy(
                    total.at[:, pl.ds(start, columns)],
                    outs[0].at[:, pl.ds(sum(widths[:index]) + to, columns)],
                    sems.at[len(copies)],
                )
            )
        if make:
            started(fresh)()
        copies += fresh
        start += columns
    return copies


def leave(*args):
    arrived(leaving(*args, True))()


def pieces_of(sources, first, widths):
    pieces = []
    for turned, right, at, columns in sources:
        end = at + columns
        while at < end:
            index, to, left = place_of(first, widths)
            size = min(512, end - at, left)
            pieces.append((turned, right, at, size, index, to))
            at, first = at + size, first + size
    return pieces


def place_of(column, widths):
    for index, width in enumerate(widths):
        if column < width:
            return index, column, width - column
        column -= width


def step_rows(length):
    return pl.ds(pl.multiple_of(pl.program_id(0) * length, length), length)


def gradient_outs(tables, widths, width):
    if not tables:
        return [jax.ShapeDtypeStruct((width, sum(widths)), F32)], 8
    blocks = len(tables[0][0])
    shapes = [
        jax.ShapeDtypeStruct((blocks // 2, width // blocks, columns), F32)
        for columns in widths
        for _ in range(2)
    ]
    return shapes, blocks * 6


def in_turn(stages, count):
    for turn in range(count + len(stages) - 1):
        for late, stage in enumerate(stages):
            if 0 <= turn - late < count:
                stage(turn - late)


def lane_halves(width):
    lane = lax.broadcasted_iota(jnp.int32, (1, width), 1)
    low = (lane % PAIR < HD).astype(F32)
    return low, 1.0 - low


def attend_kernel(
    seg_ref, gain, shift, bq, bv, bo, wq_far, wk_far, wv_far, wo_far, x_ref, *refs, first_row
):
    normed_ref, qkv_ref, probs_ref, context_ref, out_ref = refs[-10:-5]
    wq, wk, wv, wo, sems = refs[-5:]
    fetches = []
    for i, (far, near) in enumerate(((wq_far, wq), (wk_far, wk), (wv_far, wv), (wo_far, wo))):
        fetches += in_rows(far, near, sems, 2 * i, 2)
    when_first(started(fetches))

    cols = wq.shape[1]
    gain_row, shift_row = line(gain), line(shift)
    for at in range(0, x_ref.shape[0], SLAB):
        slab = slice(at, at + SLAB)
        unit, _ = unit_rows(x_ref[slab, :])
        normed_ref[slab, :] = (unit * gain_row + shift_row).astype(BF16)
    normed = normed_ref[...]
    low, high = lane_halves(cols)
    when_first(arrived(fetches))
    queries = (product(normed, wq[...], (1, 0)) + line(bq)) * SCALE
    keys = product(normed, wk[...], (1, 0)).astype(BF16)
    values = (product(normed, wv[...], (1, 0)) + line(bv)).astype(BF16)
    qkv_ref[:, :cols] = queries.astype(BF16)
    qkv_ref[:, cols : 2 * cols] = keys
    qkv_ref[:, 2 * cols :] = values
    split = ((queries * low).astype(BF16), (queries * high).astype(BF16))
    seg_row = seg_ref[pl.ds(pl.program_id(0) + first_row, 1), :].astype(F32)
    length = seg_row.shape[1]
    seg_col = jnp.broadcast_to(seg_row, (128, length)).T
    same = jnp.concatenate([seg_col] * (length // 128), axis=1) == seg_row
    first = lax.broadcasted_iota(jnp.int32, (1, PAIR), 1) < HD
    scores, probs, made = {}, {}, {}

    def score(head):
        part = slice(head // 2 * PAIR, head // 2 * PAIR + PAIR)
        scores[head] = product(keys[:, part], split[head % 2][:, part], (1, 1))

    def soften(head):
        masked = jnp.where(same, scores.pop(head), MASKED)
        expo = jnp.exp(masked - jnp.max(masked, axis=0, keepdims=True))
        probs[head] = (expo * (1.0 / column_sum(expo))).astype(BF16)
        probs_ref[0, head] = probs[head]

    def gather(head):
        part = slice(head // 2 * PAIR, head // 2 * PAIR + PAIR)
        made[head] = product(probs.pop(head), values[:, part], (0, 0))
        if head % 2:
            context_ref[:, part] = jnp.where(first, made.pop(head - 1), made.pop(head)).astype(BF16)

    in_turn((score, soften, gather), cols // HD)
    out_ref[...] = product(context_ref[...], wo[...], (1, 0)) + 0.5 * (x_ref[...] + line(bo))


def whole(array):
    zeros = (0,) * array.ndim
    return pl.BlockSpec(array.shape, lambda i: zeros, pipeline_mode=pl.Buffered(1))


def rows_of(length, width):
    return pl.BlockSpec((length, width), lambda i: (i, 0))


def cost(name, flops, moved):
    weight = COSTS[name]
    return pl.CostEstimate(
        flops=int(weight * flops), bytes_accessed=int(weight * moved), transcendentals=0
    )


def params(limit=26 << 20):
    return pltpu.CompilerParams(vmem_limit_bytes=limit)


def attend(x, segments, gain, shift, wq, bq, wk, wv, bv, wo, bo, first_row, count, made):
    rows, length = segments.shape
    tokens, width = x.shape
    cols = wq.shape[1]
    heads = cols // HD
    at = lambda w: pl.BlockSpec((length, w), lambda i: (i + first_row, 0))
    shape = lambda w, kind: jax.ShapeDtypeStruct((tokens, w), kind)
    fixed = (segments, gain, shift, bq, bv, bo)
    weights = (wq, wk, wv, wo)
    done = tokens * count // rows
    return pl.pallas_call(
        lambda *refs: attend_kernel(*refs, first_row=first_row),
        grid=(count,),
        in_specs=[whole(w) for w in fixed]
        + [pl.BlockSpec(memory_space=pl.ANY)] * len(weights)
        + [at(width)]
        + [pl.BlockSpec(memory_space=pl.ANY)] * len(made),
        out_specs=[
            at(width),
            at(3 * cols),
            pl.BlockSpec((1, heads, length, length), lambda i: (i + first_row, 0, 0, 0)),
            at(cols),
            rows_of(length, width),
        ],
        out_shape=[
            shape(width, BF16),
            shape(3 * cols, BF16),
            jax.ShapeDtypeStruct((rows, heads, length, length), BF16),
            shape(cols, BF16),
            jax.ShapeDtypeStruct((count * length, width), F32),
        ],
        input_output_aliases={len(fixed) + len(weights) + 1 + i: i for i in range(len(made))},
        scratch_shapes=[pltpu.VMEM(w.shape, w.dtype) for w in weights]
        + [pltpu.SemaphoreType.DMA((2 * len(weights),))],
        name="attend",
        cost_estimate=cost("attend",
            8 * done * width * cols + 4 * done * length * cols,
            done * (10 * width + 8 * cols + 2 * heads * length) + 8 * width * cols,
        ),
        compiler_params=params(BIG),
    )(*fixed, *weights, x, *made)


def forward_kernel(*refs, tables, rows, rows_low, widths):
    mine_low, mine_high, other_low, other_high, top_ref, gain, shift, b_up, w_up, w_down = refs[:10]
    middle_ref, down_ref, back_ref, by_top, by_up = refs[10:15]
    outs, refs = refs[15:-14], refs[-14:]
    up_near, down_near, tops, turned_top, turned, acts, slopes, down_total, up_total = refs[:9]
    normed, up_sems, down_sems, down_outs, up_outs = refs[9:]
    step, length = pl.program_id(0), top_ref.shape[0]
    here = pl.ds(pl.multiple_of(step % rows * length, length), length)
    ups, downs = in_rows(w_up, up_near, up_sems, 0, 4), in_rows(w_down, down_near, down_sems, 0, 4)
    hidden = up_near.shape[1]
    of_down = pieces_of([(turned_top, acts, 0, hidden)], 0, widths)
    of_up = pieces_of([(turned, slopes, 0, hidden)], hidden, widths)
    down_args = (tables, outs, of_down, widths, down_total, down_outs)
    up_args = (tables, outs, of_up, widths, up_total, up_outs)
    when_first(started(ups))
    pl.when(step == 1)(started(downs))

    @pl.when(step < rows)
    def _():
        bias_up, gain_row, shift_row, top_sum = line(b_up), line(gain), line(shift), 0.0
        for at in range(0, length, SLAB):
            slab = slice(at, at + SLAB)
            middle = either(mine_low, mine_high, rows_low, slab) + either(
                other_low, other_high, rows_low, slab
            )
            middle_ref[slab, :] = middle
            unit, _ = unit_rows(middle)
            normed[slab, :] = (unit * gain_row + shift_row).astype(BF16)
            top_sum += column_sum(top_ref[slab, :])
        add_up(by_top, top_sum)
        tops[here, :] = top_ref[...].astype(BF16)
        turned_top[:, here] = tops[here, :].T
        turned[:, here] = normed[...].T
        when_first(arrived(ups))
        for at in range(0, hidden, STEP):
            units = slice(at, at + STEP)
            u = product(normed[...], up_near[:, units], (1, 0)) + bias_up[:, units]
            square = u * u
            bend = jnp.tanh(u * (CURVE + (CURVE * CUBIC) * square))
            above = 0.5 + 0.5 * bend
            act = u * above
            acts[here, units] = act.astype(BF16)
            slope = above + act * (1.0 - bend) * (CURVE + (3.0 * CURVE * CUBIC) * square)
            slopes[here, units] = slope.astype(BF16)

    @pl.when(step == rows - 1)
    def _():
        leaving(*down_args, True)

    @pl.when(step == rows)
    def _():
        arrived(downs)()
        by_up[...] = jnp.zeros_like(by_up)

    @pl.when(step >= rows)
    def _():
        for at in range(0, hidden, STEP):
            units = slice(at, at + STEP)
            grad = product(tops[here, :], down_near[units, :], (1, 1))
            grad = (grad * slopes[here, units].astype(F32)).astype(BF16)
            slopes[here, units] = grad
            by_up[:, units] += column_sum(grad.astype(F32))
        back_ref[...] = product(slopes[here, :], up_near[...], (1, 1))
        down_ref[...] = product(acts[here, :], down_near[...], (1, 0))

    @pl.when(step == 2 * rows - 1)
    def _():
        leave(*up_args)
        arrived(leaving(*down_args, False))()


def forward(mines, others, top, gain, shift, w_up, b_up, w_down, length, tables, widths):
    tokens, width = top.shape
    hidden = w_up.shape[1]
    rows, low = tokens // length, mines[0].shape[0] // length
    first = lambda i: jnp.minimum(i, rows - 1)
    low_spec = pl.BlockSpec((length, width), lambda i: (jnp.minimum(i, low - 1), 0))
    high_spec = pl.BlockSpec((length, width), lambda i: (jnp.clip(i - low, 0, rows - low - 1), 0))
    up_spec = pl.BlockSpec((length, width), lambda i: (first(i), 0))
    back_spec = pl.BlockSpec((length, width), lambda i: (jnp.maximum(i - rows, 0), 0))
    sum_spec = lambda w: pl.BlockSpec((1, w), lambda i: (0, 0))
    shape = lambda *dims: jax.ShapeDtypeStruct(dims, F32)
    anywhere = pl.BlockSpec(memory_space=pl.ANY)
    outs, copies = gradient_outs(tables, widths, width)
    fixed = (gain, shift, b_up)
    made = pl.pallas_call(
        lambda *refs: forward_kernel(
            *refs, tables=tables, rows=rows, rows_low=low, widths=widths
        ),
        grid=(2 * rows,),
        in_specs=[low_spec, high_spec] * 2
        + [up_spec]
        + [whole(w) for w in fixed]
        + [anywhere] * 2,
        out_specs=[up_spec, back_spec, back_spec, sum_spec(width), sum_spec(hidden)]
        + [anywhere] * len(outs),
        out_shape=[shape(tokens, width)] * 3 + [shape(1, width), shape(1, hidden)] + outs,
        scratch_shapes=[
            pltpu.VMEM(w_up.shape, BF16),
            pltpu.VMEM(w_down.shape, BF16),
            pltpu.VMEM((tokens, width), BF16),
            pltpu.VMEM((width, tokens), BF16),
            pltpu.VMEM((width, tokens), BF16),
            pltpu.VMEM((tokens, hidden), BF16),
            pltpu.VMEM((tokens, hidden), BF16),
            pltpu.VMEM((width, hidden), F32),
            pltpu.VMEM((width, hidden), F32),
            pltpu.VMEM((length, width), BF16),
            pltpu.SemaphoreType.DMA((4,)),
            pltpu.SemaphoreType.DMA((4,)),
            pltpu.SemaphoreType.DMA((copies,)),
            pltpu.SemaphoreType.DMA((copies,)),
        ],
        name="forward",
        cost_estimate=cost(
            "forward",
            12 * tokens * width * hidden,
            tokens * 24 * width + 12 * width * hidden,
        ),
        compiler_params=params(BIG),
    )(*mines, *others, top, *fixed, w_up, w_down)
    return made[:5], made[5:]


def attend_back_kernel(*refs, tables, widths):
    mine, other, refs = refs[0], refs[1], refs[2:]
    top_ref, middle_ref, gain, qkv_ref, probs_ref, normed_ref, context_ref = refs[:7]
    wo_far, wq_far, wk_far, wv_far = refs[7:11]
    grad_middle_ref, back_ref, sum_gain, sum_shift, sum_out, sum_qkv = refs[11:17]
    outs, refs = refs[17:-12], refs[-12:]
    rounded, grad_qkv_ref, contexts, turned, turned_two, total, wo, wq, wk, wv = refs[:10]
    sems, out_sems = refs[10:]
    cols, length = wq.shape[1], top_ref.shape[0]
    here = step_rows(length)
    fetches = []
    for i, (far, near) in enumerate(((wo_far, wo), (wq_far, wq), (wk_far, wk), (wv_far, wv))):
        fetches += in_rows(far, near, sems, 2 * i, 2)
    when_first(started(fetches))
    gain_row, by_gain, by_shift, by_out = line(gain), 0.0, 0.0, 0.0
    for at in range(0, length, SLAB):
        slab = slice(at, at + SLAB)
        unit, inv_std = unit_rows(middle_ref[slab, :])
        grad_normed = mine[slab, :] + other[slab, :]
        by_gain += column_sum(grad_normed * unit)
        by_shift += column_sum(grad_normed)
        grad_middle = top_ref[slab, :] + norm_back(grad_normed, unit, inv_std, gain_row)
        grad_middle_ref[slab, :] = grad_middle
        by_out += column_sum(grad_middle)
        rounded[slab, :] = grad_middle.astype(BF16)
    add_up(sum_gain, by_gain)
    add_up(sum_shift, by_shift)
    add_up(sum_out, by_out)
    turned[:, here] = normed_ref[...].T
    turned_two[:, here] = rounded[...].T
    contexts[here, :] = context_ref[...]
    when_first(arrived(fetches))
    grad_context = product(rounded[...], wo[...], (1, 1)).astype(BF16).astype(F32)
    low, high = lane_halves(cols)
    split = ((grad_context * low).astype(BF16), (grad_context * high).astype(BF16))
    first = lax.broadcasted_iota(jnp.int32, (1, PAIR), 1) < HD
    grad_probs, grad_scores, made = {}, {}, {}

    def at(head, which):
        start = which * cols + head // 2 * PAIR
        return slice(start, start + PAIR)

    def spread(head):
        grad_probs[head] = product(
            qkv_ref[:, at(head, 2)], split[head % 2][:, at(head, 0)], (1, 1)
        )

    def soften(head):
        wide = probs_ref[0, head].astype(F32)
        moved = wide * grad_probs.pop(head)
        grad_scores[head] = (moved - wide * column_sum(moved)).astype(BF16)

    def gather(head):
        grads = grad_scores.pop(head)
        made[head] = (
            product(grads, qkv_ref[:, at(head, 1)], (0, 0)),
            product(grads, qkv_ref[:, at(head, 0)], (1, 0)),
            product(probs_ref[0, head], split[head % 2][:, at(head, 0)], (1, 0)),
        )
        if head % 2:
            even, odd = made.pop(head - 1), made.pop(head)
            grad_query = jnp.where(first, even[0], odd[0]) * SCALE
            grad_qkv_ref[here, at(head, 0)] = grad_query.astype(BF16)
            grad_qkv_ref[here, at(head, 1)] = jnp.where(first, even[1], odd[1]).astype(BF16)
            grad_qkv_ref[here, at(head, 2)] = (even[2] + odd[2]).astype(BF16)

    in_turn((spread, soften, gather), cols // HD)
    grads = grad_qkv_ref[here, :]
    add_up(sum_qkv, column_sum(grads.astype(F32)))
    back_ref[...] = (
        product(grads[:, :cols], wq[...], (1, 1))
        + product(grads[:, cols : 2 * cols], wk[...], (1, 1))
        + product(grads[:, 2 * cols :], wv[...], (1, 1))
    )
    pieces = pieces_of(
        [(turned, grad_qkv_ref, 0, 3 * cols), (turned_two, contexts, 0, cols)], 0, widths
    )
    pl.when(last_step())(lambda: leave(tables, outs, pieces, widths, total, out_sems))


def attend_back(
    top, mine, other, middle, gain, wo, qkv, probs, normed, context, wq, wk, wv, tables, widths
):
    tokens, width = top.shape
    rows, heads, length, _ = probs.shape
    cols = wq.shape[1]
    line = lambda w: jax.ShapeDtypeStruct((1, w), F32)
    fixed = lambda w: pl.BlockSpec((1, w), lambda i: (0, 0))
    weights = (wo, wq, wk, wv)
    outs, copies = gradient_outs(tables, widths, width)
    anywhere = pl.BlockSpec(memory_space=pl.ANY)
    made = pl.pallas_call(
        lambda *refs: attend_back_kernel(*refs, tables=tables, widths=widths),
        grid=(rows,),
        in_specs=[rows_of(length, width)] * 4
        + [whole(gain), rows_of(length, 3 * cols)]
        + [pl.BlockSpec((1, heads, length, length), lambda i: (i, 0, 0, 0))]
        + [rows_of(length, width), rows_of(length, cols)]
        + [anywhere] * len(weights),
        out_specs=[rows_of(length, width)] * 2
        + [fixed(width), fixed(width), fixed(width), fixed(3 * cols)]
        + [anywhere] * len(outs),
        out_shape=[jax.ShapeDtypeStruct((tokens, width), F32)] * 2
        + [line(width), line(width), line(width), line(3 * cols)]
        + outs,
        scratch_shapes=[
            pltpu.VMEM((length, width), BF16),
            pltpu.VMEM((tokens, 3 * cols), BF16),
            pltpu.VMEM((tokens, cols), BF16),
            pltpu.VMEM((width, tokens), BF16),
            pltpu.VMEM((width, tokens), BF16),
            pltpu.VMEM((width, 4 * cols), F32),
        ]
        + [pltpu.VMEM(w.shape, w.dtype) for w in weights]
        + [
            pltpu.SemaphoreType.DMA((2 * len(weights),)),
            pltpu.SemaphoreType.DMA((copies,)),
        ],
        name="back",
        cost_estimate=cost(
            "back",
            16 * tokens * width * cols + 8 * tokens * length * cols,
            tokens * (26 * width + 8 * cols + 2 * heads * length) + 24 * width * cols,
        ),
        compiler_params=params(BIG),
    )(mine, other, top, middle, gain, qkv, probs, normed, context, *weights)
    return made[:6], made[6:]


def first_back_kernel(*refs):
    mine, other, refs = refs[0], refs[1], refs[2:]
    x_ref, above, gain, qkv_sum, out_sum, gain_two, shift_two, up_sum, top_sum = refs[:9]
    out_ref, smalls_ref, sum_gain, sum_shift = refs[9:]
    gain_row, by_gain, by_shift = line(gain), 0.0, 0.0
    for at in range(0, x_ref.shape[0], SLAB):
        slab = slice(at, at + SLAB)
        unit, inv_std = unit_rows(x_ref[slab, :])
        grad_normed = mine[slab, :] + other[slab, :]
        by_gain += column_sum(grad_normed * unit)
        by_shift += column_sum(grad_normed)
        out_ref[slab, :] = above[slab, :] + norm_back(grad_normed, unit, inv_std, gain_row)
    add_up(sum_gain, by_gain)
    add_up(sum_shift, by_shift)

    @pl.when(pl.program_id(0) == pl.num_programs(0) - 1)
    def _():
        smalls_ref[...] = jnp.zeros_like(smalls_ref)
        cols = qkv_sum.shape[1] // 3
        to = 0
        for ref, start, size in (
            (sum_gain, 0, sum_gain.shape[1]),
            (sum_shift, 0, sum_shift.shape[1]),
            (qkv_sum, 0, cols),
            (qkv_sum, 2 * cols, cols),
            (out_sum, 0, out_sum.shape[1]),
            (gain_two, 0, gain_two.shape[1]),
            (shift_two, 0, shift_two.shape[1]),
            (up_sum, 0, up_sum.shape[1]),
            (top_sum, 0, top_sum.shape[1]),
        ):
            wide = smalls_ref.shape[2]
            for at in range(0, size, wide):
                count = min(wide, size - at)
                smalls_ref[0, to : to + 1, :count] = ref[:, start + at : start + at + count]
                to += 1
            to += to % 2


def first_back(x, mine, other, above, gain, sums, length, shape):
    tokens, width = x.shape
    cols = sums[0].shape[1] // 3
    sizes = [width, width, cols, cols] + [array.shape[1] for array in sums[1:]]
    grad_x, smalls = pl.pallas_call(
        first_back_kernel,
        grid=(tokens // length,),
        in_specs=[rows_of(length, width)] * 4
        + [whole(w) for w in (gain, *sums)],
        out_specs=[rows_of(length, width), pl.BlockSpec(shape, lambda i: (0, 0, 0))],
        out_shape=[
            jax.ShapeDtypeStruct((tokens, width), F32),
            jax.ShapeDtypeStruct(shape, F32),
        ],
        scratch_shapes=[pltpu.VMEM((1, width), F32)] * 2,
        name="first",
        cost_estimate=cost("first", 20 * tokens * width, 20 * tokens * width),
        compiler_params=params(),
    )(mine, other, x, above, gain, *sums)
    return grad_x, smalls, sizes


def from_partner(part):
    return lax.ppermute(part, "mp", [(0, 1), (1, 0)])


ORDERS = {"a": ("xynf", "yfxn"), "b": ("fnxy", "nyfx"), "q": ("xfyn", "xyfn"), "r": ("nyxf", "yxnf")}
SIXTHS = {"a": 4, "b": 2, "q": 3, "r": 3}


def orders_for(kind, bits):
    orders = []
    for names in kind:
        order = ["xynf".index(name) for name in names]
        order = [b for b in order if b < bits] + list(range(4, bits))
        orders.append([1 << b for b in order])
    return orders


def order_of_member(orders, member):
    return orders[member % 2]


def block_masks(orders, bits):
    return [
        [
            sum(order[k] for k in range(bits) if r >> (bits - 1 - k) & 1)
            for r in range(1 << bits)
        ]
        for order in orders
    ]


def exchange(array, orders, stage):
    dp, mp = lax.axis_size("dp"), lax.axis_size("mp")
    pairs = []
    for d in range(dp):
        for m in range(mp):
            pairs.append((d * mp + m, (d ^ order_of_member(orders, m)[stage]) * mp + m))
    return lax.ppermute(array, ("dp", "mp"), pairs)


def last_block(array):
    last = array.shape[0] - 1
    return pl.BlockSpec((1, *array.shape[1:]), lambda i: (last, 0, 0))


def add_kernel(*refs, counts, riders):
    outs, at = refs[sum(counts) + riders :], riders
    for k, count in enumerate(counts):
        total = refs[at][...]
        for ref in refs[at + 1 : at + count]:
            total = total + ref[...]
        if riders and not k:
            blocks = outs[k].shape[0] - 1
            outs[k][:blocks] = total
            outs[k][blocks:] = refs[0][...] + refs[1][...]
        else:
            outs[k][...] = total
        at += count


class Scatter:
    def __init__(self, send, keep, orders):
        self.keep, self.orders = keep, orders
        self.got, self.riders = [exchange(send, orders, 0)], ()

    def board(self, block):
        self.riders = (block, exchange(block, self.orders, 0))

    def take(self, after):
        self.got[-1] = lax.optimization_barrier((self.got[-1], after))[0]
        return [self.keep, *self.got]


def advance(scatters, after, passing=()):
    arrays = [scatter.take(after) for scatter in scatters]
    riders = list(scatters[0].riders)
    stage = len(scatters[0].got)
    half = scatters[0].keep.shape[0] >> stage
    step = half if riders or half == 1 else half // 2
    shapes, in_specs, out_specs = [], [last_block(array) for array in riders], []
    for k, group in enumerate(arrays):
        kept = group[0].shape[1:]
        more = 1 if riders and not k else 0
        spec = pl.BlockSpec((step, *kept), lambda i: (i + half // step, 0, 0))
        in_specs += [spec] * len(group)
        out_specs.append(pl.BlockSpec((step + more, *kept), lambda i: (i, 0, 0)))
        shapes.append(jax.ShapeDtypeStruct((half + more, *kept), F32))
    flat = riders + [array for group in arrays for array in group]
    anywhere = [pl.BlockSpec(memory_space=pl.ANY)] * len(passing)
    counts = [len(group) for group in arrays]
    made = pl.pallas_call(
        lambda *refs: add_kernel(
            *refs[: len(flat)],
            *refs[len(flat) + len(passing) : len(flat) + len(passing) + len(counts)],
            counts=counts,
            riders=len(riders),
        ),
        grid=(half // step,),
        in_specs=in_specs + anywhere,
        out_specs=out_specs + anywhere,
        out_shape=shapes + [jax.ShapeDtypeStruct(array.shape, array.dtype) for array in passing],
        input_output_aliases={len(flat) + i: len(shapes) + i for i in range(len(passing))},
        name="add",
        cost_estimate=cost("add", 0, 4 * sum(math.prod(shape.shape) for shape in shapes)),
        compiler_params=params(),
    )(*flat, *passing)
    for scatter, send in zip(scatters, made):
        scatter.got.append(exchange(send, scatter.orders, stage))
        if scatter.riders:
            scatter.riders = (send, scatter.got[-1])
    return made[0], made[len(scatters) :]


def finish_kernel(*refs, counts, outs, riders):
    values, at = [], riders
    for count in counts:
        total = refs[at][0]
        for ref in refs[at + 1 : at + count]:
            total = total + ref[0]
        values.append(total)
        at += count
    for out_ref, pieces in zip(refs[at:], outs):
        to = 0
        for part, start, columns in pieces:
            out_ref[:, to : to + columns] = values[part][:, start : start + columns]
            to += columns
    if riders:
        block, row = refs[0][0] + refs[1][0], 0
        for out_ref in refs[at + len(outs) :]:
            count, wide = out_ref.shape[0], block.shape[1] // 128
            for r in range(count):
                start = r % wide * 128
                out_ref[r : r + 1, :] = block[row + r // wide : row + r // wide + 1, start : start + 128]
            rows = -(-count // wide)
            row += rows + rows % 2


def finish(scatters, after, widths, sizes=()):
    arrays = [scatter.take(after) for scatter in scatters]
    riders = [array for scatter in scatters for array in scatter.riders]
    flat = [array for group in arrays for array in group]
    size, parts = flat[0].shape[1], [group[0].shape[2] for group in arrays]
    outs, first = [], 0
    for width in widths:
        pieces, end = [], first + width
        while first < end:
            index, start, left = place_of(first, parts)
            pieces.append((index, start, min(end - first, left)))
            first += min(end - first, left)
        outs.append(pieces)
    shapes = [(size, width) for width in widths] + [(count // 128, 128) for count in sizes]
    block = lambda array: pl.BlockSpec((1, *array.shape[1:]), lambda i: (0, 0, 0))
    return pl.pallas_call(
        lambda *refs: finish_kernel(
            *refs, counts=[len(group) for group in arrays], outs=outs, riders=len(riders)
        ),
        grid=(1,),
        in_specs=[last_block(array) for array in riders] + [block(array) for array in flat],
        out_specs=[pl.BlockSpec(shape, lambda i: (0, 0)) for shape in shapes],
        out_shape=[jax.ShapeDtypeStruct(shape, F32) for shape in shapes],
        name="finish",
        cost_estimate=cost("add", 0, 4 * len(flat) * size * max(parts)),
        compiler_params=params(),
    )(*riders, *flat)


def butterfly_bits(width):
    dp = lax.axis_size("dp")
    bits = dp.bit_length() - 1
    return bits if (1 << bits) == dp and bits >= 3 and width // dp % 8 == 0 else 0


def parted(block, sizes):
    out, at, wide = [], 0, block.shape[1]
    for size in sizes:
        rows = -(-size // wide)
        out.append(block[at : at + rows].reshape(-1)[:size])
        at += rows + rows % 2
    return out


def on_device(
    inputs,
    segment_ids,
    ln1_gain,
    ln1_bias,
    w_query,
    b_query,
    w_key,
    w_value,
    b_value,
    w_output,
    b_output,
    ln2_gain,
    ln2_bias,
    w_up,
    b_up,
    w_down,
    b_down,
    cotangent,
):
    rows, length, width = inputs.shape
    cols = w_query.shape[1]
    tokens = rows * length
    hidden = w_up.shape[1]
    row = lambda vector: vector.reshape(-1, 128)
    pin = lambda values, after: lax.optimization_barrier((values, after))[0]
    x = inputs.reshape(tokens, width)
    top = cotangent.reshape(tokens, width)
    bits = butterfly_bits(width)

    orders = {key: orders_for(ORDERS[key], bits) for key in ORDERS}
    widths = [2 * hidden * SIXTHS[key] // 6 for key in "ab"] + [4 * cols * SIXTHS[key] // 6 for key in "qr"]
    tables = {key: block_masks(orders[key], bits) for key in ORDERS} if bits else {}

    most = rows - 1
    firsts = (
        row(ln1_gain), row(ln1_bias), w_query, row(b_query), w_key, w_value, row(b_value),
        w_output, row(b_output),
    )
    *made, out_low = attend(x, segment_ids, *firsts, 0, most, ())
    low_other = from_partner(out_low)
    *made, out_high = attend(x, segment_ids, *firsts, most, rows - most, made)
    high_other = from_partner(out_high)
    normed, qkv, probs, context = made
    (middle, down_mine, back_mine, sum_top, sum_up), grad_hidden = forward(
        (out_low, out_high), (low_other, high_other), top, row(ln2_gain), row(ln2_bias),
        w_up, row(b_up), w_down, length, [tables[key] for key in "ab" if bits], widths[:2],
    )
    back_other, down_other = from_partner(back_mine), from_partner(down_mine)
    if bits:
        hiddens = [
            Scatter(*grad_hidden[:2], orders["a"]), Scatter(*grad_hidden[2:], orders["b"])
        ]
    (
        grad_middle, first_mine, sum_gain_two, sum_shift_two, sum_out, sum_qkv,
    ), grad_heads = attend_back(
        top, back_mine, back_other, middle, row(ln2_gain), w_output, qkv, probs, normed, context,
        w_query, w_key, w_value, [tables[key] for key in "qr" if bits], widths[2:],
    )
    outcome = pin(middle, sum_qkv) + (down_mine + down_other) + b_down

    if bits:
        after, passed = advance(hiddens, outcome, (first_mine, grad_heads[0], grad_heads[2]))
        first_mine = passed[0]
        heads = [
            Scatter(passed[1], grad_heads[1], orders["q"]),
            Scatter(passed[2], grad_heads[3], orders["r"]),
        ]
    first_other = from_partner(first_mine)
    grad_x, smalls, sizes = first_back(
        x, first_mine, first_other, grad_middle, row(ln1_gain),
        (sum_qkv, sum_out, sum_gain_two, sum_shift_two, sum_up, sum_top), length,
        (1, width // (1 << bits) if bits else 48, widths[2]),
    )
    if bits:
        heads[0].board(smalls)
        after, _ = advance(heads, smalls)
        for _ in range(2, bits):
            after, _ = advance(hiddens, after)
            after, _ = advance(heads, after)
        out_down, out_up = finish(hiddens, after, (hidden,) * 2)
        out_query, out_key, out_value, out_output, *smalls = finish(
            heads, out_up, (cols,) * 4, sizes
        )
        smalls = [vector.reshape(-1) for vector in smalls]
    else:
        scatter = lambda whole: lax.psum_scatter(whole, "dp", scatter_dimension=0, tiled=True)
        out_down, out_up = scatter(grad_hidden[0][:, :hidden]), scatter(grad_hidden[0][:, hidden:])
        out_query, out_key, out_value, out_output = (
            scatter(grad_heads[0][:, at : at + cols]) for at in range(0, 4 * cols, cols)
        )
        smalls = parted(lax.psum(smalls[0], "dp"), sizes)
    out_down, out_output = out_down.T, out_output.T
    shape = inputs.shape
    return (
        outcome.reshape(shape),
        grad_x.reshape(shape),
        smalls[0],
        smalls[1],
        out_query,
        smalls[2],
        out_key,
        out_value,
        smalls[3],
        out_output,
        smalls[4],
        smalls[5],
        smalls[6],
        out_up,
        smalls[7],
        out_down,
        smalls[8],
    )


def solution(mesh):
    return jax.shard_map(
        on_device,
        mesh=mesh,
        in_specs=(
            P("dp", None, None),
            P("dp", None),
            P(),
            P(),
            P(None, "mp"),
            P("mp"),
            P(None, "mp"),
            P(None, "mp"),
            P("mp"),
            P("mp", None),
            P(),
            P(),
            P(),
            P(None, "mp"),
            P("mp"),
            P("mp", None),
            P(),
            P("dp", None, None),
        ),
        out_specs=(
            P("dp", None, None),
            P("dp", None, None),
            P(),
            P(),
            P("dp", "mp"),
            P("mp"),
            P("dp", "mp"),
            P("dp", "mp"),
            P("mp"),
            P("mp", "dp"),
            P(),
            P(),
            P(),
            P("dp", "mp"),
            P("mp"),
            P("mp", "dp"),
            P(),
        ),
        check_vma=False,
    )
```

```python
import math

import jax
import jax.numpy as jnp
from jax import lax
from jax.experimental import pallas as pl
from jax.experimental.pallas import tpu as pltpu
from jax.sharding import PartitionSpec as P

HD = 64
PAIR = 2 * HD
EPSILON = 1e-06
MASKED = -1000000000.0
SCALE = 1.0 / math.sqrt(HD)
CURVE = math.sqrt(2.0 / math.pi)
CUBIC = 0.044715
COSTS = {"attend": 0.01, "forward": 0.01, "back": 0.01, "first": 0.01, "add": 0.01}
BIG = 67043328
STEP = 512
SLAB = 64
F32 = jnp.float32
BF16 = jnp.bfloat16


def product(left, right, over):
    return lax.dot_general(
        left, right, ((over[:1], over[1:]), ((), ())), preferred_element_type=F32
    )


def left_product(left, right):
    return product(left, right, (0, 0))


def unit_rows(values):
    centered = values - jnp.mean(values, axis=-1, keepdims=True)
    inv_std = lax.rsqrt(jnp.mean(centered * centered, axis=-1, keepdims=True) + EPSILON)
    return centered * inv_std, inv_std


def norm_back(grad_out, unit, inv_std, gain):
    grad_unit = grad_out * gain
    return inv_std * (
        grad_unit
        - jnp.mean(grad_unit, axis=-1, keepdims=True)
        - unit * jnp.mean(grad_unit * unit, axis=-1, keepdims=True)
    )


def column_sum(values):
    return jnp.sum(values, axis=0, keepdims=True)


def line(ref):
    return jnp.concatenate([ref[r : r + 1, :] for r in range(ref.shape[0])], axis=1)


def add_up(ref, value):
    @pl.when(pl.program_id(0) == 0)
    def _():
        ref[...] = jnp.zeros_like(ref)

    ref[...] += value


def in_rows(far, near, sems, first, chunks):
    size = far.shape[0] // chunks
    rows = [pl.ds(c * size, size) for c in range(chunks)]
    return [
        pltpu.make_async_copy(far.at[part], near.at[part], sems.at[first + c])
        for c, part in enumerate(rows)
    ]


def fetch_heads(fars, near, out_far, out_near, sems):
    copies = in_rows(out_far, out_near, sems, 0, 2)
    cols = fars[0].shape[1]
    for i, far in enumerate(fars):
        size = far.shape[0] // 2
        for c in range(2):
            copies.append(
                pltpu.make_async_copy(
                    far.at[pl.ds(c * size, size)],
                    near.at[pl.ds(c * size, size), pl.ds(i * cols, cols)],
                    sems.at[2 + 2 * i + c],
                )
            )
    return copies


def started(copies):
    return lambda: [copy.start() for copy in copies] and None


def arrived(copies):
    return lambda: [copy.wait() for copy in copies] and None


def when_first(action):
    pl.when(pl.program_id(0) == 0)(action)


def either(low, high, rows_low, slab):
    return jnp.where(pl.program_id(0) < rows_low, low[slab, :], high[slab, :])


def last_step():
    return pl.program_id(0) == pl.num_programs(0) - 1


def leaving(tables, outs, pieces, widths, total, sems, make):
    copies, start = [], 0
    me, even = lax.axis_index("dp"), lax.axis_index("mp") % 2 == 0
    for turned, right, at, columns, index, to in pieces:
        if make:
            total[:, start : start + columns] = product(
                turned[...], right[:, at : at + columns], (1, 0)
            )
        fresh = []
        if tables:
            table, send, keep = tables[index], outs[2 * index], outs[2 * index + 1]
            half, size, _ = send.shape
            for r in range(2 * half):
                owner = jnp.where(even, table[0][r], table[1][r]) ^ me
                row = pl.multiple_of(owner * size, 8)
                far = send.at[r - half] if r >= half else keep.at[r]
                fresh.append(
                    pltpu.make_async_copy(
                        total.at[pl.ds(row, size), pl.ds(start, columns)],
                        far.at[:, pl.ds(to, columns)],
                        sems.at[len(copies) + r],
                    )
                )
        else:
            fresh.append(
                pltpu.make_async_copy(
                    total.at[:, pl.ds(start, columns)],
                    outs[0].at[:, pl.ds(sum(widths[:index]) + to, columns)],
                    sems.at[len(copies)],
                )
            )
        if make:
            started(fresh)()
        copies += fresh
        start += columns
    return copies


def leave(*args):
    arrived(leaving(*args, True))()


def pieces_of(sources, first, widths):
    pieces = []
    for turned, right, at, columns in sources:
        end = at + columns
        while at < end:
            index, to, left = place_of(first, widths)
            size = min(512, end - at, left)
            pieces.append((turned, right, at, size, index, to))
            at, first = at + size, first + size
    return pieces


def place_of(column, widths):
    for index, width in enumerate(widths):
        if column < width:
            return index, column, width - column
        column -= width


def step_rows(length):
    return pl.ds(pl.multiple_of(pl.program_id(0) * length, length), length)


def gradient_outs(tables, widths, width):
    if not tables:
        return [jax.ShapeDtypeStruct((width, sum(widths)), F32)], 8
    blocks = len(tables[0][0])
    shapes = [
        jax.ShapeDtypeStruct((blocks // 2, width // blocks, columns), F32)
        for columns in widths
        for _ in range(2)
    ]
    return shapes, blocks * 6


def in_turn(stages, count):
    for turn in range(count + len(stages) - 1):
        for late, stage in enumerate(stages):
            if 0 <= turn - late < count:
                stage(turn - late)


def lane_halves(width):
    lane = lax.broadcasted_iota(jnp.int32, (1, width), 1)
    low = (lane % PAIR < HD).astype(F32)
    return low, 1.0 - low


def attend_kernel(
    seg_ref, gain, shift, bq, bv, bo, wq_far, wk_far, wv_far, wo_far, x_ref, *refs, first_row
):
    normed_ref, qkv_ref, probs_ref, context_ref, out_ref = refs[-8:-3]
    w_all, wo, sems = refs[-3:]
    fetches = fetch_heads((wq_far, wk_far, wv_far), w_all, wo_far, wo, sems)
    when_first(started(fetches))

    cols = wo.shape[0]
    gain_row, shift_row = line(gain), line(shift)
    for at in range(0, x_ref.shape[0], SLAB):
        slab = slice(at, at + SLAB)
        unit, _ = unit_rows(x_ref[slab, :])
        normed_ref[slab, :] = (unit * gain_row + shift_row).astype(BF16)
    normed = normed_ref[...]
    low, high = lane_halves(cols)
    when_first(arrived(fetches))
    made_all = product(normed, w_all[...], (1, 0))
    queries = (made_all[:, :cols] + line(bq)) * SCALE
    keys = made_all[:, cols : 2 * cols].astype(BF16)
    values = (made_all[:, 2 * cols :] + line(bv)).astype(BF16)
    qkv_ref[:, :cols] = queries.astype(BF16)
    qkv_ref[:, cols : 2 * cols] = keys
    qkv_ref[:, 2 * cols :] = values
    split = ((queries * low).astype(BF16), (queries * high).astype(BF16))
    seg_row = seg_ref[pl.ds(pl.program_id(0) + first_row, 1), :].astype(F32)
    length = seg_row.shape[1]
    seg_col = jnp.broadcast_to(seg_row, (128, length)).T
    same = jnp.concatenate([seg_col] * (length // 128), axis=1) == seg_row
    first = lax.broadcasted_iota(jnp.int32, (1, PAIR), 1) < HD
    scores, probs, made = {}, {}, {}

    def score(head):
        part = slice(head // 2 * PAIR, head // 2 * PAIR + PAIR)
        scores[head] = product(keys[:, part], split[head % 2][:, part], (1, 1))

    def soften(head):
        masked = jnp.where(same, scores.pop(head), MASKED)
        expo = jnp.exp(masked - jnp.max(masked, axis=0, keepdims=True))
        probs[head] = (expo * (1.0 / column_sum(expo))).astype(BF16)
        probs_ref[0, head] = probs[head]

    def gather(head):
        part = slice(head // 2 * PAIR, head // 2 * PAIR + PAIR)
        made[head] = product(probs.pop(head), values[:, part], (0, 0))
        if head % 2:
            context_ref[:, part] = jnp.where(first, made.pop(head - 1), made.pop(head)).astype(BF16)

    in_turn((score, soften, gather), cols // HD)
    out_ref[...] = product(context_ref[...], wo[...], (1, 0)) + 0.5 * (x_ref[...] + line(bo))


def whole(array):
    zeros = (0,) * array.ndim
    return pl.BlockSpec(array.shape, lambda i: zeros, pipeline_mode=pl.Buffered(1))


def rows_of(length, width):
    return pl.BlockSpec((length, width), lambda i: (i, 0))


def cost(name, flops, moved):
    weight = COSTS[name]
    return pl.CostEstimate(
        flops=int(weight * flops), bytes_accessed=int(weight * moved), transcendentals=0
    )


def params(limit=26 << 20):
    return pltpu.CompilerParams(vmem_limit_bytes=limit)


def attend(x, segments, gain, shift, wq, bq, wk, wv, bv, wo, bo, first_row, count, made):
    rows, length = segments.shape
    tokens, width = x.shape
    cols = wq.shape[1]
    heads = cols // HD
    at = lambda w: pl.BlockSpec((length, w), lambda i: (i + first_row, 0))
    shape = lambda w, kind: jax.ShapeDtypeStruct((tokens, w), kind)
    fixed = (segments, gain, shift, bq, bv, bo)
    weights = (wq, wk, wv, wo)
    done = tokens * count // rows
    return pl.pallas_call(
        lambda *refs: attend_kernel(*refs, first_row=first_row),
        grid=(count,),
        in_specs=[whole(w) for w in fixed]
        + [pl.BlockSpec(memory_space=pl.ANY)] * len(weights)
        + [at(width)]
        + [pl.BlockSpec(memory_space=pl.ANY)] * len(made),
        out_specs=[
            at(width),
            at(3 * cols),
            pl.BlockSpec((1, heads, length, length), lambda i: (i + first_row, 0, 0, 0)),
            at(cols),
            rows_of(length, width),
        ],
        out_shape=[
            shape(width, BF16),
            shape(3 * cols, BF16),
            jax.ShapeDtypeStruct((rows, heads, length, length), BF16),
            shape(cols, BF16),
            jax.ShapeDtypeStruct((count * length, width), F32),
        ],
        input_output_aliases={len(fixed) + len(weights) + 1 + i: i for i in range(len(made))},
        scratch_shapes=[
            pltpu.VMEM((width, 3 * cols), BF16),
            pltpu.VMEM(wo.shape, BF16),
            pltpu.SemaphoreType.DMA((2 * len(weights),)),
        ],
        name="attend",
        cost_estimate=cost("attend",
            8 * done * width * cols + 4 * done * length * cols,
            done * (10 * width + 8 * cols + 2 * heads * length) + 8 * width * cols,
        ),
        compiler_params=params(BIG),
    )(*fixed, *weights, x, *made)


def forward_kernel(*refs, tables, rows, rows_low, widths):
    mine_low, mine_high, other_low, other_high, top_ref, gain, shift, b_up, w_up, w_down = refs[:10]
    middle_ref, down_ref, back_ref, by_top, by_up = refs[10:15]
    outs, refs = refs[15:-14], refs[-14:]
    up_near, down_near, tops, turned_top, turned, acts, slopes, down_total, up_total = refs[:9]
    normed, up_sems, down_sems, down_outs, up_outs = refs[9:]
    step, length = pl.program_id(0), top_ref.shape[0]
    here = pl.ds(pl.multiple_of(step % rows * length, length), length)
    ups, downs = in_rows(w_up, up_near, up_sems, 0, 4), in_rows(w_down, down_near, down_sems, 0, 4)
    hidden = up_near.shape[1]
    of_down = pieces_of([(turned_top, acts, 0, hidden)], 0, widths)
    of_up = pieces_of([(turned, slopes, 0, hidden)], hidden, widths)
    down_args = (tables, outs, of_down, widths, down_total, down_outs)
    up_args = (tables, outs, of_up, widths, up_total, up_outs)
    when_first(started(ups))
    pl.when(step == 1)(started(downs))

    @pl.when(step < rows)
    def _():
        bias_up, gain_row, shift_row, top_sum = line(b_up), line(gain), line(shift), 0.0
        for at in range(0, length, SLAB):
            slab = slice(at, at + SLAB)
            middle = either(mine_low, mine_high, rows_low, slab) + either(
                other_low, other_high, rows_low, slab
            )
            middle_ref[slab, :] = middle
            unit, _ = unit_rows(middle)
            normed[slab, :] = (unit * gain_row + shift_row).astype(BF16)
            top_sum += column_sum(top_ref[slab, :])
        add_up(by_top, top_sum)
        tops[here, :] = top_ref[...].astype(BF16)
        turned_top[:, here] = tops[here, :].T
        turned[:, here] = normed[...].T
        when_first(arrived(ups))
        for at in range(0, hidden, STEP):
            units = slice(at, at + STEP)
            u = product(normed[...], up_near[:, units], (1, 0)) + bias_up[:, units]
            square = u * u
            bend = jnp.tanh(u * (CURVE + (CURVE * CUBIC) * square))
            above = 0.5 + 0.5 * bend
            act = u * above
            acts[here, units] = act.astype(BF16)
            slope = above + act * (1.0 - bend) * (CURVE + (3.0 * CURVE * CUBIC) * square)
            slopes[here, units] = slope.astype(BF16)

    @pl.when(step == rows - 1)
    def _():
        leaving(*down_args, True)

    @pl.when(step == rows)
    def _():
        arrived(downs)()
        by_up[...] = jnp.zeros_like(by_up)

    @pl.when(step >= rows)
    def _():
        for at in range(0, hidden, STEP):
            units = slice(at, at + STEP)
            grad = product(tops[here, :], down_near[units, :], (1, 1))
            grad = (grad * slopes[here, units].astype(F32)).astype(BF16)
            slopes[here, units] = grad
            by_up[:, units] += column_sum(grad.astype(F32))
        down_ref[...] = product(acts[here, :], down_near[...], (1, 0))
        back_ref[...] = product(slopes[here, :], up_near[...], (1, 1))

    @pl.when(step == 2 * rows - 1)
    def _():
        leave(*up_args)
        arrived(leaving(*down_args, False))()


def forward(mines, others, top, gain, shift, w_up, b_up, w_down, length, tables, widths):
    tokens, width = top.shape
    hidden = w_up.shape[1]
    rows, low = tokens // length, mines[0].shape[0] // length
    first = lambda i: jnp.minimum(i, rows - 1)
    low_spec = pl.BlockSpec((length, width), lambda i: (jnp.minimum(i, low - 1), 0))
    high_spec = pl.BlockSpec((length, width), lambda i: (jnp.clip(i - low, 0, rows - low - 1), 0))
    up_spec = pl.BlockSpec((length, width), lambda i: (first(i), 0))
    back_spec = pl.BlockSpec((length, width), lambda i: (jnp.maximum(i - rows, 0), 0))
    sum_spec = lambda w: pl.BlockSpec((1, w), lambda i: (0, 0))
    shape = lambda *dims: jax.ShapeDtypeStruct(dims, F32)
    anywhere = pl.BlockSpec(memory_space=pl.ANY)
    outs, copies = gradient_outs(tables, widths, width)
    fixed = (gain, shift, b_up)
    made = pl.pallas_call(
        lambda *refs: forward_kernel(
            *refs, tables=tables, rows=rows, rows_low=low, widths=widths
        ),
        grid=(2 * rows,),
        in_specs=[low_spec, high_spec] * 2
        + [up_spec]
        + [whole(w) for w in fixed]
        + [anywhere] * 2,
        out_specs=[up_spec, back_spec, back_spec, sum_spec(width), sum_spec(hidden)]
        + [anywhere] * len(outs),
        out_shape=[shape(tokens, width)] * 3 + [shape(1, width), shape(1, hidden)] + outs,
        scratch_shapes=[
            pltpu.VMEM(w_up.shape, BF16),
            pltpu.VMEM(w_down.shape, BF16),
            pltpu.VMEM((tokens, width), BF16),
            pltpu.VMEM((width, tokens), BF16),
            pltpu.VMEM((width, tokens), BF16),
            pltpu.VMEM((tokens, hidden), BF16),
            pltpu.VMEM((tokens, hidden), BF16),
            pltpu.VMEM((width, hidden), F32),
            pltpu.VMEM((width, hidden), F32),
            pltpu.VMEM((length, width), BF16),
            pltpu.SemaphoreType.DMA((4,)),
            pltpu.SemaphoreType.DMA((4,)),
            pltpu.SemaphoreType.DMA((copies,)),
            pltpu.SemaphoreType.DMA((copies,)),
        ],
        name="forward",
        cost_estimate=cost(
            "forward",
            12 * tokens * width * hidden,
            tokens * 24 * width + 12 * width * hidden,
        ),
        compiler_params=params(BIG),
    )(*mines, *others, top, *fixed, w_up, w_down)
    return made[:5], made[5:]


def attend_back_kernel(*refs, tables, widths):
    mine, other, refs = refs[0], refs[1], refs[2:]
    top_ref, middle_ref, gain, qkv_ref, probs_ref, normed_ref, context_ref = refs[:7]
    wo_far, wq_far, wk_far, wv_far = refs[7:11]
    grad_middle_ref, back_ref, sum_gain, sum_shift, sum_out, sum_qkv = refs[11:17]
    outs, refs = refs[17:-10], refs[-10:]
    rounded, grad_qkv_ref, contexts, turned, turned_two, total, wo, w_all = refs[:8]
    sems, out_sems = refs[8:]
    cols, length = wo.shape[0], top_ref.shape[0]
    here = step_rows(length)
    fetches = fetch_heads((wq_far, wk_far, wv_far), w_all, wo_far, wo, sems)
    when_first(started(fetches))
    gain_row, by_gain, by_shift, by_out = line(gain), 0.0, 0.0, 0.0
    for at in range(0, length, SLAB):
        slab = slice(at, at + SLAB)
        unit, inv_std = unit_rows(middle_ref[slab, :])
        grad_normed = mine[slab, :] + other[slab, :]
        by_gain += column_sum(grad_normed * unit)
        by_shift += column_sum(grad_normed)
        grad_middle = top_ref[slab, :] + norm_back(grad_normed, unit, inv_std, gain_row)
        grad_middle_ref[slab, :] = grad_middle
        by_out += column_sum(grad_middle)
        rounded[slab, :] = grad_middle.astype(BF16)
    add_up(sum_gain, by_gain)
    add_up(sum_shift, by_shift)
    add_up(sum_out, by_out)
    turned[:, here] = normed_ref[...].T
    turned_two[:, here] = rounded[...].T
    contexts[here, :] = context_ref[...]
    when_first(arrived(fetches))
    grad_context = product(rounded[...], wo[...], (1, 1)).astype(BF16).astype(F32)
    low, high = lane_halves(cols)
    split = ((grad_context * low).astype(BF16), (grad_context * high).astype(BF16))
    first = lax.broadcasted_iota(jnp.int32, (1, PAIR), 1) < HD
    grad_probs, grad_scores, made = {}, {}, {}

    def at(head, which):
        start = which * cols + head // 2 * PAIR
        return slice(start, start + PAIR)

    def spread(head):
        grad_probs[head] = product(
            qkv_ref[:, at(head, 2)], split[head % 2][:, at(head, 0)], (1, 1)
        )

    def soften(head):
        wide = probs_ref[0, head].astype(F32)
        moved = wide * grad_probs.pop(head)
        grad_scores[head] = (moved - wide * column_sum(moved)).astype(BF16)

    def gather(head):
        grads = grad_scores.pop(head)
        made[head] = (
            product(grads, qkv_ref[:, at(head, 1)], (0, 0)),
            product(grads, qkv_ref[:, at(head, 0)], (1, 0)),
            product(probs_ref[0, head], split[head % 2][:, at(head, 0)], (1, 0)),
        )
        if head % 2:
            even, odd = made.pop(head - 1), made.pop(head)
            grad_query = jnp.where(first, even[0], odd[0]) * SCALE
            grad_qkv_ref[here, at(head, 0)] = grad_query.astype(BF16)
            grad_qkv_ref[here, at(head, 1)] = jnp.where(first, even[1], odd[1]).astype(BF16)
            grad_qkv_ref[here, at(head, 2)] = (even[2] + odd[2]).astype(BF16)

    in_turn((spread, soften, gather), cols // HD)
    grads = grad_qkv_ref[here, :]
    add_up(sum_qkv, column_sum(grads.astype(F32)))
    back_ref[...] = product(grads, w_all[...], (1, 1))
    pieces = pieces_of(
        [(turned, grad_qkv_ref, 0, 3 * cols), (turned_two, contexts, 0, cols)], 0, widths
    )
    pl.when(last_step())(lambda: leave(tables, outs, pieces, widths, total, out_sems))


def attend_back(
    top, mine, other, middle, gain, wo, qkv, probs, normed, context, wq, wk, wv, tables, widths
):
    tokens, width = top.shape
    rows, heads, length, _ = probs.shape
    cols = wq.shape[1]
    line = lambda w: jax.ShapeDtypeStruct((1, w), F32)
    fixed = lambda w: pl.BlockSpec((1, w), lambda i: (0, 0))
    weights = (wo, wq, wk, wv)
    outs, copies = gradient_outs(tables, widths, width)
    anywhere = pl.BlockSpec(memory_space=pl.ANY)
    made = pl.pallas_call(
        lambda *refs: attend_back_kernel(*refs, tables=tables, widths=widths),
        grid=(rows,),
        in_specs=[rows_of(length, width)] * 4
        + [whole(gain), rows_of(length, 3 * cols)]
        + [pl.BlockSpec((1, heads, length, length), lambda i: (i, 0, 0, 0))]
        + [rows_of(length, width), rows_of(length, cols)]
        + [anywhere] * len(weights),
        out_specs=[rows_of(length, width)] * 2
        + [fixed(width), fixed(width), fixed(width), fixed(3 * cols)]
        + [anywhere] * len(outs),
        out_shape=[jax.ShapeDtypeStruct((tokens, width), F32)] * 2
        + [line(width), line(width), line(width), line(3 * cols)]
        + outs,
        scratch_shapes=[
            pltpu.VMEM((length, width), BF16),
            pltpu.VMEM((tokens, 3 * cols), BF16),
            pltpu.VMEM((tokens, cols), BF16),
            pltpu.VMEM((width, tokens), BF16),
            pltpu.VMEM((width, tokens), BF16),
            pltpu.VMEM((width, 4 * cols), F32),
        ]
        + [
            pltpu.VMEM(wo.shape, BF16),
            pltpu.VMEM((width, 3 * cols), BF16),
            pltpu.SemaphoreType.DMA((2 * len(weights),)),
            pltpu.SemaphoreType.DMA((copies,)),
        ],
        name="back",
        cost_estimate=cost(
            "back",
            16 * tokens * width * cols + 8 * tokens * length * cols,
            tokens * (26 * width + 8 * cols + 2 * heads * length) + 24 * width * cols,
        ),
        compiler_params=params(BIG),
    )(mine, other, top, middle, gain, qkv, probs, normed, context, *weights)
    return made[:6], made[6:]


def first_back_kernel(*refs):
    mine, other, refs = refs[0], refs[1], refs[2:]
    x_ref, above, gain, qkv_sum, out_sum, gain_two, shift_two, up_sum, top_sum = refs[:9]
    out_ref, smalls_ref, sum_gain, sum_shift = refs[9:]
    gain_row, by_gain, by_shift = line(gain), 0.0, 0.0
    for at in range(0, x_ref.shape[0], SLAB):
        slab = slice(at, at + SLAB)
        unit, inv_std = unit_rows(x_ref[slab, :])
        grad_normed = mine[slab, :] + other[slab, :]
        by_gain += column_sum(grad_normed * unit)
        by_shift += column_sum(grad_normed)
        out_ref[slab, :] = above[slab, :] + norm_back(grad_normed, unit, inv_std, gain_row)
    add_up(sum_gain, by_gain)
    add_up(sum_shift, by_shift)

    @pl.when(pl.program_id(0) == pl.num_programs(0) - 1)
    def _():
        smalls_ref[...] = jnp.zeros_like(smalls_ref)
        cols = qkv_sum.shape[1] // 3
        to = 0
        for ref, start, size in (
            (sum_gain, 0, sum_gain.shape[1]),
            (sum_shift, 0, sum_shift.shape[1]),
            (qkv_sum, 0, cols),
            (qkv_sum, 2 * cols, cols),
            (out_sum, 0, out_sum.shape[1]),
            (gain_two, 0, gain_two.shape[1]),
            (shift_two, 0, shift_two.shape[1]),
            (up_sum, 0, up_sum.shape[1]),
            (top_sum, 0, top_sum.shape[1]),
        ):
            wide = smalls_ref.shape[2]
            for at in range(0, size, wide):
                count = min(wide, size - at)
                smalls_ref[0, to : to + 1, :count] = ref[:, start + at : start + at + count]
                to += 1
            to += to % 2


def first_back(x, mine, other, above, gain, sums, length, shape):
    tokens, width = x.shape
    cols = sums[0].shape[1] // 3
    sizes = [width, width, cols, cols] + [array.shape[1] for array in sums[1:]]
    grad_x, smalls = pl.pallas_call(
        first_back_kernel,
        grid=(tokens // length,),
        in_specs=[rows_of(length, width)] * 4
        + [whole(w) for w in (gain, *sums)],
        out_specs=[rows_of(length, width), pl.BlockSpec(shape, lambda i: (0, 0, 0))],
        out_shape=[
            jax.ShapeDtypeStruct((tokens, width), F32),
            jax.ShapeDtypeStruct(shape, F32),
        ],
        scratch_shapes=[pltpu.VMEM((1, width), F32)] * 2,
        name="first",
        cost_estimate=cost("first", 20 * tokens * width, 20 * tokens * width),
        compiler_params=params(),
    )(mine, other, x, above, gain, *sums)
    return grad_x, smalls, sizes


def from_partner(part):
    return lax.ppermute(part, "mp", [(0, 1), (1, 0)])


ORDERS = {"a": ("ynxf", "xfyn"), "b": ("nxfy", "fxny"), "q": ("yfxn", "yxfn"), "r": ("xnyf", "xynf")}
SIXTHS = {"a": 4, "b": 2, "q": 3, "r": 3}


def orders_for(kind, bits):
    orders = []
    for names in kind:
        order = ["xynf".index(name) for name in names]
        order = [b for b in order if b < bits] + list(range(4, bits))
        orders.append([1 << b for b in order])
    return orders


def order_of_member(orders, member):
    return orders[member % 2]


def block_masks(orders, bits):
    return [
        [
            sum(order[k] for k in range(bits) if r >> (bits - 1 - k) & 1)
            for r in range(1 << bits)
        ]
        for order in orders
    ]


def exchange(array, orders, stage):
    dp, mp = lax.axis_size("dp"), lax.axis_size("mp")
    pairs = []
    for d in range(dp):
        for m in range(mp):
            pairs.append((d * mp + m, (d ^ order_of_member(orders, m)[stage]) * mp + m))
    return lax.ppermute(array, ("dp", "mp"), pairs)


def last_block(array):
    last = array.shape[0] - 1
    return pl.BlockSpec((1, *array.shape[1:]), lambda i: (last, 0, 0))


def add_kernel(*refs, counts, riders):
    outs, at = refs[sum(counts) + riders :], riders
    for k, count in enumerate(counts):
        total = refs[at][...]
        for ref in refs[at + 1 : at + count]:
            total = total + ref[...]
        if riders and not k:
            blocks = outs[k].shape[0] - 1
            outs[k][:blocks] = total
            outs[k][blocks:] = refs[0][...] + refs[1][...]
        else:
            outs[k][...] = total
        at += count


class Scatter:
    def __init__(self, send, keep, orders):
        self.keep, self.orders = keep, orders
        self.got, self.riders = [exchange(send, orders, 0)], ()

    def board(self, block):
        self.riders = (block, exchange(block, self.orders, 0))

    def take(self, after):
        self.got[-1] = lax.optimization_barrier((self.got[-1], after))[0]
        return [self.keep, *self.got]


def advance(scatters, after, passing=()):
    arrays = [scatter.take(after) for scatter in scatters]
    riders = list(scatters[0].riders)
    stage = len(scatters[0].got)
    half = scatters[0].keep.shape[0] >> stage
    step = half if riders or half == 1 else half // 2
    shapes, in_specs, out_specs = [], [last_block(array) for array in riders], []
    for k, group in enumerate(arrays):
        kept = group[0].shape[1:]
        more = 1 if riders and not k else 0
        spec = pl.BlockSpec((step, *kept), lambda i: (i + half // step, 0, 0))
        in_specs += [spec] * len(group)
        out_specs.append(pl.BlockSpec((step + more, *kept), lambda i: (i, 0, 0)))
        shapes.append(jax.ShapeDtypeStruct((half + more, *kept), F32))
    flat = riders + [array for group in arrays for array in group]
    anywhere = [pl.BlockSpec(memory_space=pl.ANY)] * len(passing)
    counts = [len(group) for group in arrays]
    made = pl.pallas_call(
        lambda *refs: add_kernel(
            *refs[: len(flat)],
            *refs[len(flat) + len(passing) : len(flat) + len(passing) + len(counts)],
            counts=counts,
            riders=len(riders),
        ),
        grid=(half // step,),
        in_specs=in_specs + anywhere,
        out_specs=out_specs + anywhere,
        out_shape=shapes + [jax.ShapeDtypeStruct(array.shape, array.dtype) for array in passing],
        input_output_aliases={len(flat) + i: len(shapes) + i for i in range(len(passing))},
        name="add",
        cost_estimate=cost("add", 0, 4 * sum(math.prod(shape.shape) for shape in shapes)),
        compiler_params=params(),
    )(*flat, *passing)
    for scatter, send in zip(scatters, made):
        scatter.got.append(exchange(send, scatter.orders, stage))
        if scatter.riders:
            scatter.riders = (send, scatter.got[-1])
    return made[0], made[len(scatters) :]


def finish_kernel(*refs, counts, outs, riders):
    values, at = [], riders
    for count in counts:
        total = refs[at][0]
        for ref in refs[at + 1 : at + count]:
            total = total + ref[0]
        values.append(total)
        at += count
    for out_ref, pieces in zip(refs[at:], outs):
        to = 0
        for part, start, columns in pieces:
            out_ref[:, to : to + columns] = values[part][:, start : start + columns]
            to += columns
    if riders:
        block, row = refs[0][0] + refs[1][0], 0
        for out_ref in refs[at + len(outs) :]:
            count, wide = out_ref.shape[0], block.shape[1] // 128
            for r in range(count):
                start = r % wide * 128
                out_ref[r : r + 1, :] = block[row + r // wide : row + r // wide + 1, start : start + 128]
            rows = -(-count // wide)
            row += rows + rows % 2


def finish(scatters, after, widths, sizes=()):
    arrays = [scatter.take(after) for scatter in scatters]
    riders = [array for scatter in scatters for array in scatter.riders]
    flat = [array for group in arrays for array in group]
    size, parts = flat[0].shape[1], [group[0].shape[2] for group in arrays]
    outs, first = [], 0
    for width in widths:
        pieces, end = [], first + width
        while first < end:
            index, start, left = place_of(first, parts)
            pieces.append((index, start, min(end - first, left)))
            first += min(end - first, left)
        outs.append(pieces)
    shapes = [(size, width) for width in widths] + [(count // 128, 128) for count in sizes]
    block = lambda array: pl.BlockSpec((1, *array.shape[1:]), lambda i: (0, 0, 0))
    return pl.pallas_call(
        lambda *refs: finish_kernel(
            *refs, counts=[len(group) for group in arrays], outs=outs, riders=len(riders)
        ),
        grid=(1,),
        in_specs=[last_block(array) for array in riders] + [block(array) for array in flat],
        out_specs=[pl.BlockSpec(shape, lambda i: (0, 0)) for shape in shapes],
        out_shape=[jax.ShapeDtypeStruct(shape, F32) for shape in shapes],
        name="finish",
        cost_estimate=cost("add", 0, 4 * len(flat) * size * max(parts)),
        compiler_params=params(),
    )(*riders, *flat)


def butterfly_bits(width):
    dp = lax.axis_size("dp")
    bits = dp.bit_length() - 1
    return bits if (1 << bits) == dp and bits >= 3 and width // dp % 8 == 0 else 0


def parted(block, sizes):
    out, at, wide = [], 0, block.shape[1]
    for size in sizes:
        rows = -(-size // wide)
        out.append(block[at : at + rows].reshape(-1)[:size])
        at += rows + rows % 2
    return out


def on_device(
    inputs,
    segment_ids,
    ln1_gain,
    ln1_bias,
    w_query,
    b_query,
    w_key,
    w_value,
    b_value,
    w_output,
    b_output,
    ln2_gain,
    ln2_bias,
    w_up,
    b_up,
    w_down,
    b_down,
    cotangent,
):
    rows, length, width = inputs.shape
    cols = w_query.shape[1]
    tokens = rows * length
    hidden = w_up.shape[1]
    row = lambda vector: vector.reshape(-1, 128)
    pin = lambda values, after: lax.optimization_barrier((values, after))[0]
    x = inputs.reshape(tokens, width)
    top = cotangent.reshape(tokens, width)
    bits = butterfly_bits(width)

    orders = {key: orders_for(ORDERS[key], bits) for key in ORDERS}
    widths = [2 * hidden * SIXTHS[key] // 6 for key in "ab"] + [4 * cols * SIXTHS[key] // 6 for key in "qr"]
    tables = {key: block_masks(orders[key], bits) for key in ORDERS} if bits else {}

    most = rows - 1
    firsts = (
        row(ln1_gain), row(ln1_bias), w_query, row(b_query), w_key, w_value, row(b_value),
        w_output, row(b_output),
    )
    *made, out_low = attend(x, segment_ids, *firsts, 0, most, ())
    low_other = from_partner(out_low)
    *made, out_high = attend(x, segment_ids, *firsts, most, rows - most, made)
    high_other = from_partner(out_high)
    normed, qkv, probs, context = made
    (middle, down_mine, back_mine, sum_top, sum_up), grad_hidden = forward(
        (out_low, out_high), (low_other, high_other), top, row(ln2_gain), row(ln2_bias),
        w_up, row(b_up), w_down, length, [tables[key] for key in "ab" if bits], widths[:2],
    )
    back_other, down_other = from_partner(back_mine), from_partner(down_mine)
    if bits:
        hiddens = [
            Scatter(*grad_hidden[:2], orders["a"]), Scatter(*grad_hidden[2:], orders["b"])
        ]
    (
        grad_middle, first_mine, sum_gain_two, sum_shift_two, sum_out, sum_qkv,
    ), grad_heads = attend_back(
        top, back_mine, back_other, middle, row(ln2_gain), w_output, qkv, probs, normed, context,
        w_query, w_key, w_value, [tables[key] for key in "qr" if bits], widths[2:],
    )
    outcome = pin(middle, sum_qkv) + (down_mine + down_other) + b_down

    if bits:
        after, passed = advance(hiddens, outcome, (first_mine, grad_heads[0], grad_heads[2]))
        first_mine = passed[0]
        heads = [
            Scatter(passed[1], grad_heads[1], orders["q"]),
            Scatter(passed[2], grad_heads[3], orders["r"]),
        ]
    first_other = from_partner(first_mine)
    grad_x, smalls, sizes = first_back(
        x, first_mine, first_other, grad_middle, row(ln1_gain),
        (sum_qkv, sum_out, sum_gain_two, sum_shift_two, sum_up, sum_top), length,
        (1, width // (1 << bits) if bits else 48, widths[2]),
    )
    if bits:
        heads[0].board(smalls)
        after, _ = advance(heads, smalls)
        for _ in range(2, bits):
            after, _ = advance(hiddens, after)
            after, _ = advance(heads, after)
        out_down, out_up = finish(hiddens, after, (hidden,) * 2)
        out_query, out_key, out_value, out_output, *smalls = finish(
            heads, out_up, (cols,) * 4, sizes
        )
        smalls = [vector.reshape(-1) for vector in smalls]
    else:
        scatter = lambda whole: lax.psum_scatter(whole, "dp", scatter_dimension=0, tiled=True)
        out_down, out_up = scatter(grad_hidden[0][:, :hidden]), scatter(grad_hidden[0][:, hidden:])
        out_query, out_key, out_value, out_output = (
            scatter(grad_heads[0][:, at : at + cols]) for at in range(0, 4 * cols, cols)
        )
        smalls = parted(lax.psum(smalls[0], "dp"), sizes)
    out_down, out_output = out_down.T, out_output.T
    shape = inputs.shape
    return (
        outcome.reshape(shape),
        grad_x.reshape(shape),
        smalls[0],
        smalls[1],
        out_query,
        smalls[2],
        out_key,
        out_value,
        smalls[3],
        out_output,
        smalls[4],
        smalls[5],
        smalls[6],
        out_up,
        smalls[7],
        out_down,
        smalls[8],
    )


def solution(mesh):
    return jax.shard_map(
        on_device,
        mesh=mesh,
        in_specs=(
            P("dp", None, None),
            P("dp", None),
            P(),
            P(),
            P(None, "mp"),
            P("mp"),
            P(None, "mp"),
            P(None, "mp"),
            P("mp"),
            P("mp", None),
            P(),
            P(),
            P(),
            P(None, "mp"),
            P("mp"),
            P("mp", None),
            P(),
            P("dp", None, None),
        ),
        out_specs=(
            P("dp", None, None),
            P("dp", None, None),
            P(),
            P(),
            P("dp", "mp"),
            P("mp"),
            P("dp", "mp"),
            P("dp", "mp"),
            P("mp"),
            P("mp", "dp"),
            P(),
            P(),
            P(),
            P("dp", "mp"),
            P("mp"),
            P("mp", "dp"),
            P(),
        ),
        check_vma=False,
    )
```

```python
import math

import jax
import jax.numpy as jnp
from jax import lax
from jax.experimental import pallas as pl
from jax.experimental.pallas import tpu as pltpu
from jax.sharding import PartitionSpec as P

HD = 64
PAIR = 2 * HD
EPSILON = 1e-06
MASKED = -1000000000.0
SCALE = 1.0 / math.sqrt(HD)
CURVE = math.sqrt(2.0 / math.pi)
CUBIC = 0.044715
COSTS = {"attend": 0.01, "forward": 0.01, "back": 0.01, "first": 0.01, "add": 0.01}
BIG = 67043328
STEP = 512
SLAB = 64
F32 = jnp.float32
BF16 = jnp.bfloat16


def product(left, right, over):
    return lax.dot_general(
        left, right, ((over[:1], over[1:]), ((), ())), preferred_element_type=F32
    )


def left_product(left, right):
    return product(left, right, (0, 0))


def unit_rows(values):
    centered = values - jnp.mean(values, axis=-1, keepdims=True)
    inv_std = lax.rsqrt(jnp.mean(centered * centered, axis=-1, keepdims=True) + EPSILON)
    return centered * inv_std, inv_std


def norm_back(grad_out, unit, inv_std, gain):
    grad_unit = grad_out * gain
    return inv_std * (
        grad_unit
        - jnp.mean(grad_unit, axis=-1, keepdims=True)
        - unit * jnp.mean(grad_unit * unit, axis=-1, keepdims=True)
    )


def column_sum(values):
    return jnp.sum(values, axis=0, keepdims=True)


def line(ref):
    return jnp.concatenate([ref[r : r + 1, :] for r in range(ref.shape[0])], axis=1)


def add_up(ref, value):
    @pl.when(pl.program_id(0) == 0)
    def _():
        ref[...] = jnp.zeros_like(ref)

    ref[...] += value


def in_rows(far, near, sems, first, chunks):
    size = far.shape[0] // chunks
    rows = [pl.ds(c * size, size) for c in range(chunks)]
    return [
        pltpu.make_async_copy(far.at[part], near.at[part], sems.at[first + c])
        for c, part in enumerate(rows)
    ]


def fetch_heads(fars, near, out_far, out_near, sems):
    copies = in_rows(out_far, out_near, sems, 0, 2)
    cols = fars[0].shape[1]
    for i, far in enumerate(fars):
        size = far.shape[0] // 2
        for c in range(2):
            copies.append(
                pltpu.make_async_copy(
                    far.at[pl.ds(c * size, size)],
                    near.at[pl.ds(c * size, size), pl.ds(i * cols, cols)],
                    sems.at[2 + 2 * i + c],
                )
            )
    return copies


def started(copies):
    return lambda: [copy.start() for copy in copies] and None


def arrived(copies):
    return lambda: [copy.wait() for copy in copies] and None


def when_first(action):
    pl.when(pl.program_id(0) == 0)(action)


def either(low, high, rows_low, slab):
    return jnp.where(pl.program_id(0) < rows_low, low[slab, :], high[slab, :])


def last_step():
    return pl.program_id(0) == pl.num_programs(0) - 1


def leaving(tables, outs, pieces, widths, total, sems, make):
    copies, start = [], 0
    me, even = lax.axis_index("dp"), lax.axis_index("mp") % 2 == 0
    for turned, right, at, columns, index, to in pieces:
        if make:
            total[:, start : start + columns] = product(
                turned[...], right[:, at : at + columns], (1, 0)
            )
        fresh = []
        if tables:
            table, send, keep = tables[index], outs[2 * index], outs[2 * index + 1]
            half, size, _ = send.shape
            for r in range(2 * half):
                owner = jnp.where(even, table[0][r], table[1][r]) ^ me
                row = pl.multiple_of(owner * size, 8)
                far = send.at[r - half] if r >= half else keep.at[r]
                fresh.append(
                    pltpu.make_async_copy(
                        total.at[pl.ds(row, size), pl.ds(start, columns)],
                        far.at[:, pl.ds(to, columns)],
                        sems.at[len(copies) + r],
                    )
                )
        else:
            fresh.append(
                pltpu.make_async_copy(
                    total.at[:, pl.ds(start, columns)],
                    outs[0].at[:, pl.ds(sum(widths[:index]) + to, columns)],
                    sems.at[len(copies)],
                )
            )
        if make:
            started(fresh)()
        copies += fresh
        start += columns
    return copies


def leave(*args):
    arrived(leaving(*args, True))()


def pieces_of(sources, first, widths):
    pieces = []
    for turned, right, at, columns in sources:
        end = at + columns
        while at < end:
            index, to, left = place_of(first, widths)
            size = min(512, end - at, left)
            pieces.append((turned, right, at, size, index, to))
            at, first = at + size, first + size
    return pieces


def place_of(column, widths):
    for index, width in enumerate(widths):
        if column < width:
            return index, column, width - column
        column -= width


def step_rows(length):
    return pl.ds(pl.multiple_of(pl.program_id(0) * length, length), length)


def gradient_outs(tables, widths, width):
    if not tables:
        return [jax.ShapeDtypeStruct((width, sum(widths)), F32)], 8
    blocks = len(tables[0][0])
    shapes = [
        jax.ShapeDtypeStruct((blocks // 2, width // blocks, columns), F32)
        for columns in widths
        for _ in range(2)
    ]
    return shapes, blocks * 6


def in_turn(stages, count):
    for turn in range(count + len(stages) - 1):
        for late, stage in enumerate(stages):
            if 0 <= turn - late < count:
                stage(turn - late)


def lane_halves(width):
    lane = lax.broadcasted_iota(jnp.int32, (1, width), 1)
    low = (lane % PAIR < HD).astype(F32)
    return low, 1.0 - low


def attend_kernel(
    seg_ref, gain, shift, bq, bv, bo, wq_far, wk_far, wv_far, wo_far, x_ref, *refs, first_row
):
    normed_ref, qkv_ref, probs_ref, context_ref, out_ref = refs[-8:-3]
    w_all, wo, sems = refs[-3:]
    fetches = fetch_heads((wq_far, wk_far, wv_far), w_all, wo_far, wo, sems)
    when_first(started(fetches))

    cols = wo.shape[0]
    gain_row, shift_row = line(gain), line(shift)
    for at in range(0, x_ref.shape[0], SLAB):
        slab = slice(at, at + SLAB)
        unit, _ = unit_rows(x_ref[slab, :])
        normed_ref[slab, :] = (unit * gain_row + shift_row).astype(BF16)
    normed = normed_ref[...]
    low, high = lane_halves(cols)
    when_first(arrived(fetches))
    made_all = product(normed, w_all[...], (1, 0))
    queries = (made_all[:, :cols] + line(bq)) * SCALE
    keys = made_all[:, cols : 2 * cols].astype(BF16)
    values = (made_all[:, 2 * cols :] + line(bv)).astype(BF16)
    qkv_ref[:, :cols] = queries.astype(BF16)
    qkv_ref[:, cols : 2 * cols] = keys
    qkv_ref[:, 2 * cols :] = values
    split = ((queries * low).astype(BF16), (queries * high).astype(BF16))
    seg_row = seg_ref[pl.ds(pl.program_id(0) + first_row, 1), :].astype(F32)
    length = seg_row.shape[1]
    seg_col = jnp.broadcast_to(seg_row, (128, length)).T
    same = jnp.concatenate([seg_col] * (length // 128), axis=1) == seg_row
    first = lax.broadcasted_iota(jnp.int32, (1, PAIR), 1) < HD
    scores, probs, made = {}, {}, {}

    def score(head):
        part = slice(head // 2 * PAIR, head // 2 * PAIR + PAIR)
        scores[head] = product(keys[:, part], split[head % 2][:, part], (1, 1))

    def soften(head):
        masked = jnp.where(same, scores.pop(head), MASKED)
        expo = jnp.exp(masked - jnp.max(masked, axis=0, keepdims=True))
        probs[head] = (expo * (1.0 / column_sum(expo))).astype(BF16)
        probs_ref[0, head] = probs[head]

    def gather(head):
        part = slice(head // 2 * PAIR, head // 2 * PAIR + PAIR)
        made[head] = product(probs.pop(head), values[:, part], (0, 0))
        if head % 2:
            context_ref[:, part] = jnp.where(first, made.pop(head - 1), made.pop(head)).astype(BF16)

    in_turn((score, soften, gather), cols // HD)
    out_ref[...] = product(context_ref[...], wo[...], (1, 0)) + 0.5 * (x_ref[...] + line(bo))


def whole(array):
    zeros = (0,) * array.ndim
    return pl.BlockSpec(array.shape, lambda i: zeros, pipeline_mode=pl.Buffered(1))


def rows_of(length, width):
    return pl.BlockSpec((length, width), lambda i: (i, 0))


def cost(name, flops, moved):
    weight = COSTS[name]
    return pl.CostEstimate(
        flops=int(weight * flops), bytes_accessed=int(weight * moved), transcendentals=0
    )


def params(limit=26 << 20):
    return pltpu.CompilerParams(vmem_limit_bytes=limit)


def attend(x, segments, gain, shift, wq, bq, wk, wv, bv, wo, bo, first_row, count, made):
    rows, length = segments.shape
    tokens, width = x.shape
    cols = wq.shape[1]
    heads = cols // HD
    at = lambda w: pl.BlockSpec((length, w), lambda i: (i + first_row, 0))
    shape = lambda w, kind: jax.ShapeDtypeStruct((tokens, w), kind)
    fixed = (segments, gain, shift, bq, bv, bo)
    weights = (wq, wk, wv, wo)
    done = tokens * count // rows
    return pl.pallas_call(
        lambda *refs: attend_kernel(*refs, first_row=first_row),
        grid=(count,),
        in_specs=[whole(w) for w in fixed]
        + [pl.BlockSpec(memory_space=pl.ANY)] * len(weights)
        + [at(width)]
        + [pl.BlockSpec(memory_space=pl.ANY)] * len(made),
        out_specs=[
            at(width),
            at(3 * cols),
            pl.BlockSpec((1, heads, length, length), lambda i: (i + first_row, 0, 0, 0)),
            at(cols),
            rows_of(length, width),
        ],
        out_shape=[
            shape(width, BF16),
            shape(3 * cols, BF16),
            jax.ShapeDtypeStruct((rows, heads, length, length), BF16),
            shape(cols, BF16),
            jax.ShapeDtypeStruct((count * length, width), F32),
        ],
        input_output_aliases={len(fixed) + len(weights) + 1 + i: i for i in range(len(made))},
        scratch_shapes=[
            pltpu.VMEM((width, 3 * cols), BF16),
            pltpu.VMEM(wo.shape, BF16),
            pltpu.SemaphoreType.DMA((2 * len(weights),)),
        ],
        name="attend",
        cost_estimate=cost("attend",
            8 * done * width * cols + 4 * done * length * cols,
            done * (10 * width + 8 * cols + 2 * heads * length) + 8 * width * cols,
        ),
        compiler_params=params(BIG),
    )(*fixed, *weights, x, *made)


def forward_kernel(*refs, tables, rows, rows_low, widths):
    mine_low, mine_high, other_low, other_high, top_ref, gain, shift, b_up, w_up, w_down = refs[:10]
    middle_ref, down_ref, back_ref, by_top, by_up = refs[10:15]
    outs, refs = refs[15:-14], refs[-14:]
    up_near, down_near, tops, turned_top, turned, acts, slopes, down_total, up_total = refs[:9]
    normed, up_sems, down_sems, down_outs, up_outs = refs[9:]
    step, length = pl.program_id(0), top_ref.shape[0]
    here = pl.ds(pl.multiple_of(step % rows * length, length), length)
    ups, downs = in_rows(w_up, up_near, up_sems, 0, 4), in_rows(w_down, down_near, down_sems, 0, 4)
    hidden = up_near.shape[1]
    of_down = pieces_of([(turned_top, acts, 0, hidden)], 0, widths)
    of_up = pieces_of([(turned, slopes, 0, hidden)], hidden, widths)
    down_args = (tables, outs, of_down, widths, down_total, down_outs)
    up_args = (tables, outs, of_up, widths, up_total, up_outs)
    when_first(started(ups))
    pl.when(step == 1)(started(downs))

    @pl.when(step < rows)
    def _():
        bias_up, gain_row, shift_row, top_sum = line(b_up), line(gain), line(shift), 0.0
        for at in range(0, length, SLAB):
            slab = slice(at, at + SLAB)
            middle = either(mine_low, mine_high, rows_low, slab) + either(
                other_low, other_high, rows_low, slab
            )
            middle_ref[slab, :] = middle
            unit, _ = unit_rows(middle)
            normed[slab, :] = (unit * gain_row + shift_row).astype(BF16)
            top_sum += column_sum(top_ref[slab, :])
        add_up(by_top, top_sum)
        tops[here, :] = top_ref[...].astype(BF16)
        turned_top[:, here] = tops[here, :].T
        turned[:, here] = normed[...].T
        when_first(arrived(ups))
        for at in range(0, hidden, STEP):
            units = slice(at, at + STEP)
            u = product(normed[...], up_near[:, units], (1, 0)) + bias_up[:, units]
            square = u * u
            bend = jnp.tanh(u * (CURVE + (CURVE * CUBIC) * square))
            above = 0.5 + 0.5 * bend
            act = u * above
            acts[here, units] = act.astype(BF16)
            slope = above + act * (1.0 - bend) * (CURVE + (3.0 * CURVE * CUBIC) * square)
            slopes[here, units] = slope.astype(BF16)

    @pl.when(step == rows - 1)
    def _():
        leaving(*down_args, True)

    @pl.when(step == rows)
    def _():
        arrived(downs)()
        by_up[...] = jnp.zeros_like(by_up)

    @pl.when(step >= rows)
    def _():
        for at in range(0, hidden, STEP):
            units = slice(at, at + STEP)
            grad = product(tops[here, :], down_near[units, :], (1, 1))
            grad = (grad * slopes[here, units].astype(F32)).astype(BF16)
            slopes[here, units] = grad
            by_up[:, units] += column_sum(grad.astype(F32))
        down_ref[...] = product(acts[here, :], down_near[...], (1, 0))
        back_ref[...] = product(slopes[here, :], up_near[...], (1, 1))

    @pl.when(step == 2 * rows - 1)
    def _():
        leave(*up_args)
        arrived(leaving(*down_args, False))()


def forward(mines, others, top, gain, shift, w_up, b_up, w_down, length, tables, widths):
    tokens, width = top.shape
    hidden = w_up.shape[1]
    rows, low = tokens // length, mines[0].shape[0] // length
    first = lambda i: jnp.minimum(i, rows - 1)
    low_spec = pl.BlockSpec((length, width), lambda i: (jnp.minimum(i, low - 1), 0))
    high_spec = pl.BlockSpec((length, width), lambda i: (jnp.clip(i - low, 0, rows - low - 1), 0))
    up_spec = pl.BlockSpec((length, width), lambda i: (first(i), 0))
    back_spec = pl.BlockSpec((length, width), lambda i: (jnp.maximum(i - rows, 0), 0))
    sum_spec = lambda w: pl.BlockSpec((1, w), lambda i: (0, 0))
    shape = lambda *dims: jax.ShapeDtypeStruct(dims, F32)
    anywhere = pl.BlockSpec(memory_space=pl.ANY)
    outs, copies = gradient_outs(tables, widths, width)
    fixed = (gain, shift, b_up)
    made = pl.pallas_call(
        lambda *refs: forward_kernel(
            *refs, tables=tables, rows=rows, rows_low=low, widths=widths
        ),
        grid=(2 * rows,),
        in_specs=[low_spec, high_spec] * 2
        + [up_spec]
        + [whole(w) for w in fixed]
        + [anywhere] * 2,
        out_specs=[up_spec, back_spec, back_spec, sum_spec(width), sum_spec(hidden)]
        + [anywhere] * len(outs),
        out_shape=[shape(tokens, width)] * 3 + [shape(1, width), shape(1, hidden)] + outs,
        scratch_shapes=[
            pltpu.VMEM(w_up.shape, BF16),
            pltpu.VMEM(w_down.shape, BF16),
            pltpu.VMEM((tokens, width), BF16),
            pltpu.VMEM((width, tokens), BF16),
            pltpu.VMEM((width, tokens), BF16),
            pltpu.VMEM((tokens, hidden), BF16),
            pltpu.VMEM((tokens, hidden), BF16),
            pltpu.VMEM((width, hidden), F32),
            pltpu.VMEM((width, hidden), F32),
            pltpu.VMEM((length, width), BF16),
            pltpu.SemaphoreType.DMA((4,)),
            pltpu.SemaphoreType.DMA((4,)),
            pltpu.SemaphoreType.DMA((copies,)),
            pltpu.SemaphoreType.DMA((copies,)),
        ],
        name="forward",
        cost_estimate=cost(
            "forward",
            12 * tokens * width * hidden,
            tokens * 24 * width + 12 * width * hidden,
        ),
        compiler_params=params(BIG),
    )(*mines, *others, top, *fixed, w_up, w_down)
    return made[:5], made[5:]


def attend_back_kernel(*refs, tables, widths):
    mine, other, refs = refs[0], refs[1], refs[2:]
    top_ref, middle_ref, gain, qkv_ref, probs_ref, normed_ref, context_ref = refs[:7]
    wo_far, wq_far, wk_far, wv_far = refs[7:11]
    grad_middle_ref, back_ref, sum_gain, sum_shift, sum_out, sum_qkv = refs[11:17]
    outs, refs = refs[17:-10], refs[-10:]
    rounded, grad_qkv_ref, contexts, turned, turned_two, total, wo, w_all = refs[:8]
    sems, out_sems = refs[8:]
    cols, length = wo.shape[0], top_ref.shape[0]
    here = step_rows(length)
    fetches = fetch_heads((wq_far, wk_far, wv_far), w_all, wo_far, wo, sems)
    when_first(started(fetches))
    gain_row, by_gain, by_shift, by_out = line(gain), 0.0, 0.0, 0.0
    for at in range(0, length, SLAB):
        slab = slice(at, at + SLAB)
        unit, inv_std = unit_rows(middle_ref[slab, :])
        grad_normed = mine[slab, :] + other[slab, :]
        by_gain += column_sum(grad_normed * unit)
        by_shift += column_sum(grad_normed)
        grad_middle = top_ref[slab, :] + norm_back(grad_normed, unit, inv_std, gain_row)
        grad_middle_ref[slab, :] = grad_middle
        by_out += column_sum(grad_middle)
        rounded[slab, :] = grad_middle.astype(BF16)
    add_up(sum_gain, by_gain)
    add_up(sum_shift, by_shift)
    add_up(sum_out, by_out)
    turned[:, here] = normed_ref[...].T
    turned_two[:, here] = rounded[...].T
    contexts[here, :] = context_ref[...]
    when_first(arrived(fetches))
    grad_context = product(rounded[...], wo[...], (1, 1)).astype(BF16).astype(F32)
    low, high = lane_halves(cols)
    split = ((grad_context * low).astype(BF16), (grad_context * high).astype(BF16))
    first = lax.broadcasted_iota(jnp.int32, (1, PAIR), 1) < HD
    grad_probs, grad_scores, made = {}, {}, {}

    def at(head, which):
        start = which * cols + head // 2 * PAIR
        return slice(start, start + PAIR)

    def spread(head):
        grad_probs[head] = product(
            qkv_ref[:, at(head, 2)], split[head % 2][:, at(head, 0)], (1, 1)
        )

    def soften(head):
        wide = probs_ref[0, head].astype(F32)
        moved = wide * grad_probs.pop(head)
        grad_scores[head] = (moved - wide * column_sum(moved)).astype(BF16)

    def gather(head):
        grads = grad_scores.pop(head)
        made[head] = (
            product(grads, qkv_ref[:, at(head, 1)], (0, 0)),
            product(grads, qkv_ref[:, at(head, 0)], (1, 0)),
            product(probs_ref[0, head], split[head % 2][:, at(head, 0)], (1, 0)),
        )
        if head % 2:
            even, odd = made.pop(head - 1), made.pop(head)
            grad_query = jnp.where(first, even[0], odd[0]) * SCALE
            grad_qkv_ref[here, at(head, 0)] = grad_query.astype(BF16)
            grad_qkv_ref[here, at(head, 1)] = jnp.where(first, even[1], odd[1]).astype(BF16)
            grad_qkv_ref[here, at(head, 2)] = (even[2] + odd[2]).astype(BF16)

    in_turn((spread, soften, gather), cols // HD)
    grads = grad_qkv_ref[here, :]
    add_up(sum_qkv, column_sum(grads.astype(F32)))
    back_ref[...] = product(grads, w_all[...], (1, 1))
    pieces = pieces_of(
        [(turned, grad_qkv_ref, 0, 3 * cols), (turned_two, contexts, 0, cols)], 0, widths
    )
    pl.when(last_step())(lambda: leave(tables, outs, pieces, widths, total, out_sems))


def attend_back(
    top, mine, other, middle, gain, wo, qkv, probs, normed, context, wq, wk, wv, tables, widths
):
    tokens, width = top.shape
    rows, heads, length, _ = probs.shape
    cols = wq.shape[1]
    line = lambda w: jax.ShapeDtypeStruct((1, w), F32)
    fixed = lambda w: pl.BlockSpec((1, w), lambda i: (0, 0))
    weights = (wo, wq, wk, wv)
    outs, copies = gradient_outs(tables, widths, width)
    anywhere = pl.BlockSpec(memory_space=pl.ANY)
    made = pl.pallas_call(
        lambda *refs: attend_back_kernel(*refs, tables=tables, widths=widths),
        grid=(rows,),
        in_specs=[rows_of(length, width)] * 4
        + [whole(gain), rows_of(length, 3 * cols)]
        + [pl.BlockSpec((1, heads, length, length), lambda i: (i, 0, 0, 0))]
        + [rows_of(length, width), rows_of(length, cols)]
        + [anywhere] * len(weights),
        out_specs=[rows_of(length, width)] * 2
        + [fixed(width), fixed(width), fixed(width), fixed(3 * cols)]
        + [anywhere] * len(outs),
        out_shape=[jax.ShapeDtypeStruct((tokens, width), F32)] * 2
        + [line(width), line(width), line(width), line(3 * cols)]
        + outs,
        scratch_shapes=[
            pltpu.VMEM((length, width), BF16),
            pltpu.VMEM((tokens, 3 * cols), BF16),
            pltpu.VMEM((tokens, cols), BF16),
            pltpu.VMEM((width, tokens), BF16),
            pltpu.VMEM((width, tokens), BF16),
            pltpu.VMEM((width, 4 * cols), F32),
        ]
        + [
            pltpu.VMEM(wo.shape, BF16),
            pltpu.VMEM((width, 3 * cols), BF16),
            pltpu.SemaphoreType.DMA((2 * len(weights),)),
            pltpu.SemaphoreType.DMA((copies,)),
        ],
        name="back",
        cost_estimate=cost(
            "back",
            16 * tokens * width * cols + 8 * tokens * length * cols,
            tokens * (26 * width + 8 * cols + 2 * heads * length) + 24 * width * cols,
        ),
        compiler_params=params(BIG),
    )(mine, other, top, middle, gain, qkv, probs, normed, context, *weights)
    return made[:6], made[6:]


def first_back_kernel(*refs):
    mine, other, refs = refs[0], refs[1], refs[2:]
    x_ref, above, gain, qkv_sum, out_sum, gain_two, shift_two, up_sum, top_sum = refs[:9]
    out_ref, smalls_ref, sum_gain, sum_shift = refs[9:]
    gain_row, by_gain, by_shift = line(gain), 0.0, 0.0
    for at in range(0, x_ref.shape[0], SLAB):
        slab = slice(at, at + SLAB)
        unit, inv_std = unit_rows(x_ref[slab, :])
        grad_normed = mine[slab, :] + other[slab, :]
        by_gain += column_sum(grad_normed * unit)
        by_shift += column_sum(grad_normed)
        out_ref[slab, :] = above[slab, :] + norm_back(grad_normed, unit, inv_std, gain_row)
    add_up(sum_gain, by_gain)
    add_up(sum_shift, by_shift)

    @pl.when(pl.program_id(0) == pl.num_programs(0) - 1)
    def _():
        smalls_ref[...] = jnp.zeros_like(smalls_ref)
        cols = qkv_sum.shape[1] // 3
        to = 0
        for ref, start, size in (
            (sum_gain, 0, sum_gain.shape[1]),
            (sum_shift, 0, sum_shift.shape[1]),
            (qkv_sum, 0, cols),
            (qkv_sum, 2 * cols, cols),
            (out_sum, 0, out_sum.shape[1]),
            (gain_two, 0, gain_two.shape[1]),
            (shift_two, 0, shift_two.shape[1]),
            (up_sum, 0, up_sum.shape[1]),
            (top_sum, 0, top_sum.shape[1]),
        ):
            wide = smalls_ref.shape[2]
            for at in range(0, size, wide):
                count = min(wide, size - at)
                smalls_ref[0, to : to + 1, :count] = ref[:, start + at : start + at + count]
                to += 1
            to += to % 2


def first_back(x, mine, other, above, gain, sums, length, shape):
    tokens, width = x.shape
    cols = sums[0].shape[1] // 3
    sizes = [width, width, cols, cols] + [array.shape[1] for array in sums[1:]]
    grad_x, smalls = pl.pallas_call(
        first_back_kernel,
        grid=(tokens // length,),
        in_specs=[rows_of(length, width)] * 4
        + [whole(w) for w in (gain, *sums)],
        out_specs=[rows_of(length, width), pl.BlockSpec(shape, lambda i: (0, 0, 0))],
        out_shape=[
            jax.ShapeDtypeStruct((tokens, width), F32),
            jax.ShapeDtypeStruct(shape, F32),
        ],
        scratch_shapes=[pltpu.VMEM((1, width), F32)] * 2,
        name="first",
        cost_estimate=cost("first", 20 * tokens * width, 20 * tokens * width),
        compiler_params=params(),
    )(mine, other, x, above, gain, *sums)
    return grad_x, smalls, sizes


def from_partner(part):
    return lax.ppermute(part, "mp", [(0, 1), (1, 0)])


ORDERS = {"a": ("yfxn", "xnyf"), "b": ("nxfy", "fxny"), "q": ("ynxf", "yfxn"), "r": ("xyfn", "xynf")}
SIXTHS = {"a": 4, "b": 2, "q": 3, "r": 3}


def orders_for(kind, bits):
    orders = []
    for names in kind:
        order = ["xynf".index(name) for name in names]
        order = [b for b in order if b < bits] + list(range(4, bits))
        orders.append([1 << b for b in order])
    return orders


def order_of_member(orders, member):
    return orders[member % 2]


def block_masks(orders, bits):
    return [
        [
            sum(order[k] for k in range(bits) if r >> (bits - 1 - k) & 1)
            for r in range(1 << bits)
        ]
        for order in orders
    ]


def exchange(array, orders, stage):
    dp, mp = lax.axis_size("dp"), lax.axis_size("mp")
    pairs = []
    for d in range(dp):
        for m in range(mp):
            pairs.append((d * mp + m, (d ^ order_of_member(orders, m)[stage]) * mp + m))
    return lax.ppermute(array, ("dp", "mp"), pairs)


def last_block(array):
    last = array.shape[0] - 1
    return pl.BlockSpec((1, *array.shape[1:]), lambda i: (last, 0, 0))


def add_kernel(*refs, counts, riders):
    outs, at = refs[sum(counts) + riders :], riders
    for k, count in enumerate(counts):
        total = refs[at][...]
        for ref in refs[at + 1 : at + count]:
            total = total + ref[...]
        if riders and not k:
            blocks = outs[k].shape[0] - 1
            outs[k][:blocks] = total
            outs[k][blocks:] = refs[0][...] + refs[1][...]
        else:
            outs[k][...] = total
        at += count


class Scatter:
    def __init__(self, send, keep, orders):
        self.keep, self.orders = keep, orders
        self.got, self.riders = [exchange(send, orders, 0)], ()

    def board(self, block):
        self.riders = (block, exchange(block, self.orders, 0))

    def take(self, after):
        self.got[-1] = lax.optimization_barrier((self.got[-1], after))[0]
        return [self.keep, *self.got]


def advance(scatters, after, passing=()):
    arrays = [scatter.take(after) for scatter in scatters]
    riders = list(scatters[0].riders)
    stage = len(scatters[0].got)
    half = scatters[0].keep.shape[0] >> stage
    step = half if riders or half == 1 else half // 2
    shapes, in_specs, out_specs = [], [last_block(array) for array in riders], []
    for k, group in enumerate(arrays):
        kept = group[0].shape[1:]
        more = 1 if riders and not k else 0
        spec = pl.BlockSpec((step, *kept), lambda i: (i + half // step, 0, 0))
        in_specs += [spec] * len(group)
        out_specs.append(pl.BlockSpec((step + more, *kept), lambda i: (i, 0, 0)))
        shapes.append(jax.ShapeDtypeStruct((half + more, *kept), F32))
    flat = riders + [array for group in arrays for array in group]
    anywhere = [pl.BlockSpec(memory_space=pl.ANY)] * len(passing)
    counts = [len(group) for group in arrays]
    made = pl.pallas_call(
        lambda *refs: add_kernel(
            *refs[: len(flat)],
            *refs[len(flat) + len(passing) : len(flat) + len(passing) + len(counts)],
            counts=counts,
            riders=len(riders),
        ),
        grid=(half // step,),
        in_specs=in_specs + anywhere,
        out_specs=out_specs + anywhere,
        out_shape=shapes + [jax.ShapeDtypeStruct(array.shape, array.dtype) for array in passing],
        input_output_aliases={len(flat) + i: len(shapes) + i for i in range(len(passing))},
        name="add",
        cost_estimate=cost("add", 0, 4 * sum(math.prod(shape.shape) for shape in shapes)),
        compiler_params=params(),
    )(*flat, *passing)
    for scatter, send in zip(scatters, made):
        scatter.got.append(exchange(send, scatter.orders, stage))
        if scatter.riders:
            scatter.riders = (send, scatter.got[-1])
    return made[0], made[len(scatters) :]


def finish_kernel(*refs, counts, outs, riders):
    values, at = [], riders
    for count in counts:
        total = refs[at][0]
        for ref in refs[at + 1 : at + count]:
            total = total + ref[0]
        values.append(total)
        at += count
    for out_ref, pieces in zip(refs[at:], outs):
        to = 0
        for part, start, columns in pieces:
            out_ref[:, to : to + columns] = values[part][:, start : start + columns]
            to += columns
    if riders:
        block, row = refs[0][0] + refs[1][0], 0
        for out_ref in refs[at + len(outs) :]:
            count, wide = out_ref.shape[0], block.shape[1] // 128
            for r in range(count):
                start = r % wide * 128
                out_ref[r : r + 1, :] = block[row + r // wide : row + r // wide + 1, start : start + 128]
            rows = -(-count // wide)
            row += rows + rows % 2


def finish(scatters, after, widths, sizes=()):
    arrays = [scatter.take(after) for scatter in scatters]
    riders = [array for scatter in scatters for array in scatter.riders]
    flat = [array for group in arrays for array in group]
    size, parts = flat[0].shape[1], [group[0].shape[2] for group in arrays]
    outs, first = [], 0
    for width in widths:
        pieces, end = [], first + width
        while first < end:
            index, start, left = place_of(first, parts)
            pieces.append((index, start, min(end - first, left)))
            first += min(end - first, left)
        outs.append(pieces)
    shapes = [(size, width) for width in widths] + [(count // 128, 128) for count in sizes]
    block = lambda array: pl.BlockSpec((1, *array.shape[1:]), lambda i: (0, 0, 0))
    return pl.pallas_call(
        lambda *refs: finish_kernel(
            *refs, counts=[len(group) for group in arrays], outs=outs, riders=len(riders)
        ),
        grid=(1,),
        in_specs=[last_block(array) for array in riders] + [block(array) for array in flat],
        out_specs=[pl.BlockSpec(shape, lambda i: (0, 0)) for shape in shapes],
        out_shape=[jax.ShapeDtypeStruct(shape, F32) for shape in shapes],
        name="finish",
        cost_estimate=cost("add", 0, 4 * len(flat) * size * max(parts)),
        compiler_params=params(),
    )(*riders, *flat)


def butterfly_bits(width):
    dp = lax.axis_size("dp")
    bits = dp.bit_length() - 1
    return bits if (1 << bits) == dp and bits >= 3 and width // dp % 8 == 0 else 0


def parted(block, sizes):
    out, at, wide = [], 0, block.shape[1]
    for size in sizes:
        rows = -(-size // wide)
        out.append(block[at : at + rows].reshape(-1)[:size])
        at += rows + rows % 2
    return out


def on_device(
    inputs,
    segment_ids,
    ln1_gain,
    ln1_bias,
    w_query,
    b_query,
    w_key,
    w_value,
    b_value,
    w_output,
    b_output,
    ln2_gain,
    ln2_bias,
    w_up,
    b_up,
    w_down,
    b_down,
    cotangent,
):
    rows, length, width = inputs.shape
    cols = w_query.shape[1]
    tokens = rows * length
    hidden = w_up.shape[1]
    row = lambda vector: vector.reshape(-1, 128)
    pin = lambda values, after: lax.optimization_barrier((values, after))[0]
    x = inputs.reshape(tokens, width)
    top = cotangent.reshape(tokens, width)
    bits = butterfly_bits(width)

    orders = {key: orders_for(ORDERS[key], bits) for key in ORDERS}
    widths = [2 * hidden * SIXTHS[key] // 6 for key in "ab"] + [4 * cols * SIXTHS[key] // 6 for key in "qr"]
    tables = {key: block_masks(orders[key], bits) for key in ORDERS} if bits else {}

    most = rows - 1
    firsts = (
        row(ln1_gain), row(ln1_bias), w_query, row(b_query), w_key, w_value, row(b_value),
        w_output, row(b_output),
    )
    *made, out_low = attend(x, segment_ids, *firsts, 0, most, ())
    low_other = from_partner(out_low)
    *made, out_high = attend(x, segment_ids, *firsts, most, rows - most, made)
    high_other = from_partner(out_high)
    normed, qkv, probs, context = made
    (middle, down_mine, back_mine, sum_top, sum_up), grad_hidden = forward(
        (out_low, out_high), (low_other, high_other), top, row(ln2_gain), row(ln2_bias),
        w_up, row(b_up), w_down, length, [tables[key] for key in "ab" if bits], widths[:2],
    )
    back_other, down_other = from_partner(back_mine), from_partner(down_mine)
    if bits:
        hiddens = [
            Scatter(*grad_hidden[:2], orders["a"]), Scatter(*grad_hidden[2:], orders["b"])
        ]
    (
        grad_middle, first_mine, sum_gain_two, sum_shift_two, sum_out, sum_qkv,
    ), grad_heads = attend_back(
        top, back_mine, back_other, middle, row(ln2_gain), w_output, qkv, probs, normed, context,
        w_query, w_key, w_value, [tables[key] for key in "qr" if bits], widths[2:],
    )
    outcome = pin(middle, sum_qkv) + (down_mine + down_other) + b_down

    if bits:
        after, passed = advance(hiddens, outcome, (first_mine, grad_heads[0], grad_heads[2]))
        first_mine = passed[0]
        heads = [
            Scatter(passed[1], grad_heads[1], orders["q"]),
            Scatter(passed[2], grad_heads[3], orders["r"]),
        ]
    first_other = from_partner(first_mine)
    grad_x, smalls, sizes = first_back(
        x, first_mine, first_other, grad_middle, row(ln1_gain),
        (sum_qkv, sum_out, sum_gain_two, sum_shift_two, sum_up, sum_top), length,
        (1, width // (1 << bits) if bits else 48, widths[2]),
    )
    if bits:
        heads[0].board(smalls)
        after, _ = advance(heads, smalls)
        for _ in range(2, bits):
            after, _ = advance(hiddens, after)
            after, _ = advance(heads, after)
        out_down, out_up = finish(hiddens, after, (hidden,) * 2)
        out_query, out_key, out_value, out_output, *smalls = finish(
            heads, out_up, (cols,) * 4, sizes
        )
        smalls = [vector.reshape(-1) for vector in smalls]
    else:
        scatter = lambda whole: lax.psum_scatter(whole, "dp", scatter_dimension=0, tiled=True)
        out_down, out_up = scatter(grad_hidden[0][:, :hidden]), scatter(grad_hidden[0][:, hidden:])
        out_query, out_key, out_value, out_output = (
            scatter(grad_heads[0][:, at : at + cols]) for at in range(0, 4 * cols, cols)
        )
        smalls = parted(lax.psum(smalls[0], "dp"), sizes)
    out_down, out_output = out_down.T, out_output.T
    shape = inputs.shape
    return (
        outcome.reshape(shape),
        grad_x.reshape(shape),
        smalls[0],
        smalls[1],
        out_query,
        smalls[2],
        out_key,
        out_value,
        smalls[3],
        out_output,
        smalls[4],
        smalls[5],
        smalls[6],
        out_up,
        smalls[7],
        out_down,
        smalls[8],
    )


def solution(mesh):
    return jax.shard_map(
        on_device,
        mesh=mesh,
        in_specs=(
            P("dp", None, None),
            P("dp", None),
            P(),
            P(),
            P(None, "mp"),
            P("mp"),
            P(None, "mp"),
            P(None, "mp"),
            P("mp"),
            P("mp", None),
            P(),
            P(),
            P(),
            P(None, "mp"),
            P("mp"),
            P("mp", None),
            P(),
            P("dp", None, None),
        ),
        out_specs=(
            P("dp", None, None),
            P("dp", None, None),
            P(),
            P(),
            P("dp", "mp"),
            P("mp"),
            P("dp", "mp"),
            P("dp", "mp"),
            P("mp"),
            P("mp", "dp"),
            P(),
            P(),
            P(),
            P("dp", "mp"),
            P("mp"),
            P("mp", "dp"),
            P(),
        ),
        check_vma=False,
    )
```

```python
import math

import jax
import jax.numpy as jnp
from jax import lax
from jax.experimental import pallas as pl
from jax.experimental.pallas import tpu as pltpu
from jax.sharding import PartitionSpec as P

HD = 64
PAIR = 2 * HD
EPSILON = 1e-06
MASKED = -1000000000.0
SCALE = 1.0 / math.sqrt(HD)
CURVE = math.sqrt(2.0 / math.pi)
CUBIC = 0.044715
COSTS = {"attend": 0.01, "forward": 0.01, "back": 0.01, "first": 0.01, "add": 0.01}
BIG = 67043328
STEP = 512
SLAB = 64
F32 = jnp.float32
BF16 = jnp.bfloat16


def product(left, right, over):
    return lax.dot_general(
        left, right, ((over[:1], over[1:]), ((), ())), preferred_element_type=F32
    )


def left_product(left, right):
    return product(left, right, (0, 0))


def unit_rows(values):
    centered = values - jnp.mean(values, axis=-1, keepdims=True)
    inv_std = lax.rsqrt(jnp.mean(centered * centered, axis=-1, keepdims=True) + EPSILON)
    return centered * inv_std, inv_std


def norm_back(grad_out, unit, inv_std, gain):
    grad_unit = grad_out * gain
    return inv_std * (
        grad_unit
        - jnp.mean(grad_unit, axis=-1, keepdims=True)
        - unit * jnp.mean(grad_unit * unit, axis=-1, keepdims=True)
    )


def column_sum(values):
    return jnp.sum(values, axis=0, keepdims=True)


def line(ref):
    return jnp.concatenate([ref[r : r + 1, :] for r in range(ref.shape[0])], axis=1)


def add_up(ref, value):
    @pl.when(pl.program_id(0) == 0)
    def _():
        ref[...] = jnp.zeros_like(ref)

    ref[...] += value


def in_rows(far, near, sems, first, chunks):
    size = far.shape[0] // chunks
    rows = [pl.ds(c * size, size) for c in range(chunks)]
    return [
        pltpu.make_async_copy(far.at[part], near.at[part], sems.at[first + c])
        for c, part in enumerate(rows)
    ]


def fetch_heads(fars, near, out_far, out_near, sems):
    copies = in_rows(out_far, out_near, sems, 0, 2)
    cols = fars[0].shape[1]
    for i, far in enumerate(fars):
        size = far.shape[0] // 2
        for c in range(2):
            copies.append(
                pltpu.make_async_copy(
                    far.at[pl.ds(c * size, size)],
                    near.at[pl.ds(c * size, size), pl.ds(i * cols, cols)],
                    sems.at[2 + 2 * i + c],
                )
            )
    return copies


def started(copies):
    return lambda: [copy.start() for copy in copies] and None


def arrived(copies):
    return lambda: [copy.wait() for copy in copies] and None


def when_first(action):
    pl.when(pl.program_id(0) == 0)(action)


def either(low, high, rows_low, slab):
    return jnp.where(pl.program_id(0) < rows_low, low[slab, :], high[slab, :])


def last_step():
    return pl.program_id(0) == pl.num_programs(0) - 1


def leaving(tables, outs, pieces, widths, total, sems, make):
    copies, start = [], 0
    me, even = lax.axis_index("dp"), lax.axis_index("mp") % 2 == 0
    for turned, right, at, columns, index, to in pieces:
        if make:
            total[:, start : start + columns] = product(
                turned[...], right[:, at : at + columns], (1, 0)
            )
        fresh = []
        if tables:
            table, send, keep = tables[index], outs[2 * index], outs[2 * index + 1]
            half, size, _ = send.shape
            for r in range(2 * half):
                owner = jnp.where(even, table[0][r], table[1][r]) ^ me
                row = pl.multiple_of(owner * size, 8)
                far = send.at[r - half] if r >= half else keep.at[r]
                fresh.append(
                    pltpu.make_async_copy(
                        total.at[pl.ds(row, size), pl.ds(start, columns)],
                        far.at[:, pl.ds(to, columns)],
                        sems.at[len(copies) + r],
                    )
                )
        else:
            fresh.append(
                pltpu.make_async_copy(
                    total.at[:, pl.ds(start, columns)],
                    outs[0].at[:, pl.ds(sum(widths[:index]) + to, columns)],
                    sems.at[len(copies)],
                )
            )
        if make:
            started(fresh)()
        copies += fresh
        start += columns
    return copies


def leave(*args):
    arrived(leaving(*args, True))()


def pieces_of(sources, first, widths):
    pieces = []
    for turned, right, at, columns in sources:
        end = at + columns
        while at < end:
            index, to, left = place_of(first, widths)
            size = min(512, end - at, left)
            pieces.append((turned, right, at, size, index, to))
            at, first = at + size, first + size
    return pieces


def place_of(column, widths):
    for index, width in enumerate(widths):
        if column < width:
            return index, column, width - column
        column -= width


def step_rows(length):
    return pl.ds(pl.multiple_of(pl.program_id(0) * length, length), length)


def gradient_outs(tables, widths, width):
    if not tables:
        return [jax.ShapeDtypeStruct((width, sum(widths)), F32)], 8
    blocks = len(tables[0][0])
    shapes = [
        jax.ShapeDtypeStruct((blocks // 2, width // blocks, columns), F32)
        for columns in widths
        for _ in range(2)
    ]
    return shapes, blocks * 6


def in_turn(stages, count):
    for turn in range(count + len(stages) - 1):
        for late, stage in enumerate(stages):
            if 0 <= turn - late < count:
                stage(turn - late)


def lane_halves(width):
    lane = lax.broadcasted_iota(jnp.int32, (1, width), 1)
    low = (lane % PAIR < HD).astype(F32)
    return low, 1.0 - low


def attend_kernel(
    seg_ref, gain, shift, bq, bv, bo, wq_far, wk_far, wv_far, wo_far, x_ref, *refs, first_row
):
    normed_ref, qkv_ref, probs_ref, context_ref, out_ref = refs[-8:-3]
    w_all, wo, sems = refs[-3:]
    fetches = fetch_heads((wq_far, wk_far, wv_far), w_all, wo_far, wo, sems)
    when_first(started(fetches))

    cols = wo.shape[0]
    gain_row, shift_row = line(gain), line(shift)
    for at in range(0, x_ref.shape[0], SLAB):
        slab = slice(at, at + SLAB)
        unit, _ = unit_rows(x_ref[slab, :])
        normed_ref[slab, :] = (unit * gain_row + shift_row).astype(BF16)
    normed = normed_ref[...]
    low, high = lane_halves(cols)
    when_first(arrived(fetches))
    made_all = product(normed, w_all[...], (1, 0))
    queries = (made_all[:, :cols] + line(bq)) * SCALE
    keys = made_all[:, cols : 2 * cols].astype(BF16)
    values = (made_all[:, 2 * cols :] + line(bv)).astype(BF16)
    qkv_ref[:, :cols] = queries.astype(BF16)
    qkv_ref[:, cols : 2 * cols] = keys
    qkv_ref[:, 2 * cols :] = values
    split = ((queries * low).astype(BF16), (queries * high).astype(BF16))
    seg_row = seg_ref[pl.ds(pl.program_id(0) + first_row, 1), :].astype(F32)
    length = seg_row.shape[1]
    seg_col = jnp.broadcast_to(seg_row, (128, length)).T
    same = jnp.concatenate([seg_col] * (length // 128), axis=1) == seg_row
    first = lax.broadcasted_iota(jnp.int32, (1, PAIR), 1) < HD
    scores, probs, made = {}, {}, {}

    def score(head):
        part = slice(head // 2 * PAIR, head // 2 * PAIR + PAIR)
        scores[head] = product(keys[:, part], split[head % 2][:, part], (1, 1))

    def soften(head):
        masked = jnp.where(same, scores.pop(head), MASKED)
        expo = jnp.exp(masked - jnp.max(masked, axis=0, keepdims=True))
        probs[head] = (expo * (1.0 / column_sum(expo))).astype(BF16)
        probs_ref[0, head] = probs[head]

    def gather(head):
        part = slice(head // 2 * PAIR, head // 2 * PAIR + PAIR)
        made[head] = product(probs.pop(head), values[:, part], (0, 0))
        if head % 2:
            context_ref[:, part] = jnp.where(first, made.pop(head - 1), made.pop(head)).astype(BF16)

    in_turn((score, soften, gather), cols // HD)
    out_ref[...] = product(context_ref[...], wo[...], (1, 0)) + 0.5 * (x_ref[...] + line(bo))


def whole(array):
    zeros = (0,) * array.ndim
    return pl.BlockSpec(array.shape, lambda i: zeros, pipeline_mode=pl.Buffered(1))


def rows_of(length, width):
    return pl.BlockSpec((length, width), lambda i: (i, 0))


def cost(name, flops, moved):
    weight = COSTS[name]
    return pl.CostEstimate(
        flops=int(weight * flops), bytes_accessed=int(weight * moved), transcendentals=0
    )


def params(limit=26 << 20):
    return pltpu.CompilerParams(vmem_limit_bytes=limit)


def attend(x, segments, gain, shift, wq, bq, wk, wv, bv, wo, bo, first_row, count, made):
    rows, length = segments.shape
    tokens, width = x.shape
    cols = wq.shape[1]
    heads = cols // HD
    at = lambda w: pl.BlockSpec((length, w), lambda i: (i + first_row, 0))
    shape = lambda w, kind: jax.ShapeDtypeStruct((tokens, w), kind)
    fixed = (segments, gain, shift, bq, bv, bo)
    weights = (wq, wk, wv, wo)
    done = tokens * count // rows
    return pl.pallas_call(
        lambda *refs: attend_kernel(*refs, first_row=first_row),
        grid=(count,),
        in_specs=[whole(w) for w in fixed]
        + [pl.BlockSpec(memory_space=pl.ANY)] * len(weights)
        + [at(width)]
        + [pl.BlockSpec(memory_space=pl.ANY)] * len(made),
        out_specs=[
            at(width),
            at(3 * cols),
            pl.BlockSpec((1, heads, length, length), lambda i: (i + first_row, 0, 0, 0)),
            at(cols),
            rows_of(length, width),
        ],
        out_shape=[
            shape(width, BF16),
            shape(3 * cols, BF16),
            jax.ShapeDtypeStruct((rows, heads, length, length), BF16),
            shape(cols, BF16),
            jax.ShapeDtypeStruct((count * length, width), F32),
        ],
        input_output_aliases={len(fixed) + len(weights) + 1 + i: i for i in range(len(made))},
        scratch_shapes=[
            pltpu.VMEM((width, 3 * cols), BF16),
            pltpu.VMEM(wo.shape, BF16),
            pltpu.SemaphoreType.DMA((2 * len(weights),)),
        ],
        name="attend",
        cost_estimate=cost("attend",
            8 * done * width * cols + 4 * done * length * cols,
            done * (10 * width + 8 * cols + 2 * heads * length) + 8 * width * cols,
        ),
        compiler_params=params(BIG),
    )(*fixed, *weights, x, *made)


def forward_kernel(*refs, tables, rows, rows_low, widths):
    mine_low, mine_high, other_low, other_high, top_ref, gain, shift, b_up, w_up, w_down = refs[:10]
    middle_ref, down_ref, back_ref, by_top, by_up = refs[10:15]
    outs, refs = refs[15:-14], refs[-14:]
    up_near, down_near, tops, turned_top, turned, acts, slopes, down_total, up_total = refs[:9]
    normed, up_sems, down_sems, down_outs, up_outs = refs[9:]
    step, length = pl.program_id(0), top_ref.shape[0]
    here = pl.ds(pl.multiple_of(step % rows * length, length), length)
    ups, downs = in_rows(w_up, up_near, up_sems, 0, 4), in_rows(w_down, down_near, down_sems, 0, 4)
    hidden = up_near.shape[1]
    of_down = pieces_of([(turned_top, acts, 0, hidden)], 0, widths)
    of_up = pieces_of([(turned, slopes, 0, hidden)], hidden, widths)
    down_args = (tables, outs, of_down, widths, down_total, down_outs)
    up_args = (tables, outs, of_up, widths, up_total, up_outs)
    when_first(started(ups))
    pl.when(step == 1)(started(downs))

    @pl.when(step < rows)
    def _():
        bias_up, gain_row, shift_row, top_sum = line(b_up), line(gain), line(shift), 0.0
        for at in range(0, length, SLAB):
            slab = slice(at, at + SLAB)
            middle = either(mine_low, mine_high, rows_low, slab) + either(
                other_low, other_high, rows_low, slab
            )
            middle_ref[slab, :] = middle
            unit, _ = unit_rows(middle)
            normed[slab, :] = (unit * gain_row + shift_row).astype(BF16)
            top_sum += column_sum(top_ref[slab, :])
        add_up(by_top, top_sum)
        tops[here, :] = top_ref[...].astype(BF16)
        turned_top[:, here] = tops[here, :].T
        turned[:, here] = normed[...].T
        when_first(arrived(ups))
        for at in range(0, hidden, STEP):
            units = slice(at, at + STEP)
            u = product(normed[...], up_near[:, units], (1, 0)) + bias_up[:, units]
            square = u * u
            bend = jnp.tanh(u * (CURVE + (CURVE * CUBIC) * square))
            above = 0.5 + 0.5 * bend
            act = u * above
            acts[here, units] = act.astype(BF16)
            slope = above + act * (1.0 - bend) * (CURVE + (3.0 * CURVE * CUBIC) * square)
            slopes[here, units] = slope.astype(BF16)

    @pl.when(step == rows - 1)
    def _():
        leaving(*down_args, True)

    @pl.when(step == rows)
    def _():
        arrived(downs)()
        by_up[...] = jnp.zeros_like(by_up)

    @pl.when(step >= rows)
    def _():
        for at in range(0, hidden, STEP):
            units = slice(at, at + STEP)
            grad = product(tops[here, :], down_near[units, :], (1, 1))
            grad = (grad * slopes[here, units].astype(F32)).astype(BF16)
            slopes[here, units] = grad
            by_up[:, units] += column_sum(grad.astype(F32))
        down_ref[...] = product(acts[here, :], down_near[...], (1, 0))
        back_ref[...] = product(slopes[here, :], up_near[...], (1, 1))

    @pl.when(step == 2 * rows - 1)
    def _():
        leave(*up_args)
        arrived(leaving(*down_args, False))()


def forward(mines, others, top, gain, shift, w_up, b_up, w_down, length, tables, widths):
    tokens, width = top.shape
    hidden = w_up.shape[1]
    rows, low = tokens // length, mines[0].shape[0] // length
    first = lambda i: jnp.minimum(i, rows - 1)
    low_spec = pl.BlockSpec((length, width), lambda i: (jnp.minimum(i, low - 1), 0))
    high_spec = pl.BlockSpec((length, width), lambda i: (jnp.clip(i - low, 0, rows - low - 1), 0))
    up_spec = pl.BlockSpec((length, width), lambda i: (first(i), 0))
    back_spec = pl.BlockSpec((length, width), lambda i: (jnp.maximum(i - rows, 0), 0))
    sum_spec = lambda w: pl.BlockSpec((1, w), lambda i: (0, 0))
    shape = lambda *dims: jax.ShapeDtypeStruct(dims, F32)
    anywhere = pl.BlockSpec(memory_space=pl.ANY)
    outs, copies = gradient_outs(tables, widths, width)
    fixed = (gain, shift, b_up)
    made = pl.pallas_call(
        lambda *refs: forward_kernel(
            *refs, tables=tables, rows=rows, rows_low=low, widths=widths
        ),
        grid=(2 * rows,),
        in_specs=[low_spec, high_spec] * 2
        + [up_spec]
        + [whole(w) for w in fixed]
        + [anywhere] * 2,
        out_specs=[up_spec, back_spec, back_spec, sum_spec(width), sum_spec(hidden)]
        + [anywhere] * len(outs),
        out_shape=[shape(tokens, width)] * 3 + [shape(1, width), shape(1, hidden)] + outs,
        scratch_shapes=[
            pltpu.VMEM(w_up.shape, BF16),
            pltpu.VMEM(w_down.shape, BF16),
            pltpu.VMEM((tokens, width), BF16),
            pltpu.VMEM((width, tokens), BF16),
            pltpu.VMEM((width, tokens), BF16),
            pltpu.VMEM((tokens, hidden), BF16),
            pltpu.VMEM((tokens, hidden), BF16),
            pltpu.VMEM((width, hidden), F32),
            pltpu.VMEM((width, hidden), F32),
            pltpu.VMEM((length, width), BF16),
            pltpu.SemaphoreType.DMA((4,)),
            pltpu.SemaphoreType.DMA((4,)),
            pltpu.SemaphoreType.DMA((copies,)),
            pltpu.SemaphoreType.DMA((copies,)),
        ],
        name="forward",
        cost_estimate=cost(
            "forward",
            12 * tokens * width * hidden,
            tokens * 24 * width + 12 * width * hidden,
        ),
        compiler_params=params(BIG),
    )(*mines, *others, top, *fixed, w_up, w_down)
    return made[:5], made[5:]


def attend_back_kernel(*refs, tables, widths):
    mine, other, refs = refs[0], refs[1], refs[2:]
    top_ref, middle_ref, gain, qkv_ref, probs_ref, normed_ref, context_ref = refs[:7]
    wo_far, wq_far, wk_far, wv_far = refs[7:11]
    grad_middle_ref, back_ref, sum_gain, sum_shift, sum_out, sum_qkv = refs[11:17]
    outs, refs = refs[17:-10], refs[-10:]
    rounded, grad_qkv_ref, contexts, turned, turned_two, total, wo, w_all = refs[:8]
    sems, out_sems = refs[8:]
    cols, length = wo.shape[0], top_ref.shape[0]
    here = step_rows(length)
    fetches = fetch_heads((wq_far, wk_far, wv_far), w_all, wo_far, wo, sems)
    when_first(started(fetches))
    gain_row, by_gain, by_shift, by_out = line(gain), 0.0, 0.0, 0.0
    for at in range(0, length, SLAB):
        slab = slice(at, at + SLAB)
        unit, inv_std = unit_rows(middle_ref[slab, :])
        grad_normed = mine[slab, :] + other[slab, :]
        by_gain += column_sum(grad_normed * unit)
        by_shift += column_sum(grad_normed)
        grad_middle = top_ref[slab, :] + norm_back(grad_normed, unit, inv_std, gain_row)
        grad_middle_ref[slab, :] = grad_middle
        by_out += column_sum(grad_middle)
        rounded[slab, :] = grad_middle.astype(BF16)
    add_up(sum_gain, by_gain)
    add_up(sum_shift, by_shift)
    add_up(sum_out, by_out)
    turned[:, here] = normed_ref[...].T
    turned_two[:, here] = rounded[...].T
    contexts[here, :] = context_ref[...]
    when_first(arrived(fetches))
    grad_context = product(rounded[...], wo[...], (1, 1)).astype(BF16).astype(F32)
    low, high = lane_halves(cols)
    split = ((grad_context * low).astype(BF16), (grad_context * high).astype(BF16))
    first = lax.broadcasted_iota(jnp.int32, (1, PAIR), 1) < HD
    grad_probs, grad_scores, made = {}, {}, {}

    def at(head, which):
        start = which * cols + head // 2 * PAIR
        return slice(start, start + PAIR)

    def spread(head):
        grad_probs[head] = product(
            qkv_ref[:, at(head, 2)], split[head % 2][:, at(head, 0)], (1, 1)
        )

    def soften(head):
        wide = probs_ref[0, head].astype(F32)
        moved = wide * grad_probs.pop(head)
        grad_scores[head] = (moved - wide * column_sum(moved)).astype(BF16)

    def gather(head):
        grads = grad_scores.pop(head)
        made[head] = (
            product(grads, qkv_ref[:, at(head, 1)], (0, 0)),
            product(grads, qkv_ref[:, at(head, 0)], (1, 0)),
            product(probs_ref[0, head], split[head % 2][:, at(head, 0)], (1, 0)),
        )
        if head % 2:
            even, odd = made.pop(head - 1), made.pop(head)
            grad_query = jnp.where(first, even[0], odd[0]) * SCALE
            grad_qkv_ref[here, at(head, 0)] = grad_query.astype(BF16)
            grad_qkv_ref[here, at(head, 1)] = jnp.where(first, even[1], odd[1]).astype(BF16)
            grad_qkv_ref[here, at(head, 2)] = (even[2] + odd[2]).astype(BF16)

    in_turn((spread, soften, gather), cols // HD)
    grads = grad_qkv_ref[here, :]
    add_up(sum_qkv, column_sum(grads.astype(F32)))
    back_ref[...] = product(grads, w_all[...], (1, 1))
    pieces = pieces_of(
        [(turned, grad_qkv_ref, 0, 3 * cols), (turned_two, contexts, 0, cols)], 0, widths
    )
    pl.when(last_step())(lambda: leave(tables, outs, pieces, widths, total, out_sems))


def attend_back(
    top, mine, other, middle, gain, wo, qkv, probs, normed, context, wq, wk, wv, tables, widths
):
    tokens, width = top.shape
    rows, heads, length, _ = probs.shape
    cols = wq.shape[1]
    line = lambda w: jax.ShapeDtypeStruct((1, w), F32)
    fixed = lambda w: pl.BlockSpec((1, w), lambda i: (0, 0))
    weights = (wo, wq, wk, wv)
    outs, copies = gradient_outs(tables, widths, width)
    anywhere = pl.BlockSpec(memory_space=pl.ANY)
    made = pl.pallas_call(
        lambda *refs: attend_back_kernel(*refs, tables=tables, widths=widths),
        grid=(rows,),
        in_specs=[rows_of(length, width)] * 4
        + [whole(gain), rows_of(length, 3 * cols)]
        + [pl.BlockSpec((1, heads, length, length), lambda i: (i, 0, 0, 0))]
        + [rows_of(length, width), rows_of(length, cols)]
        + [anywhere] * len(weights),
        out_specs=[rows_of(length, width)] * 2
        + [fixed(width), fixed(width), fixed(width), fixed(3 * cols)]
        + [anywhere] * len(outs),
        out_shape=[jax.ShapeDtypeStruct((tokens, width), F32)] * 2
        + [line(width), line(width), line(width), line(3 * cols)]
        + outs,
        scratch_shapes=[
            pltpu.VMEM((length, width), BF16),
            pltpu.VMEM((tokens, 3 * cols), BF16),
            pltpu.VMEM((tokens, cols), BF16),
            pltpu.VMEM((width, tokens), BF16),
            pltpu.VMEM((width, tokens), BF16),
            pltpu.VMEM((width, 4 * cols), F32),
        ]
        + [
            pltpu.VMEM(wo.shape, BF16),
            pltpu.VMEM((width, 3 * cols), BF16),
            pltpu.SemaphoreType.DMA((2 * len(weights),)),
            pltpu.SemaphoreType.DMA((copies,)),
        ],
        name="back",
        cost_estimate=cost(
            "back",
            16 * tokens * width * cols + 8 * tokens * length * cols,
            tokens * (26 * width + 8 * cols + 2 * heads * length) + 24 * width * cols,
        ),
        compiler_params=params(BIG),
    )(mine, other, top, middle, gain, qkv, probs, normed, context, *weights)
    return made[:6], made[6:]


def first_back_kernel(*refs):
    mine, other, refs = refs[0], refs[1], refs[2:]
    x_ref, above, gain, qkv_sum, out_sum, gain_two, shift_two, up_sum, top_sum = refs[:9]
    out_ref, smalls_ref, sum_gain, sum_shift = refs[9:]
    gain_row, by_gain, by_shift = line(gain), 0.0, 0.0
    for at in range(0, x_ref.shape[0], SLAB):
        slab = slice(at, at + SLAB)
        unit, inv_std = unit_rows(x_ref[slab, :])
        grad_normed = mine[slab, :] + other[slab, :]
        by_gain += column_sum(grad_normed * unit)
        by_shift += column_sum(grad_normed)
        out_ref[slab, :] = above[slab, :] + norm_back(grad_normed, unit, inv_std, gain_row)
    add_up(sum_gain, by_gain)
    add_up(sum_shift, by_shift)

    @pl.when(pl.program_id(0) == pl.num_programs(0) - 1)
    def _():
        smalls_ref[...] = jnp.zeros_like(smalls_ref)
        cols = qkv_sum.shape[1] // 3
        to = 0
        for ref, start, size in (
            (sum_gain, 0, sum_gain.shape[1]),
            (sum_shift, 0, sum_shift.shape[1]),
            (qkv_sum, 0, cols),
            (qkv_sum, 2 * cols, cols),
            (out_sum, 0, out_sum.shape[1]),
            (gain_two, 0, gain_two.shape[1]),
            (shift_two, 0, shift_two.shape[1]),
            (up_sum, 0, up_sum.shape[1]),
            (top_sum, 0, top_sum.shape[1]),
        ):
            wide = smalls_ref.shape[2]
            for at in range(0, size, wide):
                count = min(wide, size - at)
                smalls_ref[0, to : to + 1, :count] = ref[:, start + at : start + at + count]
                to += 1
            to += to % 2


def first_back(x, mine, other, above, gain, sums, length, shape):
    tokens, width = x.shape
    cols = sums[0].shape[1] // 3
    sizes = [width, width, cols, cols] + [array.shape[1] for array in sums[1:]]
    grad_x, smalls = pl.pallas_call(
        first_back_kernel,
        grid=(tokens // length,),
        in_specs=[rows_of(length, width)] * 4
        + [whole(w) for w in (gain, *sums)],
        out_specs=[rows_of(length, width), pl.BlockSpec(shape, lambda i: (0, 0, 0))],
        out_shape=[
            jax.ShapeDtypeStruct((tokens, width), F32),
            jax.ShapeDtypeStruct(shape, F32),
        ],
        scratch_shapes=[pltpu.VMEM((1, width), F32)] * 2,
        name="first",
        cost_estimate=cost("first", 20 * tokens * width, 20 * tokens * width),
        compiler_params=params(),
    )(mine, other, x, above, gain, *sums)
    return grad_x, smalls, sizes


def from_partner(part):
    return lax.ppermute(part, "mp", [(0, 1), (1, 0)])


ORDERS = {"a": ("yfxn", "xnyf"), "b": ("nxfy", "fxny"), "q": ("ynxf", "yfxn"), "r": ("xyfn", "xynf")}
SHARES = {"a": 17, "b": 7, "q": 12, "r": 12}


def orders_for(kind, bits):
    orders = []
    for names in kind:
        order = ["xynf".index(name) for name in names]
        order = [b for b in order if b < bits] + list(range(4, bits))
        orders.append([1 << b for b in order])
    return orders


def order_of_member(orders, member):
    return orders[member % 2]


def block_masks(orders, bits):
    return [
        [
            sum(order[k] for k in range(bits) if r >> (bits - 1 - k) & 1)
            for r in range(1 << bits)
        ]
        for order in orders
    ]


def exchange(array, orders, stage):
    dp, mp = lax.axis_size("dp"), lax.axis_size("mp")
    pairs = []
    for d in range(dp):
        for m in range(mp):
            pairs.append((d * mp + m, (d ^ order_of_member(orders, m)[stage]) * mp + m))
    return lax.ppermute(array, ("dp", "mp"), pairs)


def last_block(array):
    last = array.shape[0] - 1
    return pl.BlockSpec((1, *array.shape[1:]), lambda i: (last, 0, 0))


def add_kernel(*refs, counts, riders):
    outs, at = refs[sum(counts) + riders :], riders
    for k, count in enumerate(counts):
        total = refs[at][...]
        for ref in refs[at + 1 : at + count]:
            total = total + ref[...]
        if riders and not k:
            blocks = outs[k].shape[0] - 1
            outs[k][:blocks] = total
            outs[k][blocks:] = refs[0][...] + refs[1][...]
        else:
            outs[k][...] = total
        at += count


class Scatter:
    def __init__(self, send, keep, orders):
        self.keep, self.orders = keep, orders
        self.got, self.riders = [exchange(send, orders, 0)], ()

    def board(self, block):
        self.riders = (block, exchange(block, self.orders, 0))

    def take(self, after):
        self.got[-1] = lax.optimization_barrier((self.got[-1], after))[0]
        return [self.keep, *self.got]


def advance(scatters, after, passing=()):
    arrays = [scatter.take(after) for scatter in scatters]
    riders = list(scatters[0].riders)
    stage = len(scatters[0].got)
    half = scatters[0].keep.shape[0] >> stage
    step = half if riders or half == 1 else half // 2
    shapes, in_specs, out_specs = [], [last_block(array) for array in riders], []
    for k, group in enumerate(arrays):
        kept = group[0].shape[1:]
        more = 1 if riders and not k else 0
        spec = pl.BlockSpec((step, *kept), lambda i: (i + half // step, 0, 0))
        in_specs += [spec] * len(group)
        out_specs.append(pl.BlockSpec((step + more, *kept), lambda i: (i, 0, 0)))
        shapes.append(jax.ShapeDtypeStruct((half + more, *kept), F32))
    flat = riders + [array for group in arrays for array in group]
    anywhere = [pl.BlockSpec(memory_space=pl.ANY)] * len(passing)
    counts = [len(group) for group in arrays]
    made = pl.pallas_call(
        lambda *refs: add_kernel(
            *refs[: len(flat)],
            *refs[len(flat) + len(passing) : len(flat) + len(passing) + len(counts)],
            counts=counts,
            riders=len(riders),
        ),
        grid=(half // step,),
        in_specs=in_specs + anywhere,
        out_specs=out_specs + anywhere,
        out_shape=shapes + [jax.ShapeDtypeStruct(array.shape, array.dtype) for array in passing],
        input_output_aliases={len(flat) + i: len(shapes) + i for i in range(len(passing))},
        name="add",
        cost_estimate=cost("add", 0, 4 * sum(math.prod(shape.shape) for shape in shapes)),
        compiler_params=params(),
    )(*flat, *passing)
    for scatter, send in zip(scatters, made):
        scatter.got.append(exchange(send, scatter.orders, stage))
        if scatter.riders:
            scatter.riders = (send, scatter.got[-1])
    return made[0], made[len(scatters) :]


def finish_kernel(*refs, counts, outs, riders):
    values, at = [], riders
    for count in counts:
        total = refs[at][0]
        for ref in refs[at + 1 : at + count]:
            total = total + ref[0]
        values.append(total)
        at += count
    for out_ref, pieces in zip(refs[at:], outs):
        to = 0
        for part, start, columns in pieces:
            out_ref[:, to : to + columns] = values[part][:, start : start + columns]
            to += columns
    if riders:
        block, row = refs[0][0] + refs[1][0], 0
        for out_ref in refs[at + len(outs) :]:
            count, wide = out_ref.shape[0], block.shape[1] // 128
            for r in range(count):
                start = r % wide * 128
                out_ref[r : r + 1, :] = block[row + r // wide : row + r // wide + 1, start : start + 128]
            rows = -(-count // wide)
            row += rows + rows % 2


def finish(scatters, after, widths, sizes=()):
    arrays = [scatter.take(after) for scatter in scatters]
    riders = [array for scatter in scatters for array in scatter.riders]
    flat = [array for group in arrays for array in group]
    size, parts = flat[0].shape[1], [group[0].shape[2] for group in arrays]
    outs, first = [], 0
    for width in widths:
        pieces, end = [], first + width
        while first < end:
            index, start, left = place_of(first, parts)
            pieces.append((index, start, min(end - first, left)))
            first += min(end - first, left)
        outs.append(pieces)
    shapes = [(size, width) for width in widths] + [(count // 128, 128) for count in sizes]
    block = lambda array: pl.BlockSpec((1, *array.shape[1:]), lambda i: (0, 0, 0))
    return pl.pallas_call(
        lambda *refs: finish_kernel(
            *refs, counts=[len(group) for group in arrays], outs=outs, riders=len(riders)
        ),
        grid=(1,),
        in_specs=[last_block(array) for array in riders] + [block(array) for array in flat],
        out_specs=[pl.BlockSpec(shape, lambda i: (0, 0)) for shape in shapes],
        out_shape=[jax.ShapeDtypeStruct(shape, F32) for shape in shapes],
        name="finish",
        cost_estimate=cost("add", 0, 4 * len(flat) * size * max(parts)),
        compiler_params=params(),
    )(*riders, *flat)


def butterfly_bits(width):
    dp = lax.axis_size("dp")
    bits = dp.bit_length() - 1
    return bits if (1 << bits) == dp and bits >= 3 and width // dp % 8 == 0 else 0


def parted(block, sizes):
    out, at, wide = [], 0, block.shape[1]
    for size in sizes:
        rows = -(-size // wide)
        out.append(block[at : at + rows].reshape(-1)[:size])
        at += rows + rows % 2
    return out


def on_device(
    inputs,
    segment_ids,
    ln1_gain,
    ln1_bias,
    w_query,
    b_query,
    w_key,
    w_value,
    b_value,
    w_output,
    b_output,
    ln2_gain,
    ln2_bias,
    w_up,
    b_up,
    w_down,
    b_down,
    cotangent,
):
    rows, length, width = inputs.shape
    cols = w_query.shape[1]
    tokens = rows * length
    hidden = w_up.shape[1]
    row = lambda vector: vector.reshape(-1, 128)
    pin = lambda values, after: lax.optimization_barrier((values, after))[0]
    x = inputs.reshape(tokens, width)
    top = cotangent.reshape(tokens, width)
    bits = butterfly_bits(width)

    orders = {key: orders_for(ORDERS[key], bits) for key in ORDERS}
    widths = [2 * hidden * SHARES[key] // 24 for key in "ab"] + [4 * cols * SHARES[key] // 24 for key in "qr"]
    tables = {key: block_masks(orders[key], bits) for key in ORDERS} if bits else {}

    most = rows - 1
    firsts = (
        row(ln1_gain), row(ln1_bias), w_query, row(b_query), w_key, w_value, row(b_value),
        w_output, row(b_output),
    )
    *made, out_low = attend(x, segment_ids, *firsts, 0, most, ())
    low_other = from_partner(out_low)
    *made, out_high = attend(x, segment_ids, *firsts, most, rows - most, made)
    high_other = from_partner(out_high)
    normed, qkv, probs, context = made
    (middle, down_mine, back_mine, sum_top, sum_up), grad_hidden = forward(
        (out_low, out_high), (low_other, high_other), top, row(ln2_gain), row(ln2_bias),
        w_up, row(b_up), w_down, length, [tables[key] for key in "ab" if bits], widths[:2],
    )
    back_other, down_other = from_partner(back_mine), from_partner(down_mine)
    if bits:
        hiddens = [
            Scatter(*grad_hidden[:2], orders["a"]), Scatter(*grad_hidden[2:], orders["b"])
        ]
    (
        grad_middle, first_mine, sum_gain_two, sum_shift_two, sum_out, sum_qkv,
    ), grad_heads = attend_back(
        top, back_mine, back_other, middle, row(ln2_gain), w_output, qkv, probs, normed, context,
        w_query, w_key, w_value, [tables[key] for key in "qr" if bits], widths[2:],
    )
    outcome = pin(middle, sum_qkv) + (down_mine + down_other) + b_down

    if bits:
        after, passed = advance(hiddens, outcome, (first_mine, grad_heads[0], grad_heads[2]))
        first_mine = passed[0]
        heads = [
            Scatter(passed[1], grad_heads[1], orders["q"]),
            Scatter(passed[2], grad_heads[3], orders["r"]),
        ]
    first_other = from_partner(first_mine)
    grad_x, smalls, sizes = first_back(
        x, first_mine, first_other, grad_middle, row(ln1_gain),
        (sum_qkv, sum_out, sum_gain_two, sum_shift_two, sum_up, sum_top), length,
        (1, width // (1 << bits) if bits else 48, widths[2]),
    )
    if bits:
        heads[0].board(smalls)
        after, _ = advance(heads, smalls)
        for _ in range(2, bits):
            after, _ = advance(hiddens, after)
            after, _ = advance(heads, after)
        out_down, out_up = finish(hiddens, after, (hidden,) * 2)
        out_query, out_key, out_value, out_output, *smalls = finish(
            heads, out_up, (cols,) * 4, sizes
        )
        smalls = [vector.reshape(-1) for vector in smalls]
    else:
        scatter = lambda whole: lax.psum_scatter(whole, "dp", scatter_dimension=0, tiled=True)
        out_down, out_up = scatter(grad_hidden[0][:, :hidden]), scatter(grad_hidden[0][:, hidden:])
        out_query, out_key, out_value, out_output = (
            scatter(grad_heads[0][:, at : at + cols]) for at in range(0, 4 * cols, cols)
        )
        smalls = parted(lax.psum(smalls[0], "dp"), sizes)
    out_down, out_output = out_down.T, out_output.T
    shape = inputs.shape
    return (
        outcome.reshape(shape),
        grad_x.reshape(shape),
        smalls[0],
        smalls[1],
        out_query,
        smalls[2],
        out_key,
        out_value,
        smalls[3],
        out_output,
        smalls[4],
        smalls[5],
        smalls[6],
        out_up,
        smalls[7],
        out_down,
        smalls[8],
    )


def solution(mesh):
    return jax.shard_map(
        on_device,
        mesh=mesh,
        in_specs=(
            P("dp", None, None),
            P("dp", None),
            P(),
            P(),
            P(None, "mp"),
            P("mp"),
            P(None, "mp"),
            P(None, "mp"),
            P("mp"),
            P("mp", None),
            P(),
            P(),
            P(),
            P(None, "mp"),
            P("mp"),
            P("mp", None),
            P(),
            P("dp", None, None),
        ),
        out_specs=(
            P("dp", None, None),
            P("dp", None, None),
            P(),
            P(),
            P("dp", "mp"),
            P("mp"),
            P("dp", "mp"),
            P("dp", "mp"),
            P("mp"),
            P("mp", "dp"),
            P(),
            P(),
            P(),
            P("dp", "mp"),
            P("mp"),
            P("mp", "dp"),
            P(),
        ),
        check_vma=False,
    )
```
